32 devices in a mesh: job: 2 (over y), slab: 16 (over z, x, core).
Axes of the slice: x: 2, y: 2, z: 4, core: 2. Of those that a mesh axis runs over, the one named last changes fastest.
Arguments:
- partials: bfloat16 [8, 32, 256, 256], P('job', None, 'slab'), parts along dimension 0, may hold values from -1.5 to 1.5
- regions: int32 [64, 256, 256], P(('job', 'slab')), parts along dimension 0, may hold values from 0 to 2
- previous: float32 [64, 256, 256], P(('job', 'slab')), parts along dimension 0, may hold values from -6 to 6
Outputs:
- potential: float32 [64, 256, 256], P(('job', 'slab')), parts along dimension 0
The draws below stay inside these ranges and needn't reach their ends.
There are 2 independent parts, one for each index of `job`. The reference program is written for one: setup_inputs(seed, part) draws one part's arguments, and reference() takes and returns one part's arrays. A program takes and returns all parts, laid end to end along the dimension named above; each array names one. Nothing has to cross between parts.
Inputs may be any that keep to these rules, and one draw needn't show every extreme that they name: `regions`: 0 marks the solute's interior, 1 the ion-free solvent layer, 2 bulk solvent.
All inputs are finite; a program needn't handle non-finite values.
Results may differ from the reference program's by a relative error of at most 0.0003.
Values sent between devices are 32-bit elements; how exact they have to be, the bound alone decides.
A program may use at most 256 MiB of HBM per device.

```python
import jax
import jax.numpy as jnp

NXY = 256
BANDS = 4
PRE_SWEEPS = 2
POST_SWEEPS = 2
COARSE_SWEEPS = 4
NZ = 32


def draw_partials(key, part):
    extent = (BANDS, NZ, NXY, NXY)
    values = jnp.clip(0.25 * jax.random.normal(key, extent, jnp.float32), -1.5, 1.5)
    return values.astype(jnp.bfloat16)


def place_ends(values, rng, least, largest):
    longest = values.shape.index(max(values.shape))
    spots = []
    for shift in (0, 1):
        where = [jax.random.randint(jax.random.fold_in(rng, axis), (), 0, length) for axis, length in enumerate(values.shape)]
        where[longest] = (where[longest] + shift) % values.shape[longest]
        spots.append(tuple(where))
    return values.at[spots[0]].set(least).at[spots[1]].set(largest)


def block_scale(key, shape, split, smallest, high):
    def one(dim, parts):
        heights = jax.random.uniform(jax.random.fold_in(jax.random.fold_in(key, 6), dim), (parts,), jnp.float32, smallest / len(split), high / len(split))
        return jnp.repeat(jnp.exp(heights), shape[dim] // parts).reshape((-1,) + (1,) * (len(shape) - dim - 1))

    loudness = one(*split[0])
    for cut in split[1:]:
        loudness = loudness * one(*cut)
    return loudness


def centred(stream_key, shape, scale, limit, cuts=(), held_as=jnp.bfloat16):
    gain = block_scale(stream_key, shape, cuts, -0.22, 0.18) if cuts else 1.0
    values = jax.random.normal(stream_key, shape, jnp.float32) * scale * gain
    return jnp.minimum(jnp.maximum(values, -limit), limit).astype(held_as)


def setup_inputs(seed: int = 0, part: int = 0) -> dict:
    arg_keys = jax.random.split(jax.random.key(seed), 4)
    part_keys = jax.random.split(jax.random.fold_in(arg_keys[3], part), 4)
    partials = draw_partials(jax.random.fold_in(jax.random.fold_in(arg_keys[3], part), 71), part)
    regions = place_ends(jax.random.randint(part_keys[1], (NZ, NXY, NXY), 0, 3), jax.random.fold_in(part_keys[1], 1), 0, 2).astype(jnp.int32)
    previous = centred(part_keys[2], (NZ, NXY, NXY), 1.0, 6.0, ((0, 16),), jnp.float32)
    return {"partials": partials, "regions": regions, "previous": previous}


DAMPING = 0.75
INSIDE = 2.0
SOLVENT = 78.4
SCREEN = 1.4
SOURCE = 16.0 * 3.141592653589793


def pad_whole(values):
    return jnp.pad(values, ((1, 1), (1, 1), (1, 1)))


def shifted_views(padded):
    return (padded[:-2, 1:-1, 1:-1], padded[2:, 1:-1, 1:-1],
            padded[1:-1, :-2, 1:-1], padded[1:-1, 2:, 1:-1],
            padded[1:-1, 1:-1, :-2], padded[1:-1, 1:-1, 2:])


def face_coefficients(padded, spacing_z, spacing_x):
    centre = padded[1:-1, 1:-1, 1:-1]
    spacings = (spacing_z, spacing_z, spacing_x, spacing_x, spacing_x, spacing_x)
    result = []
    for neighbour, spacing in zip(shifted_views(padded), spacings):
        facing = jnp.where(neighbour > 0.0, neighbour, centre)
        result.append(2.0 * centre * facing / ((centre + facing) * spacing))
    return tuple(result)


def diagonal_of(coefficients, screening):
    running = coefficients[0]
    for coefficient in coefficients[1:]:
        running = running + coefficient
    return running + screening


def beside_sum(coefficients, padded):
    neighbours = shifted_views(padded)
    running = coefficients[0] * neighbours[0]
    for position in range(1, 6):
        running = running + coefficients[position] * neighbours[position]
    return running


def remainder(source_term, solution, coefficients, diagonal):
    return source_term - diagonal * solution + beside_sum(coefficients, pad_whole(solution))


def coarsen(values, halve_plane):
    planes = values.shape[0]
    plane_width = values.shape[1]
    if halve_plane:
        blocks = values.reshape(planes // 2, 2, plane_width // 2, 2, plane_width // 2, 2)
        return jnp.mean(blocks, axis=(1, 3, 5))
    return jnp.mean(values.reshape(planes // 2, 2, plane_width, plane_width), axis=1)


def refine(values, halve_plane):
    values = jnp.repeat(values, 2, axis=0)
    if halve_plane:
        values = jnp.repeat(jnp.repeat(values, 2, axis=1), 2, axis=2)
    return values


def v_cycle(source_term, dielectric, screening, initial, spacing_z, spacing_x):
    planes = source_term.shape[0]
    plane_width = source_term.shape[1]
    coefficients = face_coefficients(pad_whole(dielectric), spacing_z, spacing_x)
    diagonal = diagonal_of(coefficients, screening)
    coarsest = planes == 1
    sweeps = COARSE_SWEEPS if coarsest else PRE_SWEEPS
    if initial is None:
        solution = jnp.zeros_like(source_term)
    else:
        solution = initial
    for sweep_index in range(sweeps):
        solution = solution + DAMPING * remainder(source_term, solution, coefficients, diagonal) / diagonal
    if coarsest:
        return solution
    residual = remainder(source_term, solution, coefficients, diagonal)
    halve_plane = plane_width > 1 and plane_width % 2 == 0
    next_x = spacing_x * 4.0 if halve_plane else spacing_x
    correction = v_cycle(coarsen(residual, halve_plane), coarsen(dielectric, halve_plane),
                         coarsen(screening, halve_plane), None, spacing_z * 4.0, next_x)
    solution = solution + refine(correction, halve_plane)
    for sweep_index in range(POST_SWEEPS):
        solution = solution + DAMPING * remainder(source_term, solution, coefficients, diagonal) / diagonal
    return solution


def reference(partials, regions, previous):
    density = jnp.sum(partials, axis=0, dtype=jnp.float32)
    source_term = SOURCE * density
    dielectric = jnp.where(regions == 0, INSIDE, SOLVENT).astype(jnp.float32)
    screening = jnp.where(regions == 2, SCREEN, 0.0).astype(jnp.float32)
    return v_cycle(source_term, dielectric, screening, previous, 1.0, 1.0)
```

```python
import functools

import jax
import jax.numpy as jnp
from jax import lax
from jax.experimental import pallas as pl
from jax.experimental.pallas import tpu as pltpu
from jax.sharding import PartitionSpec as P

PRE_SWEEPS = 2
POST_SWEEPS = 2
COARSE_SWEEPS = 4

DAMPING = 0.75
INSIDE = 2.0
SOLVENT = 78.4
SCREEN = 1.4
SOURCE = 16.0 * 3.141592653589793

F32 = jnp.float32
LANES = 128


def iota(shape, dim):
    return lax.broadcasted_iota(jnp.int32, shape, dim)


def face(mine, other, spacing):
    return mine * other / ((mine + other) * (0.5 * spacing))


def back(v, dim, by=1):
    return pltpu.roll(v, by, dim)


def ahead(v, dim, by=1):
    return pltpu.roll(v, v.shape[dim] - by, dim)


def terms(v):
    result = []
    for _ in range(3):
        result.append(v.astype(jnp.bfloat16))
        v = v - result[-1].astype(F32)
    return result


def product(a, b):
    return lax.dot_general(a, b, (((1,), (0,)), ((), ())), preferred_element_type=F32)


def times(v, selector):
    high, middle, low = (product(t, selector.astype(jnp.bfloat16)) for t in terms(v))
    return high + (middle + low)


def dot(selector, v):
    high, middle, low = (product(selector.astype(jnp.bfloat16), t) for t in terms(v))
    return high + (middle + low)


def pool_right(wide, narrow, valid):
    src, dst = iota((wide, narrow), 0), iota((wide, narrow), 1)
    return jnp.where((src // 2 == dst) & (src < valid), 1.0, 0.0).astype(F32)


def pool_left(narrow, wide):
    dst, src = iota((narrow, wide), 0), iota((narrow, wide), 1)
    return jnp.where(src // 2 == dst, 1.0, 0.0).astype(F32)


def spread_right(narrow, wide, valid):
    src, dst = iota((narrow, wide), 0), iota((narrow, wide), 1)
    return jnp.where((dst // 2 == src) & (dst < valid), 1.0, 0.0).astype(F32)


def spread_left(wide, narrow):
    dst, src = iota((wide, narrow), 0), iota((wide, narrow), 1)
    return jnp.where(dst // 2 == src, 1.0, 0.0).astype(F32)


def plane_faces(e, spacing):
    rows, cols = e.shape
    x, y = iota(e.shape, 0), iota(e.shape, 1)
    fx = jnp.where(x > 0, face(e, back(e, 0), spacing), 0.0)
    fy = jnp.where(y > 0, face(e, back(e, 1), spacing), 0.0)
    edges = (jnp.where((x == 0) | (x == rows - 1), 1.0, 0.0)
             + jnp.where((y == 0) | (y == cols - 1), 1.0, 0.0))
    total = fx + ahead(fx, 0) + fy + ahead(fy, 1) + edges * e * (1.0 / spacing)
    return fx, fy, total


def plane_sum(fx, fy, v):
    return fx * back(v, 0) + ahead(fx * v, 0) + fy * back(v, 1) + ahead(fy * v, 1)


def coarse_cycle(e, k, planes, nx, sz, sx):
    rows = e.shape[0]
    row, lane = iota(e.shape, 0), iota(e.shape, 1)
    x, z = row % nx, row // nx
    valid = (row < planes * nx) & (lane < nx)
    e = jnp.where(valid, e, 1.0)
    fx = jnp.where(valid & (x > 0), face(e, back(e, 0), sx), 0.0) if nx > 1 else None
    fy = jnp.where(valid & (lane > 0), face(e, back(e, 1), sx), 0.0) if nx > 1 else None
    wrap = nx % rows
    fz = jnp.where(valid & (z > 0), face(e, back(e, 0, wrap), sz), 0.0) if planes > 1 else None
    diag = k + e * (
        (jnp.where(x == 0, 1.0, 0.0) + jnp.where(x == nx - 1, 1.0, 0.0)
         + jnp.where(lane == 0, 1.0, 0.0) + jnp.where(lane == nx - 1, 1.0, 0.0)) * (1.0 / sx)
        + (jnp.where(z == 0, 1.0, 0.0) + jnp.where(z == planes - 1, 1.0, 0.0)) * (1.0 / sz))
    if nx > 1:
        diag = diag + fx + ahead(fx, 0) + fy + ahead(fy, 1)
    if planes > 1:
        diag = diag + fz + ahead(fz, 0, wrap)
    w = jnp.where(valid, DAMPING / jnp.where(valid, diag, 1.0), 0.0)

    def beside(v):
        total = jnp.zeros_like(v)
        if nx > 1:
            total = plane_sum(fx, fy, v)
        if planes > 1:
            total = total + fz * back(v, 0, wrap) + ahead(fz * v, 0, wrap)
        return total

    def sweep(v, b):
        return (1.0 - DAMPING) * v + w * (b + beside(v))

    def coarsest(b):
        v = w * b
        for _ in range(COARSE_SWEEPS - 1):
            v = sweep(v, b)
        return v

    if planes == 1:
        return coarsest
    halve = nx > 1 and nx % 2 == 0
    nx2 = nx // 2 if halve else nx
    sx2 = sx * 4.0 if halve else sx
    step = planes
    while step * nx > 512 and step % 4 == 0:
        step //= 2
    part = step * nx
    if step == planes:
        part = rows
    real2 = planes // 2 * nx2
    rows2 = max(8, real2)
    part2 = rows2 if step == planes else step // 2 * nx2
    ratio = 2 if halve else 1

    def member(fine, coarse):
        return ((fine < step * nx) & ((fine // nx // 2) * nx2 + fine % nx // ratio == coarse))

    down = jnp.where(member(iota((part2, part), 1), iota((part2, part), 0)), 1.0, 0.0)
    up = jnp.where(member(iota((part, part2), 0), iota((part, part2), 1)), 1.0, 0.0)
    if halve:
        right = pool_right(LANES, LANES, nx)
        left = spread_right(LANES, LANES, nx)
        scale = 0.125
    else:
        scale = 0.5

    def coarsen(f):
        if halve:
            f = times(f, right)
        parts = [dot(down, f[i:i + part]) for i in range(0, rows, part)]
        return scale * (parts[0] if len(parts) == 1 else jnp.concatenate(parts, axis=0))

    def refine(f):
        if halve:
            f = times(f, left)
        parts = [dot(up, f[i:i + part2]) for i in range(0, rows2, part2)]
        return parts[0] if len(parts) == 1 else jnp.concatenate(parts, axis=0)

    below = coarse_cycle(coarsen(jnp.where(valid, e, 0.0)), coarsen(k),
                         planes // 2, nx2, sz * 4.0, sx2)

    def run(b):
        v = w * b
        for _ in range(PRE_SWEEPS - 1):
            v = sweep(v, b)
        r = jnp.where(valid, b - diag * v + beside(v), 0.0)
        v = v + refine(below(coarsen(r)))
        for _ in range(POST_SWEEPS):
            v = sweep(v, b)
        return v

    return run


REG, V0, V1, V2, BASE, FAR = range(6)
E1, A1, A2, A3, A4, TERM = range(6)


def kernel(n, partials, regions, previous, out,
           dens, got, b0, fx0, fy0, fz0, dg0, wt0, halo_reg, far_reg, fxh, fyh, fzh, wth, halo0, v1, v2, base,
           halo1, plane1, term1, gb, gk,
           big_send, big_recv, small_send, small_recv, many_send, many_recv, c2_planes):
    me = lax.axis_index("slab")
    job = lax.axis_index("job")
    nxy = regions.shape[1]
    half = nxy // 2
    quarter = nxy // 4
    rows = partials.shape[2]
    has_lo, has_hi = me > 0, me < n - 1

    def peer(index):
        return {"slab": index}

    barrier = pltpu.get_barrier_semaphore()

    def greet(off, carry):
        pl.semaphore_signal(barrier, inc=1, device_id=peer(lax.rem(me + off, n)),
                            device_id_type=pl.DeviceIdType.MESH)
        return carry

    lax.fori_loop(1, n, greet, 0)

    @pl.when(jnp.logical_not(has_lo))
    def _():
        for i in range(4):
            halo0[i, 0] = jnp.zeros((nxy, nxy), F32)
        for i in range(6):
            halo1[i, 0] = jnp.zeros((half, half), F32)
        halo_reg[0] = jnp.zeros((nxy, nxy), jnp.int32)
        far_reg[0] = jnp.zeros((nxy, nxy), jnp.int32)

    @pl.when(jnp.logical_not(has_hi))
    def _():
        for i in range(4):
            halo0[i, 1] = jnp.zeros((nxy, nxy), F32)
        for i in range(6):
            halo1[i, 1] = jnp.zeros((half, half), F32)
        halo_reg[1] = jnp.zeros((nxy, nxy), jnp.int32)
        far_reg[1] = jnp.zeros((nxy, nxy), jnp.int32)

    density = partials[0].astype(F32)
    for g in range(1, partials.shape[0]):
        density = density + partials[g].astype(F32)
    dens[...] = (SOURCE * density).reshape(dens.shape)

    pl.semaphore_wait(barrier, n - 1)

    def copies(first, last, dst, sends, recvs, i):
        to_lo = pltpu.make_async_remote_copy(
            src_ref=first, dst_ref=dst.at[1], send_sem=sends.at[i, 0], recv_sem=recvs.at[i, 1],
            device_id=peer(jnp.maximum(me - 1, 0)), device_id_type=pl.DeviceIdType.MESH)
        to_hi = pltpu.make_async_remote_copy(
            src_ref=last, dst_ref=dst.at[0], send_sem=sends.at[i, 1], recv_sem=recvs.at[i, 0],
            device_id=peer(jnp.minimum(me + 1, n - 1)), device_id_type=pl.DeviceIdType.MESH)

        def start():
            pl.when(has_lo)(to_lo.start)
            pl.when(has_hi)(to_hi.start)

        def recv():
            pl.when(has_lo)(to_hi.wait_recv)
            pl.when(has_hi)(to_lo.wait_recv)

        def sent():
            pl.when(has_lo)(to_lo.wait_send)
            pl.when(has_hi)(to_hi.wait_send)

        return start, recv, sent

    pending = []

    def launch(first, last, dst, sends, recvs, i):
        start, recv, sent = copies(first, last, dst, sends, recvs, i)
        start()
        pending.append(sent)
        return recv

    recv_reg = launch(regions.at[0], regions.at[1], halo_reg, big_send, big_recv, REG)
    recv_v0 = launch(previous.at[0], previous.at[1], halo0.at[0], big_send, big_recv, V0)

    def scatter(step, carry):
        other = lax.rem(me + 1 + lax.rem(step + n // 2 - 1, n - 1), n)
        pltpu.make_async_remote_copy(
            src_ref=dens.at[other], dst_ref=got.at[me], send_sem=many_send.at[0],
            recv_sem=many_recv.at[0], device_id=peer(other),
            device_id_type=pl.DeviceIdType.MESH).start()
        return carry

    lax.fori_loop(0, n - 1, scatter, 0)

    def dielectric(r):
        return jnp.where(r == 0, INSIDE, SOLVENT).astype(F32)

    e = [dielectric(regions[p]) for p in range(2)]
    k = [jnp.where(regions[p] == 2, SCREEN, 0.0).astype(F32) for p in range(2)]
    right0, left0 = pool_right(nxy, half, nxy), pool_left(half, nxy)
    right1, left1 = pool_right(half, LANES, half), pool_left(quarter, half)

    def down0(a, b):
        return 0.125 * dot(left0, times(a + b, right0))

    def down1(a):
        return 0.25 * dot(left1, times(a, right1))

    e1, k1 = down0(e[0], e[1]), down0(k[0], k[1])
    plane1[E1] = e1
    recv_e1 = launch(plane1.at[E1], plane1.at[E1], halo1.at[E1], small_send, small_recv, E1)
    core, chip = lax.rem(me, 2), me // 2
    gk[core, chip] = down1(e1) + back(down1(k1), 1, LANES // 2)

    def share(ref, i):
        def one(off, carry):
            other = lax.rem(me + 2 * off, n)
            pltpu.make_async_remote_copy(
                src_ref=ref.at[core, chip], dst_ref=ref.at[core, chip], send_sem=many_send.at[i],
                recv_sem=many_recv.at[i], device_id=peer(other),
                device_id_type=pl.DeviceIdType.MESH).start()
            return carry

        lax.fori_loop(1, n // 2, one, 0)

    def relay(ref, i):
        window = ref.at[0, pl.ds(0, n // 2 - 1)]
        pltpu.make_async_copy(window, window, many_recv.at[i]).wait()
        copy = pltpu.make_async_remote_copy(
            src_ref=ref.at[core], dst_ref=ref.at[core], send_sem=many_send.at[i + 2],
            recv_sem=many_recv.at[i + 2], device_id=peer(me + 1 - 2 * core),
            device_id_type=pl.DeviceIdType.MESH)
        copy.start()
        pending.append(pltpu.make_async_copy(window, window, many_send.at[i]).wait)
        pending.append(copy.wait_send)
        return copy.wait_recv

    def all_in(ref, sems, i):
        window = ref.at[pl.ds(0, n - 1)]
        pltpu.make_async_copy(window, window, sems.at[i]).wait()

    share(gk, 1)

    totals = []
    middle = face(e[0], e[1], 1.0)
    fz0[1] = middle
    part = []
    for p in range(2):
        fx, fy, total = plane_faces(e[p], 1.0)
        fx0[p] = fx
        fy0[p] = fy
        totals.append(total + middle + k[p])
        part.append(plane_sum(fx, fy, previous[p]) + middle * previous[1 - p])
    recv_reg()
    e_side = [jnp.where(has_lo, dielectric(halo_reg[0]), e[0]),
              jnp.where(has_hi, dielectric(halo_reg[1]), e[1])]
    for p in range(2):
        outer = face(e_side[p], e[p], 1.0)
        fz0[2 * p] = outer
        total = totals[p] + outer
        dg0[p] = total
        wt0[p] = DAMPING / total

    def beside0(p, mine, below, above):
        return plane_sum(fx0[p], fy0[p], mine) + fz0[p] * below + fz0[p + 1] * above

    def sweep0(p, mine, below, above):
        return (1.0 - DAMPING) * mine + wt0[p] * (b0[p] + beside0(p, mine, below, above))

    recv_v0()
    for p in range(2):
        v1[p] = (1.0 - DAMPING) * previous[p] + wt0[p] * (part[p] + fz0[2 * p] * halo0[0, p])

    got[me] = dens[me]
    all_in(got, many_recv, 0)
    for p in range(2):
        if rows % 8 == 0:
            b0[p] = got[:, p].reshape(nxy, nxy)
        else:
            for s in range(n):
                b0[p, s * rows:(s + 1) * rows, :] = got[s, p]
    for p in range(2):
        v1[p] = v1[p] + wt0[p] * b0[p]
    recv = launch(v1.at[0], v1.at[1], halo0.at[1], big_send, big_recv, V1)
    recv_gk = relay(gk, 1)
    recv_e1()
    sz1 = sx1 = 4.0
    fx1, fy1, total1 = plane_faces(e1, sx1)
    fz1lo = face(jnp.where(has_lo, halo1[E1, 0], e1), e1, sz1)
    fz1hi = face(jnp.where(has_hi, halo1[E1, 1], e1), e1, sz1)
    dg1 = total1 + fz1lo + fz1hi + k1
    wt1 = DAMPING / dg1

    recv()
    v2[0] = sweep0(0, v1[0], halo0[1, 0], v1[1])
    v2[1] = sweep0(1, v1[1], v1[0], halo0[1, 1])
    term1[0] = 0.125 * dot(left0, times(fz0[0] * v2[0], right0))
    term1[1] = 0.125 * dot(left0, times(fz0[2] * v2[1], right0))
    recv_term = launch(term1.at[0], term1.at[1], halo1.at[TERM], small_send, small_recv, TERM)
    recv_v2 = launch(v2.at[0], v2.at[1], halo0.at[2], big_send, big_recv, V2)
    r0 = b0[0] - dg0[0] * v2[0] + plane_sum(fx0[0], fy0[0], v2[0]) + fz0[1] * v2[1]
    r1 = b0[1] - dg0[1] * v2[1] + plane_sum(fx0[1], fy0[1], v2[1]) + fz0[1] * v2[0]
    b1 = down0(r0, r1)
    recv_far = launch(regions.at[1], regions.at[0], far_reg, big_send, big_recv, FAR)
    recv_gk()
    e2 = 0.5 * (gk[0] + gk[1]).reshape(n // 2 * quarter, LANES)
    k2 = back(e2, 1, LANES // 2)
    coarse = coarse_cycle(e2, k2, n // 2, quarter, 16.0, 16.0)
    recv_term()
    b1 = b1 + halo1[TERM, 0] + halo1[TERM, 1]

    def beside1(mine, i):
        return plane_sum(fx1, fy1, mine) + fz1lo * halo1[i, 0] + fz1hi * halo1[i, 1]

    def trade1(value, i):
        plane1[i] = value
        launch(plane1.at[i], plane1.at[i], halo1.at[i], small_send, small_recv, i)()

    a = wt1 * b1
    trade1(a, A1)
    a = (1.0 - DAMPING) * a + wt1 * (b1 + beside1(a, A1))
    trade1(a, A2)
    full = down1(b1 - dg1 * a + beside1(a, A2))
    gb[core, chip] = full[:quarter // 2] + back(full[quarter // 2:], 1, LANES // 2)
    share(gb, 2)
    recv_v2()
    base[0] = sweep0(0, v2[0], halo0[2, 0], v2[1])
    base[1] = sweep0(1, v2[1], v2[0], halo0[2, 1])
    recv_base = launch(base.at[0], base.at[1], halo0.at[3], big_send, big_recv, BASE)
    relay_gb = relay(gb, 2)
    recv_far()
    for p in range(2):
        region = halo_reg[p]
        beyond = face(e_side[p], dielectric(far_reg[p]), 1.0)
        fx, fy, total = plane_faces(e_side[p], 1.0)
        fxh[p] = fx
        fyh[p] = fy
        fzh[p] = beyond
        wth[p] = DAMPING / (total + beyond + fz0[2 * p] + jnp.where(region == 2, SCREEN, 0.0))
    relay_gb()
    packed = 0.5 * (gb[0] + gb[1]).reshape(n // 2 * quarter // 2, LANES)
    split = (n // 2, quarter // 2, LANES)
    b2 = jnp.concatenate(
        [packed.reshape(split), back(packed, 1, LANES // 2).reshape(split)], axis=1
    ).reshape(n // 2 * quarter, LANES)
    c2 = coarse(b2)

    for i in range(n // 2):
        c2_planes[i] = c2[i * quarter:(i + 1) * quarter]
    grow_l, grow_r = spread_left(half, quarter), spread_right(LANES, half, half)

    def up1(index):
        return dot(grow_l, times(c2_planes[index // 2], grow_r))

    halo1[A2, 0] = halo1[A2, 0] + jnp.where(has_lo, up1(jnp.maximum(me - 1, 0)), 0.0)
    halo1[A2, 1] = halo1[A2, 1] + jnp.where(has_hi, up1(jnp.minimum(me + 1, n - 1)), 0.0)
    a = a + up1(me)
    a = (1.0 - DAMPING) * a + wt1 * (b1 + beside1(a, A2))
    trade1(a, A3)
    a = (1.0 - DAMPING) * a + wt1 * (b1 + beside1(a, A3))
    trade1(a, A4)

    big_l, big_r = spread_left(nxy, half), spread_right(half, nxy, nxy)

    def up0(c):
        return dot(big_l, times(c, big_r))

    mine = up0(a)
    recv_base()
    v3, side = [], []
    present = [has_lo, has_hi]
    for p in range(2):
        c = up0(halo1[A4, p])
        own = plane_sum(fx0[p], fy0[p], mine) + fz0[1] * mine + fz0[2 * p] * c
        v3.append(base[p] + (1.0 - DAMPING) * mine + wt0[p] * own)
        other = plane_sum(fxh[p], fyh[p], c) + fzh[p] * c + fz0[2 * p] * mine
        swept = halo0[3, p] + (1.0 - DAMPING) * c + wth[p] * other
        side.append(jnp.where(present[p], swept, 0.0))
    out[0] = sweep0(0, v3[0], side[0], v3[1])
    out[1] = sweep0(1, v3[1], v3[0], side[1])

    for sent in pending:
        sent()
    all_in(got, many_send, 0)


HALO = 16
REG_LO, REG_HI, V0_LO, V0_HI, V1_LO, V1_HI, V2_LO, V2_HI, BASE_LO, BASE_HI = range(10)
E_M1, E_P1, E_M2, E_P2, K_M1, K_P1, B_M1, B_P1, B_M2, B_P2, A3_LO, A3_HI, NEAR_LO, NEAR_HI = range(10, 24)
MESSAGES = 24


def box_kernel(n, partials, regions, previous, out,
               parts, dens, reg, v0, b0, fx0, fy0, fz0, dg0, wt0, v1, v2, base, swept,
               near, fxn, fyn, fzn, wtn, landed, corr,
               e1, k1, fx1, fy1, fz1, dg1, wt1, pack, from_lo, from_hi, far_lo, far_hi,
               b1, a1, a2, a3, a4, gk, gb, c2_planes,
               load_sem, spread_send, spread_recv, corr_send, corr_recv, dens_send, dens_recv,
               side_send, side_recv, many_send, many_recv):
    me = lax.axis_index("slab")
    nz = n // 2
    z, x, core = me // 4, lax.rem(me // 2, 2), lax.rem(me, 2)
    zi = 2 * z + core
    nxy = regions.shape[1]
    half, quarter = nxy // 2, nxy // 4
    rows = partials.shape[2]
    window = half + HALO
    window1 = window // 2
    blocks = window // rows
    first = half - HALO

    def peer(index):
        return {"slab": index}

    def at(i, j):
        return (i // 2) * 4 + j * 2 + lax.rem(i, 2)

    load = pltpu.make_async_copy(partials, parts, load_sem.at[0])
    load.start()
    load_near = pltpu.make_async_copy(regions, near.at[pl.ds(2, 2)], load_sem.at[1])
    load_near.start()
    barrier = pltpu.get_barrier_semaphore()

    def greet(off, carry):
        pl.semaphore_signal(barrier, inc=1, device_id=peer(lax.rem(me + off, n)),
                            device_id_type=pl.DeviceIdType.MESH)
        return carry

    lax.fori_loop(1, n, greet, 0)

    plane0 = jnp.zeros((window, nxy), F32)
    plane1 = jnp.zeros((window1, half), F32)

    @pl.when(zi == 0)
    def _():
        reg[0] = jnp.zeros((window, nxy), jnp.int32)
        for v in (v0, v1, v2, base):
            v[0] = plane0
        for i in range(3):
            from_lo[i] = plane1
        for i in range(2):
            e1[i] = plane1 + 1.0
            k1[i] = plane1
        a3[0] = plane1

    @pl.when(zi == nz - 1)
    def _():
        reg[5] = jnp.zeros((window, nxy), jnp.int32)
        for v in (v0, v1, v2, base):
            v[5] = plane0
        for i in range(3):
            from_hi[i] = plane1
        for i in range(2):
            e1[6 + i] = plane1 + 1.0
            k1[4 + i] = plane1
        a3[3] = plane1

    @pl.when(zi < 2)
    def _():
        far_lo[0] = plane1

    @pl.when(zi >= nz - 2)
    def _():
        far_hi[0] = plane1

    @pl.when(me == 0)
    def _():
        near[0] = jnp.zeros((nxy, nxy), jnp.int32)
        near[1] = jnp.zeros((nxy, nxy), jnp.int32)
        corr[0] = jnp.zeros((half, half), F32)

    @pl.when(me == n - 1)
    def _():
        near[4] = jnp.zeros((nxy, nxy), jnp.int32)
        near[5] = jnp.zeros((nxy, nxy), jnp.int32)
        corr[2] = jnp.zeros((half, half), F32)

    load.wait()
    density = parts[0].astype(F32)
    for g in range(1, partials.shape[0]):
        density = density + parts[g].astype(F32)
    dens[...] = (SOURCE * density).reshape(dens.shape)

    pl.semaphore_wait(barrier, n - 1)
    pending = []

    def spread(src, dst, i):
        for j in range(2):
            target = at(2 * z + x, j)
            piece = src.at[:, pl.ds(first * j, window), :]
            place = dst.at[pl.ds(1 + 2 * core, 2)]
            remote = pltpu.make_async_remote_copy(
                src_ref=piece, dst_ref=place, send_sem=spread_send.at[i, j],
                recv_sem=spread_recv.at[i, core], device_id=peer(target),
                device_id_type=pl.DeviceIdType.MESH)
            here = pltpu.make_async_copy(piece, place, spread_recv.at[i, core])
            away = target != me
            pl.when(away)(remote.start)
            pl.when(jnp.logical_not(away))(here.start)
            pending.append(lambda remote=remote, away=away: pl.when(away)(remote.wait_send))

        def arrived():
            for j in range(2):
                place = dst.at[pl.ds(1 + 2 * j, 2)]
                pltpu.make_async_copy(place, place, spread_recv.at[i, j]).wait()

        return arrived

    def send_density(step, carry):
        other = lax.rem(me + 1 + lax.rem(step + n // 2 - 1, n), n)
        oz, ox = 2 * (other // 4) + lax.rem(other, 2), lax.rem(other // 2, 2)
        block = me - (first // rows) * ox
        inside = (block >= 0) & (block < blocks)
        block = jnp.clip(block, 0, blocks - 1)
        place = b0.at[:, pl.ds(pl.multiple_of(block * rows, rows), rows), :]

        @pl.when(inside & (other != me))
        def _():
            pltpu.make_async_remote_copy(
                src_ref=dens.at[oz], dst_ref=place, send_sem=dens_send.at[other],
                recv_sem=dens_recv.at[0], device_id=peer(other),
                device_id_type=pl.DeviceIdType.MESH).start()

        @pl.when(inside & (other == me))
        def _():
            pltpu.make_async_copy(dens.at[oz], place, dens_recv.at[0]).start()

        return carry

    def sent_density(other, carry):
        ox = lax.rem(other // 2, 2)
        block = me - (first // rows) * ox

        @pl.when((block >= 0) & (block < blocks) & (other != me))
        def _():
            pltpu.make_async_copy(dens.at[0], dens.at[0], dens_send.at[other]).wait()

        return carry

    def push(src, dst, delta, i):
        can_send = (zi + delta >= 0) & (zi + delta < nz)
        can_recv = (zi - delta >= 0) & (zi - delta < nz)
        copy = pltpu.make_async_remote_copy(
            src_ref=src, dst_ref=dst, send_sem=side_send.at[i], recv_sem=side_recv.at[i],
            device_id=peer(at(jnp.clip(zi + delta, 0, nz - 1), x)),
            device_id_type=pl.DeviceIdType.MESH)
        pl.when(can_send)(copy.start)
        pending.append(lambda: pl.when(can_send)(copy.wait_send))
        return lambda: pl.when(can_recv)(copy.wait_recv)

    def trade(field, low, high, i):
        down = push(field.at[low], field.at[high + 1], -1, i)
        up = push(field.at[high], field.at[low - 1], 1, i + 1)

        def arrived():
            down()
            up()

        return arrived

    reg_in = spread(regions, reg, 0)
    v0_in = spread(previous, v0, 1)
    lax.fori_loop(0, n, send_density, 0)

    def dielectric(r):
        return jnp.where(r == 0, INSIDE, SOLVENT).astype(F32)

    right0, left0 = pool_right(nxy, half, nxy), pool_left(window1, window)
    right1 = pool_right(half, LANES, half)
    dst1, src1 = iota((quarter // 2, window1), 0), iota((quarter // 2, window1), 1)
    left1 = jnp.where((src1 - (HALO // 2) * x) // 2 == dst1, 1.0, 0.0).astype(F32)

    def down0(a):
        return 0.125 * dot(left0, times(a, right0))

    def down1(a):
        return 0.125 * dot(left1, times(a, right1))

    reg_in()
    reg_halo = trade(reg, 1, 4, REG_LO)
    e = [dielectric(reg[p]) for p in range(1, 5)]
    k = [jnp.where(reg[p] == 2, SCREEN, 0.0).astype(F32) for p in range(1, 5)]
    for i in range(2):
        e1[3 + i] = down0(e[2 * i] + e[2 * i + 1])
        k1[2 + i] = down0(k[2 * i] + k[2 * i + 1])
    e1_in = [push(e1.at[pl.ds(3, 2)], e1.at[pl.ds(1, 2)], 1, E_P1),
             push(e1.at[pl.ds(3, 2)], e1.at[pl.ds(5, 2)], -1, E_M1),
             push(e1.at[pl.ds(4, 1)], e1.at[pl.ds(0, 1)], 2, E_P2),
             push(e1.at[pl.ds(3, 1)], e1.at[pl.ds(7, 1)], -2, E_M2),
             push(k1.at[pl.ds(2, 2)], k1.at[pl.ds(0, 2)], 1, K_P1),
             push(k1.at[pl.ds(2, 2)], k1.at[pl.ds(4, 2)], -1, K_M1)]
    chip = me // 2
    gk[core, chip] = down1(e1[3] + e1[4]) + back(down1(k1[2] + k1[3]), 1, LANES // 2)

    def share(ref, i):
        def one(off, carry):
            other = lax.rem(me + 2 * off, n)
            pltpu.make_async_remote_copy(
                src_ref=ref.at[core, chip], dst_ref=ref.at[core, chip], send_sem=many_send.at[i],
                recv_sem=many_recv.at[i], device_id=peer(other),
                device_id_type=pl.DeviceIdType.MESH).start()
            return carry

        lax.fori_loop(1, n // 2, one, 0)

    def relay(ref, i):
        seven = ref.at[0, pl.ds(0, n // 2 - 1)]
        pltpu.make_async_copy(seven, seven, many_recv.at[i]).wait()
        copy = pltpu.make_async_remote_copy(
            src_ref=ref.at[core], dst_ref=ref.at[core], send_sem=many_send.at[i + 2],
            recv_sem=many_recv.at[i + 2], device_id=peer(me + 1 - 2 * core),
            device_id_type=pl.DeviceIdType.MESH)
        copy.start()
        pending.append(pltpu.make_async_copy(seven, seven, many_send.at[i]).wait)
        pending.append(copy.wait_send)
        return copy.wait_recv

    def in_order(ref):
        return [ref[c, 2 * i + j] for i in range(n // 4) for c in range(2) for j in range(2)]

    share(gk, 0)

    totals = []
    for p in range(4):
        fx, fy, total = plane_faces(e[p], 1.0)
        fx0[p] = fx
        fy0[p] = fy
        totals.append(total + k[p])
    for p in range(1, 4):
        fz0[p] = face(e[p - 1], e[p], 1.0)
    v0_in()
    v0_halo = trade(v0, 1, 4, V0_LO)

    def beside0(p, v):
        return (plane_sum(fx0[p], fy0[p], v[p + 1]) + fz0[p] * v[p] + fz0[p + 1] * v[p + 2])

    def sweep0(p, v):
        return (1.0 - DAMPING) * v[p + 1] + wt0[p] * (b0[p] + beside0(p, v))

    def first_part(p):
        v1[p + 1] = (1.0 - DAMPING) * v0[p + 1] + wt0[p] * beside0(p, v0)

    def weights(p):
        diag = totals[p] + fz0[p] + fz0[p + 1]
        dg0[p] = diag
        wt0[p] = DAMPING / diag

    for p in (1, 2):
        weights(p)
        first_part(p)
    reg_halo()
    fz0[0] = face(jnp.where(zi > 0, dielectric(reg[0]), e[0]), e[0], 1.0)
    fz0[4] = face(e[3], jnp.where(zi < nz - 1, dielectric(reg[5]), e[3]), 1.0)
    weights(0)
    weights(3)
    v0_halo()
    first_part(0)
    first_part(3)

    pltpu.make_async_copy(b0, b0, dens_recv.at[0]).wait()
    for p in (0, 3):
        v1[p + 1] = v1[p + 1] + wt0[p] * b0[p]
    v1_halo = trade(v1, 1, 4, V1_LO)
    for p in (1, 2):
        v1[p + 1] = v1[p + 1] + wt0[p] * b0[p]

    def push_near(delta, slot, i):
        can_send = (me + delta >= 0) & (me + delta < n)
        can_recv = (me - delta >= 0) & (me - delta < n)
        copy = pltpu.make_async_remote_copy(
            src_ref=regions, dst_ref=near.at[pl.ds(slot, 2)], send_sem=side_send.at[i],
            recv_sem=side_recv.at[i], device_id=peer(jnp.clip(me + delta, 0, n - 1)),
            device_id_type=pl.DeviceIdType.MESH)
        pl.when(can_send)(copy.start)
        pending.append(lambda: pl.when(can_send)(copy.wait_send))
        return lambda: pl.when(can_recv)(copy.wait_recv)

    near_in = [push_near(1, 0, NEAR_LO), push_near(-1, 4, NEAR_HI)]
    gk_in = relay(gk, 0)
    for arrived in e1_in:
        arrived()

    @pl.when(zi == 0)
    def _():
        e1[2] = e1[3]
        e1[0] = plane1 + 1.0

    @pl.when(zi == 1)
    def _():
        e1[0] = e1[1]

    @pl.when(zi == nz - 1)
    def _():
        e1[5] = e1[4]
        e1[7] = plane1 + 1.0

    @pl.when(zi == nz - 2)
    def _():
        e1[7] = e1[6]

    s1 = 4.0
    for i in range(7):
        fz1[i] = face(e1[i], e1[i + 1], s1)
    for i in range(6):
        fx, fy, total = plane_faces(e1[i + 1], s1)
        fx1[i] = fx
        fy1[i] = fy
        diag = total + fz1[i] + fz1[i + 1] + k1[i]
        dg1[i] = diag
        weight = DAMPING / diag
        if i < 2:
            weight = jnp.where(zi > 0, weight, 0.0)
        if i > 3:
            weight = jnp.where(zi < nz - 1, weight, 0.0)
        wt1[i] = weight

    for p in (1, 2):
        v2[p + 1] = sweep0(p, v1)
    v1_halo()
    for p in (0, 3):
        v2[p + 1] = sweep0(p, v1)
    v2_halo = trade(v2, 1, 4, V2_LO)
    pack[0] = down0(fz0[4] * v2[4])
    pack[3] = down0(fz0[0] * v2[1])

    def left_over(p):
        r = b0[p] - dg0[p] * v2[p + 1] + plane_sum(fx0[p], fy0[p], v2[p + 1])
        if p > 0:
            r = r + fz0[p] * v2[p]
        if p < 3:
            r = r + fz0[p + 1] * v2[p + 2]
        return r

    for i in range(2):
        pack[1 + i] = down0(left_over(2 * i) + left_over(2 * i + 1))
    b1_in = [push(pack.at[pl.ds(0, 3)], from_lo, 1, B_P1),
             push(pack.at[pl.ds(1, 3)], from_hi, -1, B_M1),
             push(pack.at[pl.ds(0, 1)], far_lo, 2, B_P2),
             push(pack.at[pl.ds(3, 1)], far_hi, -2, B_M2)]
    gk_in()
    e2 = jnp.concatenate(in_order(gk), axis=0)
    coarse = coarse_cycle(e2, back(e2, 1, LANES // 2), nz, quarter, 16.0, 16.0)
    v2_halo()
    for p in (0, 3, 1, 2):
        base[p + 1] = sweep0(p, v2)
    base_halo = trade(base, 1, 4, BASE_LO)
    for arrived in b1_in:
        arrived()
    b1[0] = from_lo[1] + far_lo[0]
    b1[1] = from_lo[2] + pack[3]
    b1[2] = pack[1] + from_lo[0]
    b1[3] = pack[2] + from_hi[2]
    b1[4] = from_hi[0] + pack[0]
    b1[5] = from_hi[1] + far_hi[0]

    def beside1(i, mine, below, above):
        return plane_sum(fx1[i], fy1[i], mine) + fz1[i] * below + fz1[i + 1] * above

    def sweep1(i, mine, below, above):
        return (1.0 - DAMPING) * mine + wt1[i] * (b1[i] + beside1(i, mine, below, above))

    for i in range(6):
        a1[i] = wt1[i] * b1[i]
    for i in range(1, 5):
        a2[i - 1] = sweep1(i, a1[i], a1[i - 1], a1[i + 1])
    rest = [b1[i] - dg1[i] * a2[i - 1] + beside1(i, a2[i - 1], a2[i - 2], a2[i]) for i in (2, 3)]
    full = down1(rest[0] + rest[1])
    gb[core, chip] = full[:quarter // 4] + back(full[quarter // 4:], 1, LANES // 2)
    share(gb, 1)
    load_near.wait()
    for arrived in near_in:
        arrived()
    en = [dielectric(near[f]) for f in range(6)]
    fzn[0] = face(en[0], en[1], 1.0)
    fzn[1] = face(jnp.where(me > 0, en[1], en[2]), en[2], 1.0)
    fzn[2] = face(en[2], en[3], 1.0)
    fzn[3] = face(en[3], jnp.where(me < n - 1, en[4], en[3]), 1.0)
    fzn[4] = face(en[4], en[5], 1.0)
    for f in range(4):
        fx, fy, total = plane_faces(en[f + 1], 1.0)
        fxn[f] = fx
        fyn[f] = fy
        kn = jnp.where(near[f + 1] == 2, SCREEN, 0.0).astype(F32)
        wtn[f] = DAMPING / (total + kn + fzn[f] + fzn[f + 1])
    gb_in = relay(gb, 1)
    base_halo()

    def deliver(j):
        target = 4 * z + 2 * core + j
        piece = swept.at[pl.ds(2 * j, 2), pl.ds(pl.multiple_of(HALO * x, HALO), half), :]
        place = landed.at[:, pl.ds(pl.multiple_of(half * x, half), half), :]
        remote = pltpu.make_async_remote_copy(
            src_ref=piece, dst_ref=place, send_sem=spread_send.at[2, j],
            recv_sem=spread_recv.at[2, x], device_id=peer(target),
            device_id_type=pl.DeviceIdType.MESH)
        here = pltpu.make_async_copy(piece, place, spread_recv.at[2, x])
        away = target != me
        pl.when(away)(remote.start)
        pl.when(jnp.logical_not(away))(here.start)
        pending.append(lambda: pl.when(away)(remote.wait_send))

    for p in range(4):
        swept[p] = sweep0(p, base)
        if p % 2:
            deliver(p // 2)
    gb_in()
    packed = jnp.stack(in_order(gb))
    b2 = jnp.concatenate([packed, back(packed.reshape(-1, LANES), 1, LANES // 2).reshape(packed.shape)],
                         axis=1).reshape(nz * quarter, LANES)
    c2 = coarse(b2)
    for i in range(nz):
        c2_planes[i] = c2[i * quarter:(i + 1) * quarter]
    fine, mid = iota((window1, quarter), 0), iota((window1, quarter), 1)
    grow_l = jnp.where((fine + first // 2 * x) // 2 == mid, 1.0, 0.0).astype(F32)
    grow_r = spread_right(LANES, half, half)

    def up1(index):
        return dot(grow_l, times(c2_planes[index], grow_r))

    mine = up1(zi)
    a2[0] = a2[0] + jnp.where(zi > 0, up1(jnp.maximum(zi - 1, 0)), 0.0)
    a2[3] = a2[3] + jnp.where(zi < nz - 1, up1(jnp.minimum(zi + 1, nz - 1)), 0.0)
    a2[1] = a2[1] + mine
    a2[2] = a2[2] + mine
    for i in (1, 2):
        a3[i] = sweep1(i + 1, a2[i], a2[i - 1], a2[i + 1])
    trade(a3, 1, 2, A3_LO)()
    for i in (1, 2):
        a4[i] = sweep1(i + 1, a3[i], a3[i - 1], a3[i + 1])

    def hand(count, low, delta, slot, i):
        target = 2 * zi + delta
        exists = (target >= 0) & (target < n)
        piece = a4.at[pl.ds(low, count), pl.ds(pl.multiple_of(HALO // 2 * x, HALO // 2), quarter), :]
        place = corr.at[pl.ds(slot, count), pl.ds(pl.multiple_of(quarter * x, quarter), quarter), :]
        kind = 2 - count
        remote = pltpu.make_async_remote_copy(
            src_ref=piece, dst_ref=place, send_sem=corr_send.at[i], recv_sem=corr_recv.at[kind, x],
            device_id=peer(jnp.clip(target, 0, n - 1)), device_id_type=pl.DeviceIdType.MESH)
        here = pltpu.make_async_copy(piece, place, corr_recv.at[kind, x])
        away = exists & (target != me)
        pl.when(away)(remote.start)
        pl.when(target == me)(here.start)
        pending.append(lambda: pl.when(away)(remote.wait_send))

    hand(2, 1, 0, 1, 0)
    hand(2, 1, 1, 0, 1)
    hand(1, 1, -1, 2, 2)
    hand(1, 2, 2, 0, 3)
    big_l, big_r = spread_left(nxy, half), spread_right(half, nxy, nxy)

    def up0(c):
        return dot(big_l, times(c, big_r))

    single = jnp.where(lax.rem(me, 2) == 0, me > 0, me < n - 1)
    for j in range(2):
        both = corr.at[pl.ds(0, 2), pl.ds(quarter * j, quarter), :]
        pltpu.make_async_copy(both, both, corr_recv.at[0, j]).wait()
        one = corr.at[pl.ds(0, 1), pl.ds(quarter * j, quarter), :]
        pl.when(single)(pltpu.make_async_copy(one, one, corr_recv.at[1, j]).wait)
    for j in range(2):
        place = landed.at[:, pl.ds(half * j, half), :]
        pltpu.make_async_copy(place, place, spread_recv.at[2, j]).wait()
    below, here, above = (up0(corr[i]) for i in range(3))
    spans = [(below, below, here), (here, below, here), (here, here, above), (above, here, above)]

    def relax(f, mine, low, high):
        return (1.0 - DAMPING) * mine + wtn[f] * (
            plane_sum(fxn[f], fyn[f], mine) + fzn[f] * low + fzn[f + 1] * high)

    y = [relax(f, *spans[f]) for f in range(4)]
    y[0] = jnp.where(me > 0, y[0], 0.0)
    y[3] = jnp.where(me < n - 1, y[3], 0.0)
    for f in (1, 2):
        out[f - 1] = landed[f - 1] + relax(f, y[f], y[f - 1], y[f + 1])
    for sent in pending:
        sent()
    lax.fori_loop(0, n, sent_density, 0)


def box_local(partials, regions, previous):
    n = lax.axis_size("slab")
    nxy = regions.shape[1]
    half, quarter = nxy // 2, nxy // 4
    rows = partials.shape[2]
    window, window1 = half + HALO, (half + HALO) // 2
    vmem = lambda *shape: pltpu.VMEM(shape, F32)
    big = lambda count: vmem(count, window, nxy)
    small = lambda count: vmem(count, window1, half)
    return pl.pallas_call(
        functools.partial(box_kernel, n),
        out_shape=pltpu.VMEM(previous.shape, F32),
        in_specs=[pl.BlockSpec(memory_space=pltpu.HBM)] * 3,
        out_specs=pl.BlockSpec(memory_space=pltpu.VMEM),
        scratch_shapes=[
            pltpu.VMEM(partials.shape, partials.dtype), vmem(n // 2, 4, rows, nxy),
            pltpu.VMEM((6, window, nxy), jnp.int32), big(6), big(4),
            big(4), big(4), big(5), big(4), big(4), big(6), big(6), big(6), big(4),
            pltpu.VMEM((6, nxy, nxy), jnp.int32), vmem(4, nxy, nxy), vmem(4, nxy, nxy),
            vmem(5, nxy, nxy), vmem(4, nxy, nxy), vmem(2, nxy, nxy), vmem(3, half, half),
            small(8), small(6), small(6), small(6), small(7), small(6), small(6),
            small(4), small(3), small(3), small(1), small(1),
            small(6), small(6), small(4), small(4), small(4),
            vmem(2, n // 2, quarter // 2, LANES), vmem(2, n // 2, quarter // 4, LANES),
            vmem(n // 2, quarter, LANES),
            pltpu.SemaphoreType.DMA((2,)),
            pltpu.SemaphoreType.DMA((3, 2)), pltpu.SemaphoreType.DMA((3, 2)),
            pltpu.SemaphoreType.DMA((4,)), pltpu.SemaphoreType.DMA((2, 2)),
            pltpu.SemaphoreType.DMA((n,)), pltpu.SemaphoreType.DMA((1,)),
            pltpu.SemaphoreType.DMA((MESSAGES,)), pltpu.SemaphoreType.DMA((MESSAGES,)),
            pltpu.SemaphoreType.DMA((4,)), pltpu.SemaphoreType.DMA((4,)),
        ],
        compiler_params=pltpu.CompilerParams(
            collective_id=1, has_side_effects=True, vmem_limit_bytes=60 * 1024 * 1024),
    )(partials, regions, previous)


def local(partials, regions, previous):
    n = lax.axis_size("slab")
    nxy = regions.shape[1]
    half, quarter = nxy // 2, nxy // 4
    rows = partials.shape[2]
    vmem = lambda *shape: pltpu.VMEM(shape, F32)
    spec = pl.BlockSpec(memory_space=pltpu.VMEM)
    return pl.pallas_call(
        functools.partial(kernel, n),
        out_shape=jax.ShapeDtypeStruct(previous.shape, F32),
        in_specs=[spec] * 3,
        out_specs=spec,
        scratch_shapes=[
            vmem(n, 2, rows, nxy), vmem(n, 2, rows, nxy), vmem(2, nxy, nxy),
            vmem(2, nxy, nxy), vmem(2, nxy, nxy), vmem(3, nxy, nxy), vmem(2, nxy, nxy),
            vmem(2, nxy, nxy),
            pltpu.VMEM((2, nxy, nxy), jnp.int32), pltpu.VMEM((2, nxy, nxy), jnp.int32),
            vmem(2, nxy, nxy), vmem(2, nxy, nxy), vmem(2, nxy, nxy), vmem(2, nxy, nxy),
            vmem(4, 2, nxy, nxy),
            vmem(2, nxy, nxy), vmem(2, nxy, nxy), vmem(2, nxy, nxy),
            vmem(6, 2, half, half), vmem(5, half, half), vmem(2, half, half),
            vmem(2, n // 2, quarter // 2, LANES), vmem(2, n // 2, quarter, LANES),
            pltpu.SemaphoreType.DMA((6, 2)), pltpu.SemaphoreType.DMA((6, 2)),
            pltpu.SemaphoreType.DMA((6, 2)), pltpu.SemaphoreType.DMA((6, 2)),
            pltpu.SemaphoreType.DMA((5,)), pltpu.SemaphoreType.DMA((5,)),
            vmem(n // 2, quarter, LANES),
        ],
        compiler_params=pltpu.CompilerParams(
            collective_id=0, has_side_effects=True, vmem_limit_bytes=60 * 1024 * 1024),
    )(partials, regions, previous)


def solution(mesh):
    in_specs = (
        P("job", None, "slab", None),
        P(("job", "slab"), None, None),
        P(("job", "slab"), None, None),
    )
    out_specs = P(("job", "slab"), None, None)
    size = mesh.shape["slab"]

    def fits(partials, regions):
        return (size == 16 and partials.shape[2] == 16 * size and partials.shape[1] == 2 * size
                and regions.shape[1] == 16 * size)

    def program(partials, regions, previous):
        chosen = box_local if fits(partials, regions) else local
        return jax.shard_map(chosen, mesh=mesh, in_specs=in_specs, out_specs=out_specs, check_vma=False)(
            partials, regions, previous)

    return program
```

```python
import functools

import jax
import jax.numpy as jnp
from jax import lax
from jax.experimental import pallas as pl
from jax.experimental.pallas import tpu as pltpu
from jax.sharding import PartitionSpec as P

PRE_SWEEPS = 2
POST_SWEEPS = 2
COARSE_SWEEPS = 4

DAMPING = 0.75
INSIDE = 2.0
SOLVENT = 78.4
SCREEN = 1.4
SOURCE = 16.0 * 3.141592653589793

F32 = jnp.float32
LANES = 128


def iota(shape, dim):
    return lax.broadcasted_iota(jnp.int32, shape, dim)


def face(mine, other, spacing):
    return mine * other / ((mine + other) * (0.5 * spacing))


def back(v, dim, by=1):
    return pltpu.roll(v, by, dim)


def ahead(v, dim, by=1):
    return pltpu.roll(v, v.shape[dim] - by, dim)


def terms(v):
    result = []
    for _ in range(3):
        result.append(v.astype(jnp.bfloat16))
        v = v - result[-1].astype(F32)
    return result


def product(a, b):
    return lax.dot_general(a, b, (((1,), (0,)), ((), ())), preferred_element_type=F32)


def times(v, selector):
    high, middle, low = (product(t, selector.astype(jnp.bfloat16)) for t in terms(v))
    return high + (middle + low)


def dot(selector, v):
    high, middle, low = (product(selector.astype(jnp.bfloat16), t) for t in terms(v))
    return high + (middle + low)


def halves(v):
    high = v.astype(jnp.bfloat16)
    return high, (v - high.astype(F32)).astype(jnp.bfloat16)


def times2(v, selector):
    high, low = (product(t, selector.astype(jnp.bfloat16)) for t in halves(v))
    return high + low


def dot2(selector, v):
    high, low = (product(selector.astype(jnp.bfloat16), t) for t in halves(v))
    return high + low


def pool_right(wide, narrow, valid):
    src, dst = iota((wide, narrow), 0), iota((wide, narrow), 1)
    return jnp.where((src // 2 == dst) & (src < valid), 1.0, 0.0).astype(F32)


def pool_left(narrow, wide):
    dst, src = iota((narrow, wide), 0), iota((narrow, wide), 1)
    return jnp.where(src // 2 == dst, 1.0, 0.0).astype(F32)


def spread_right(narrow, wide, valid):
    src, dst = iota((narrow, wide), 0), iota((narrow, wide), 1)
    return jnp.where((dst // 2 == src) & (dst < valid), 1.0, 0.0).astype(F32)


def spread_left(wide, narrow):
    dst, src = iota((wide, narrow), 0), iota((wide, narrow), 1)
    return jnp.where(dst // 2 == src, 1.0, 0.0).astype(F32)


def plane_faces(e, spacing):
    rows, cols = e.shape
    x, y = iota(e.shape, 0), iota(e.shape, 1)
    fx = jnp.where(x > 0, face(e, back(e, 0), spacing), 0.0)
    fy = jnp.where(y > 0, face(e, back(e, 1), spacing), 0.0)
    edges = (jnp.where((x == 0) | (x == rows - 1), 1.0, 0.0)
             + jnp.where((y == 0) | (y == cols - 1), 1.0, 0.0))
    total = fx + ahead(fx, 0) + fy + ahead(fy, 1) + edges * e * (1.0 / spacing)
    return fx, fy, total


def plane_sum(fx, fy, v):
    return fx * back(v, 0) + ahead(fx * v, 0) + fy * back(v, 1) + ahead(fy * v, 1)


def coarse_cycle(e, k, planes, nx, sz, sx, dot, times):
    rows = e.shape[0]
    row, lane = iota(e.shape, 0), iota(e.shape, 1)
    x, z = row % nx, row // nx
    valid = (row < planes * nx) & (lane < nx)
    e = jnp.where(valid, e, 1.0)
    fx = jnp.where(valid & (x > 0), face(e, back(e, 0), sx), 0.0) if nx > 1 else None
    fy = jnp.where(valid & (lane > 0), face(e, back(e, 1), sx), 0.0) if nx > 1 else None
    wrap = nx % rows
    fz = jnp.where(valid & (z > 0), face(e, back(e, 0, wrap), sz), 0.0) if planes > 1 else None
    diag = k + e * (
        (jnp.where(x == 0, 1.0, 0.0) + jnp.where(x == nx - 1, 1.0, 0.0)
         + jnp.where(lane == 0, 1.0, 0.0) + jnp.where(lane == nx - 1, 1.0, 0.0)) * (1.0 / sx)
        + (jnp.where(z == 0, 1.0, 0.0) + jnp.where(z == planes - 1, 1.0, 0.0)) * (1.0 / sz))
    if nx > 1:
        diag = diag + fx + ahead(fx, 0) + fy + ahead(fy, 1)
    if planes > 1:
        diag = diag + fz + ahead(fz, 0, wrap)
    w = jnp.where(valid, DAMPING / jnp.where(valid, diag, 1.0), 0.0)

    def beside(v):
        total = jnp.zeros_like(v)
        if nx > 1:
            total = plane_sum(fx, fy, v)
        if planes > 1:
            total = total + fz * back(v, 0, wrap) + ahead(fz * v, 0, wrap)
        return total

    def sweep(v, b):
        return (1.0 - DAMPING) * v + w * (b + beside(v))

    def coarsest(b):
        v = w * b
        for _ in range(COARSE_SWEEPS - 1):
            v = sweep(v, b)
        return v

    if planes == 1:
        return coarsest
    halve = nx > 1 and nx % 2 == 0
    nx2 = nx // 2 if halve else nx
    sx2 = sx * 4.0 if halve else sx
    step = planes
    while step * nx > 512 and step % 4 == 0:
        step //= 2
    part = step * nx
    if step == planes:
        part = rows
    real2 = planes // 2 * nx2
    rows2 = max(8, real2)
    part2 = rows2 if step == planes else step // 2 * nx2
    ratio = 2 if halve else 1

    def member(fine, coarse):
        return ((fine < step * nx) & ((fine // nx // 2) * nx2 + fine % nx // ratio == coarse))

    down = jnp.where(member(iota((part2, part), 1), iota((part2, part), 0)), 1.0, 0.0)
    up = jnp.where(member(iota((part, part2), 0), iota((part, part2), 1)), 1.0, 0.0)
    if halve:
        right = pool_right(LANES, LANES, nx)
        left = spread_right(LANES, LANES, nx)
        scale = 0.125
    else:
        scale = 0.5

    def coarsen(f):
        if halve:
            f = times(f, right)
        parts = [dot(down, f[i:i + part]) for i in range(0, rows, part)]
        return scale * (parts[0] if len(parts) == 1 else jnp.concatenate(parts, axis=0))

    def refine(f):
        if halve:
            f = times(f, left)
        parts = [dot(up, f[i:i + part2]) for i in range(0, rows2, part2)]
        return parts[0] if len(parts) == 1 else jnp.concatenate(parts, axis=0)

    below = coarse_cycle(coarsen(jnp.where(valid, e, 0.0)), coarsen(k),
                         planes // 2, nx2, sz * 4.0, sx2, dot, times)

    def run(b):
        v = w * b
        for _ in range(PRE_SWEEPS - 1):
            v = sweep(v, b)
        r = jnp.where(valid, b - diag * v + beside(v), 0.0)
        v = v + refine(below(coarsen(r)))
        for _ in range(POST_SWEEPS):
            v = sweep(v, b)
        return v

    return run


REG, V0, V1, V2, BASE, FAR = range(6)
E1, A1, A2, A3, A4, TERM = range(6)


def kernel(n, partials, regions, previous, out,
           dens, got, b0, fx0, fy0, fz0, dg0, wt0, halo_reg, far_reg, fxh, fyh, fzh, wth, halo0, v1, v2, base,
           halo1, plane1, term1, gb, gk,
           big_send, big_recv, small_send, small_recv, many_send, many_recv, c2_planes):
    me = lax.axis_index("slab")
    job = lax.axis_index("job")
    nxy = regions.shape[1]
    half = nxy // 2
    quarter = nxy // 4
    rows = partials.shape[2]
    has_lo, has_hi = me > 0, me < n - 1

    def peer(index):
        return {"slab": index}

    barrier = pltpu.get_barrier_semaphore()

    def greet(off, carry):
        pl.semaphore_signal(barrier, inc=1, device_id=peer(lax.rem(me + off, n)),
                            device_id_type=pl.DeviceIdType.MESH)
        return carry

    lax.fori_loop(1, n, greet, 0)

    @pl.when(jnp.logical_not(has_lo))
    def _():
        for i in range(4):
            halo0[i, 0] = jnp.zeros((nxy, nxy), F32)
        for i in range(6):
            halo1[i, 0] = jnp.zeros((half, half), F32)
        halo_reg[0] = jnp.zeros((nxy, nxy), jnp.int32)
        far_reg[0] = jnp.zeros((nxy, nxy), jnp.int32)

    @pl.when(jnp.logical_not(has_hi))
    def _():
        for i in range(4):
            halo0[i, 1] = jnp.zeros((nxy, nxy), F32)
        for i in range(6):
            halo1[i, 1] = jnp.zeros((half, half), F32)
        halo_reg[1] = jnp.zeros((nxy, nxy), jnp.int32)
        far_reg[1] = jnp.zeros((nxy, nxy), jnp.int32)

    density = partials[0].astype(F32)
    for g in range(1, partials.shape[0]):
        density = density + partials[g].astype(F32)
    dens[...] = (SOURCE * density).reshape(dens.shape)

    pl.semaphore_wait(barrier, n - 1)

    def copies(first, last, dst, sends, recvs, i):
        to_lo = pltpu.make_async_remote_copy(
            src_ref=first, dst_ref=dst.at[1], send_sem=sends.at[i, 0], recv_sem=recvs.at[i, 1],
            device_id=peer(jnp.maximum(me - 1, 0)), device_id_type=pl.DeviceIdType.MESH)
        to_hi = pltpu.make_async_remote_copy(
            src_ref=last, dst_ref=dst.at[0], send_sem=sends.at[i, 1], recv_sem=recvs.at[i, 0],
            device_id=peer(jnp.minimum(me + 1, n - 1)), device_id_type=pl.DeviceIdType.MESH)

        def start():
            pl.when(has_lo)(to_lo.start)
            pl.when(has_hi)(to_hi.start)

        def recv():
            pl.when(has_lo)(to_hi.wait_recv)
            pl.when(has_hi)(to_lo.wait_recv)

        def sent():
            pl.when(has_lo)(to_lo.wait_send)
            pl.when(has_hi)(to_hi.wait_send)

        return start, recv, sent

    pending = []

    def launch(first, last, dst, sends, recvs, i):
        start, recv, sent = copies(first, last, dst, sends, recvs, i)
        start()
        pending.append(sent)
        return recv

    recv_reg = launch(regions.at[0], regions.at[1], halo_reg, big_send, big_recv, REG)
    recv_v0 = launch(previous.at[0], previous.at[1], halo0.at[0], big_send, big_recv, V0)

    def scatter(step, carry):
        other = lax.rem(me + 1 + lax.rem(step + n // 2 - 1, n - 1), n)
        pltpu.make_async_remote_copy(
            src_ref=dens.at[other], dst_ref=got.at[me], send_sem=many_send.at[0],
            recv_sem=many_recv.at[0], device_id=peer(other),
            device_id_type=pl.DeviceIdType.MESH).start()
        return carry

    lax.fori_loop(0, n - 1, scatter, 0)

    def dielectric(r):
        return jnp.where(r == 0, INSIDE, SOLVENT).astype(F32)

    e = [dielectric(regions[p]) for p in range(2)]
    k = [jnp.where(regions[p] == 2, SCREEN, 0.0).astype(F32) for p in range(2)]
    right0, left0 = pool_right(nxy, half, nxy), pool_left(half, nxy)
    right1, left1 = pool_right(half, LANES, half), pool_left(quarter, half)

    def down0(a, b):
        return 0.125 * dot(left0, times(a + b, right0))

    def down1(a):
        return 0.25 * dot(left1, times(a, right1))

    e1, k1 = down0(e[0], e[1]), down0(k[0], k[1])
    plane1[E1] = e1
    recv_e1 = launch(plane1.at[E1], plane1.at[E1], halo1.at[E1], small_send, small_recv, E1)
    core, chip = lax.rem(me, 2), me // 2
    gk[core, chip] = down1(e1) + back(down1(k1), 1, LANES // 2)

    def share(ref, i):
        def one(off, carry):
            other = lax.rem(me + 2 * off, n)
            pltpu.make_async_remote_copy(
                src_ref=ref.at[core, chip], dst_ref=ref.at[core, chip], send_sem=many_send.at[i],
                recv_sem=many_recv.at[i], device_id=peer(other),
                device_id_type=pl.DeviceIdType.MESH).start()
            return carry

        lax.fori_loop(1, n // 2, one, 0)

    def relay(ref, i):
        window = ref.at[0, pl.ds(0, n // 2 - 1)]
        pltpu.make_async_copy(window, window, many_recv.at[i]).wait()
        copy = pltpu.make_async_remote_copy(
            src_ref=ref.at[core], dst_ref=ref.at[core], send_sem=many_send.at[i + 2],
            recv_sem=many_recv.at[i + 2], device_id=peer(me + 1 - 2 * core),
            device_id_type=pl.DeviceIdType.MESH)
        copy.start()
        pending.append(pltpu.make_async_copy(window, window, many_send.at[i]).wait)
        pending.append(copy.wait_send)
        return copy.wait_recv

    def all_in(ref, sems, i):
        window = ref.at[pl.ds(0, n - 1)]
        pltpu.make_async_copy(window, window, sems.at[i]).wait()

    share(gk, 1)

    totals = []
    middle = face(e[0], e[1], 1.0)
    fz0[1] = middle
    part = []
    for p in range(2):
        fx, fy, total = plane_faces(e[p], 1.0)
        fx0[p] = fx
        fy0[p] = fy
        totals.append(total + middle + k[p])
        part.append(plane_sum(fx, fy, previous[p]) + middle * previous[1 - p])
    recv_reg()
    e_side = [jnp.where(has_lo, dielectric(halo_reg[0]), e[0]),
              jnp.where(has_hi, dielectric(halo_reg[1]), e[1])]
    for p in range(2):
        outer = face(e_side[p], e[p], 1.0)
        fz0[2 * p] = outer
        total = totals[p] + outer
        dg0[p] = total
        wt0[p] = DAMPING / total

    def beside0(p, mine, below, above):
        return plane_sum(fx0[p], fy0[p], mine) + fz0[p] * below + fz0[p + 1] * above

    def sweep0(p, mine, below, above):
        return (1.0 - DAMPING) * mine + wt0[p] * (b0[p] + beside0(p, mine, below, above))

    recv_v0()
    for p in range(2):
        v1[p] = (1.0 - DAMPING) * previous[p] + wt0[p] * (part[p] + fz0[2 * p] * halo0[0, p])

    got[me] = dens[me]
    all_in(got, many_recv, 0)
    for p in range(2):
        if rows % 8 == 0:
            b0[p] = got[:, p].reshape(nxy, nxy)
        else:
            for s in range(n):
                b0[p, s * rows:(s + 1) * rows, :] = got[s, p]
    for p in range(2):
        v1[p] = v1[p] + wt0[p] * b0[p]
    recv = launch(v1.at[0], v1.at[1], halo0.at[1], big_send, big_recv, V1)
    recv_gk = relay(gk, 1)
    recv_e1()
    sz1 = sx1 = 4.0
    fx1, fy1, total1 = plane_faces(e1, sx1)
    fz1lo = face(jnp.where(has_lo, halo1[E1, 0], e1), e1, sz1)
    fz1hi = face(jnp.where(has_hi, halo1[E1, 1], e1), e1, sz1)
    dg1 = total1 + fz1lo + fz1hi + k1
    wt1 = DAMPING / dg1

    recv()
    v2[0] = sweep0(0, v1[0], halo0[1, 0], v1[1])
    v2[1] = sweep0(1, v1[1], v1[0], halo0[1, 1])
    term1[0] = 0.125 * dot(left0, times(fz0[0] * v2[0], right0))
    term1[1] = 0.125 * dot(left0, times(fz0[2] * v2[1], right0))
    recv_term = launch(term1.at[0], term1.at[1], halo1.at[TERM], small_send, small_recv, TERM)
    recv_v2 = launch(v2.at[0], v2.at[1], halo0.at[2], big_send, big_recv, V2)
    r0 = b0[0] - dg0[0] * v2[0] + plane_sum(fx0[0], fy0[0], v2[0]) + fz0[1] * v2[1]
    r1 = b0[1] - dg0[1] * v2[1] + plane_sum(fx0[1], fy0[1], v2[1]) + fz0[1] * v2[0]
    b1 = down0(r0, r1)
    recv_far = launch(regions.at[1], regions.at[0], far_reg, big_send, big_recv, FAR)
    recv_gk()
    e2 = 0.5 * (gk[0] + gk[1]).reshape(n // 2 * quarter, LANES)
    k2 = back(e2, 1, LANES // 2)
    coarse = coarse_cycle(e2, k2, n // 2, quarter, 16.0, 16.0, dot, times)
    recv_term()
    b1 = b1 + halo1[TERM, 0] + halo1[TERM, 1]

    def beside1(mine, i):
        return plane_sum(fx1, fy1, mine) + fz1lo * halo1[i, 0] + fz1hi * halo1[i, 1]

    def trade1(value, i):
        plane1[i] = value
        launch(plane1.at[i], plane1.at[i], halo1.at[i], small_send, small_recv, i)()

    a = wt1 * b1
    trade1(a, A1)
    a = (1.0 - DAMPING) * a + wt1 * (b1 + beside1(a, A1))
    trade1(a, A2)
    full = down1(b1 - dg1 * a + beside1(a, A2))
    gb[core, chip] = full[:quarter // 2] + back(full[quarter // 2:], 1, LANES // 2)
    share(gb, 2)
    recv_v2()
    base[0] = sweep0(0, v2[0], halo0[2, 0], v2[1])
    base[1] = sweep0(1, v2[1], v2[0], halo0[2, 1])
    recv_base = launch(base.at[0], base.at[1], halo0.at[3], big_send, big_recv, BASE)
    relay_gb = relay(gb, 2)
    recv_far()
    for p in range(2):
        region = halo_reg[p]
        beyond = face(e_side[p], dielectric(far_reg[p]), 1.0)
        fx, fy, total = plane_faces(e_side[p], 1.0)
        fxh[p] = fx
        fyh[p] = fy
        fzh[p] = beyond
        wth[p] = DAMPING / (total + beyond + fz0[2 * p] + jnp.where(region == 2, SCREEN, 0.0))
    relay_gb()
    packed = 0.5 * (gb[0] + gb[1]).reshape(n // 2 * quarter // 2, LANES)
    split = (n // 2, quarter // 2, LANES)
    b2 = jnp.concatenate(
        [packed.reshape(split), back(packed, 1, LANES // 2).reshape(split)], axis=1
    ).reshape(n // 2 * quarter, LANES)
    c2 = coarse(b2)

    for i in range(n // 2):
        c2_planes[i] = c2[i * quarter:(i + 1) * quarter]
    grow_l, grow_r = spread_left(half, quarter), spread_right(LANES, half, half)

    def up1(index):
        return dot(grow_l, times(c2_planes[index // 2], grow_r))

    halo1[A2, 0] = halo1[A2, 0] + jnp.where(has_lo, up1(jnp.maximum(me - 1, 0)), 0.0)
    halo1[A2, 1] = halo1[A2, 1] + jnp.where(has_hi, up1(jnp.minimum(me + 1, n - 1)), 0.0)
    a = a + up1(me)
    a = (1.0 - DAMPING) * a + wt1 * (b1 + beside1(a, A2))
    trade1(a, A3)
    a = (1.0 - DAMPING) * a + wt1 * (b1 + beside1(a, A3))
    trade1(a, A4)

    big_l, big_r = spread_left(nxy, half), spread_right(half, nxy, nxy)

    def up0(c):
        return dot(big_l, times(c, big_r))

    mine = up0(a)
    recv_base()
    v3, side = [], []
    present = [has_lo, has_hi]
    for p in range(2):
        c = up0(halo1[A4, p])
        own = plane_sum(fx0[p], fy0[p], mine) + fz0[1] * mine + fz0[2 * p] * c
        v3.append(base[p] + (1.0 - DAMPING) * mine + wt0[p] * own)
        other = plane_sum(fxh[p], fyh[p], c) + fzh[p] * c + fz0[2 * p] * mine
        swept = halo0[3, p] + (1.0 - DAMPING) * c + wth[p] * other
        side.append(jnp.where(present[p], swept, 0.0))
    out[0] = sweep0(0, v3[0], side[0], v3[1])
    out[1] = sweep0(1, v3[1], v3[0], side[1])

    for sent in pending:
        sent()
    all_in(got, many_send, 0)


HALO = 16
REG_LO, REG_HI, V0_LO, V0_HI, V1_LO, V1_HI, V2_LO, V2_HI, BASE_LO, BASE_HI = range(10)
E_M1, E_P1, E_M2, E_P2, K_M1, K_P1, B_M1, B_P1, B_M2, B_P2, A3_LO, A3_HI, NEAR, NEAR_CORE, FAR_LO, FAR_HI = range(10, 26)
MESSAGES = 26


def box_kernel(n, partials, regions, previous, out,
               parts, dens, reg, v0, b0, fx0, fy0, fz0, dg0, wt0, v1, v2, base, swept,
               near, fxn, fyn, fzn, wtn, landed, corr,
               e1, k1, fx1, fy1, fz1, dg1, wt1, pack, from_lo, from_hi, far_lo, far_hi,
               b1, a1, a2, a3, a4, gk, gb, c2_planes,
               load_sem, spread_send, spread_recv, corr_send, corr_recv, dens_send, dens_recv,
               side_send, side_recv, many_send, many_recv):
    me = lax.axis_index("slab")
    nz = n // 2
    z, x, core = me // 4, lax.rem(me // 2, 2), lax.rem(me, 2)
    zi = 2 * z + core
    nxy = regions.shape[1]
    half, quarter = nxy // 2, nxy // 4
    rows = partials.shape[2]
    window = half + HALO
    window1 = window // 2
    blocks = window // rows
    first = half - HALO

    def peer(index):
        return {"slab": index}

    def at(i, j):
        return (i // 2) * 4 + j * 2 + lax.rem(i, 2)

    load = pltpu.make_async_copy(partials, parts, load_sem.at[0])
    load.start()
    load_near = pltpu.make_async_copy(regions, near.at[pl.ds(2, 2)], load_sem.at[1])
    load_near.start()
    barrier = pltpu.get_barrier_semaphore()

    def greet(off, carry):
        pl.semaphore_signal(barrier, inc=1, device_id=peer(lax.rem(me + off, n)),
                            device_id_type=pl.DeviceIdType.MESH)
        return carry

    lax.fori_loop(1, n, greet, 0)

    plane0 = jnp.zeros((window, nxy), F32)
    plane1 = jnp.zeros((window1, half), F32)

    @pl.when(zi == 0)
    def _():
        for i in range(2):
            reg[i] = jnp.zeros((window, nxy), jnp.int32)
        for v in (v0, v1, v2, base):
            v[0] = plane0
        for i in range(3):
            from_lo[i] = plane1
        for i in range(2):
            e1[i] = plane1 + 1.0
            k1[i] = plane1
        a3[0] = plane1

    @pl.when(zi == nz - 1)
    def _():
        for i in range(2):
            reg[6 + i] = jnp.zeros((window, nxy), jnp.int32)
        for v in (v0, v1, v2, base):
            v[5] = plane0
        for i in range(3):
            from_hi[i] = plane1
        for i in range(2):
            e1[6 + i] = plane1 + 1.0
            k1[4 + i] = plane1
        a3[3] = plane1

    @pl.when(zi < 2)
    def _():
        far_lo[0] = plane1

    @pl.when(zi >= nz - 2)
    def _():
        far_hi[0] = plane1

    @pl.when(me == 0)
    def _():
        corr[0] = jnp.zeros((half, half), F32)

    @pl.when(me == n - 1)
    def _():
        corr[2] = jnp.zeros((half, half), F32)

    load.wait()
    density = parts[0].astype(F32)
    for g in range(1, partials.shape[0]):
        density = density + parts[g].astype(F32)
    dens[...] = (SOURCE * density).reshape(dens.shape)

    pl.semaphore_wait(barrier, n - 1)
    pending = []

    def spread(src, dst, low, i):
        for j in range(2):
            target = at(2 * z + x, j)
            piece = src.at[:, pl.ds(first * j, window), :]
            place = dst.at[pl.ds(low + 2 * core, 2)]
            remote = pltpu.make_async_remote_copy(
                src_ref=piece, dst_ref=place, send_sem=spread_send.at[i, j],
                recv_sem=spread_recv.at[i, core], device_id=peer(target),
                device_id_type=pl.DeviceIdType.MESH)
            here = pltpu.make_async_copy(piece, place, spread_recv.at[i, core])
            away = target != me
            pl.when(away)(remote.start)
            pl.when(jnp.logical_not(away))(here.start)
            pending.append(lambda remote=remote, away=away: pl.when(away)(remote.wait_send))

        def arrived():
            for j in range(2):
                place = dst.at[pl.ds(low + 2 * j, 2)]
                pltpu.make_async_copy(place, place, spread_recv.at[i, j]).wait()

        return arrived

    def send_density(step, carry):
        other = lax.rem(me + 1 + lax.rem(step + n // 2 - 1, n), n)
        oz, ox = 2 * (other // 4) + lax.rem(other, 2), lax.rem(other // 2, 2)
        block = me - (first // rows) * ox
        inside = (block >= 0) & (block < blocks)
        block = jnp.clip(block, 0, blocks - 1)
        place = b0.at[:, pl.ds(pl.multiple_of(block * rows, rows), rows), :]

        @pl.when(inside & (other != me))
        def _():
            pltpu.make_async_remote_copy(
                src_ref=dens.at[oz], dst_ref=place, send_sem=dens_send.at[other],
                recv_sem=dens_recv.at[0], device_id=peer(other),
                device_id_type=pl.DeviceIdType.MESH).start()

        @pl.when(inside & (other == me))
        def _():
            pltpu.make_async_copy(dens.at[oz], place, dens_recv.at[0]).start()

        return carry

    def sent_density(other, carry):
        ox = lax.rem(other // 2, 2)
        block = me - (first // rows) * ox

        @pl.when((block >= 0) & (block < blocks) & (other != me))
        def _():
            pltpu.make_async_copy(dens.at[0], dens.at[0], dens_send.at[other]).wait()

        return carry

    def push(src, dst, delta, i):
        can_send = (zi + delta >= 0) & (zi + delta < nz)
        can_recv = (zi - delta >= 0) & (zi - delta < nz)
        copy = pltpu.make_async_remote_copy(
            src_ref=src, dst_ref=dst, send_sem=side_send.at[i], recv_sem=side_recv.at[i],
            device_id=peer(at(jnp.clip(zi + delta, 0, nz - 1), x)),
            device_id_type=pl.DeviceIdType.MESH)
        pl.when(can_send)(copy.start)
        pending.append(lambda: pl.when(can_send)(copy.wait_send))
        return lambda: pl.when(can_recv)(copy.wait_recv)

    def trade(field, low, high, i):
        down = push(field.at[low], field.at[high + 1], -1, i)
        up = push(field.at[high], field.at[low - 1], 1, i + 1)

        def arrived():
            down()
            up()

        return arrived

    reg_in = spread(regions, reg, 2, 0)
    v0_in = spread(previous, v0, 1, 1)
    lax.fori_loop(0, n, send_density, 0)

    def dielectric(r):
        return jnp.where(r == 0, INSIDE, SOLVENT).astype(F32)

    right0, left0 = pool_right(nxy, half, nxy), pool_left(window1, window)
    right1 = pool_right(half, LANES, half)
    dst1, src1 = iota((quarter // 2, window1), 0), iota((quarter // 2, window1), 1)
    left1 = jnp.where((src1 - (HALO // 2) * x) // 2 == dst1, 1.0, 0.0).astype(F32)

    def down0(a):
        return 0.125 * dot2(left0, times2(a, right0))

    def down1(a):
        return 0.125 * dot2(left1, times2(a, right1))

    reg_in()
    reg_halo = trade(reg, 2, 5, REG_LO)
    e = [dielectric(reg[p]) for p in range(2, 6)]
    k = [jnp.where(reg[p] == 2, SCREEN, 0.0).astype(F32) for p in range(2, 6)]
    for i in range(2):
        e1[3 + i] = down0(e[2 * i] + e[2 * i + 1])
        k1[2 + i] = down0(k[2 * i] + k[2 * i + 1])
    e1_in = [push(e1.at[pl.ds(3, 2)], e1.at[pl.ds(1, 2)], 1, E_P1),
             push(e1.at[pl.ds(3, 2)], e1.at[pl.ds(5, 2)], -1, E_M1),
             push(e1.at[pl.ds(4, 1)], e1.at[pl.ds(0, 1)], 2, E_P2),
             push(e1.at[pl.ds(3, 1)], e1.at[pl.ds(7, 1)], -2, E_M2),
             push(k1.at[pl.ds(2, 2)], k1.at[pl.ds(0, 2)], 1, K_P1),
             push(k1.at[pl.ds(2, 2)], k1.at[pl.ds(4, 2)], -1, K_M1)]
    chip = me // 2
    gk[core, chip] = down1(e1[3] + e1[4]) + back(down1(k1[2] + k1[3]), 1, LANES // 2)

    def share(ref, i):
        def one(off, carry):
            other = lax.rem(me + 2 * off, n)
            pltpu.make_async_remote_copy(
                src_ref=ref.at[core, chip], dst_ref=ref.at[core, chip], send_sem=many_send.at[i],
                recv_sem=many_recv.at[i], device_id=peer(other),
                device_id_type=pl.DeviceIdType.MESH).start()
            return carry

        lax.fori_loop(1, n // 2, one, 0)

    def relay(ref, i):
        seven = ref.at[0, pl.ds(0, n // 2 - 1)]
        pltpu.make_async_copy(seven, seven, many_recv.at[i]).wait()
        copy = pltpu.make_async_remote_copy(
            src_ref=ref.at[core], dst_ref=ref.at[core], send_sem=many_send.at[i + 2],
            recv_sem=many_recv.at[i + 2], device_id=peer(me + 1 - 2 * core),
            device_id_type=pl.DeviceIdType.MESH)
        copy.start()
        pending.append(pltpu.make_async_copy(seven, seven, many_send.at[i]).wait)
        pending.append(copy.wait_send)
        return copy.wait_recv

    def in_order(ref):
        return [ref[c, 2 * i + j] for i in range(n // 4) for c in range(2) for j in range(2)]

    share(gk, 0)

    totals = []
    for p in range(4):
        fx, fy, total = plane_faces(e[p], 1.0)
        fx0[p] = fx
        fy0[p] = fy
        totals.append(total + k[p])
    for p in range(1, 4):
        fz0[p] = face(e[p - 1], e[p], 1.0)
    v0_in()
    v0_halo = trade(v0, 1, 4, V0_LO)
    far_in = [push(reg.at[3], reg.at[7], -1, FAR_LO), push(reg.at[4], reg.at[0], 1, FAR_HI)]

    def beside0(p, v):
        return (plane_sum(fx0[p], fy0[p], v[p + 1]) + fz0[p] * v[p] + fz0[p + 1] * v[p + 2])

    def sweep0(p, v):
        return (1.0 - DAMPING) * v[p + 1] + wt0[p] * (b0[p] + beside0(p, v))

    def first_part(p):
        v1[p + 1] = (1.0 - DAMPING) * v0[p + 1] + wt0[p] * beside0(p, v0)

    def weights(p):
        diag = totals[p] + fz0[p] + fz0[p + 1]
        dg0[p] = diag
        wt0[p] = DAMPING / diag

    for p in (1, 2):
        weights(p)
        first_part(p)
    reg_halo()
    fz0[0] = face(jnp.where(zi > 0, dielectric(reg[1]), e[0]), e[0], 1.0)
    fz0[4] = face(e[3], jnp.where(zi < nz - 1, dielectric(reg[6]), e[3]), 1.0)
    weights(0)
    weights(3)
    v0_halo()
    first_part(0)
    first_part(3)

    pltpu.make_async_copy(b0, b0, dens_recv.at[0]).wait()
    for p in (0, 3):
        v1[p + 1] = v1[p + 1] + wt0[p] * b0[p]
    v1_halo = trade(v1, 1, 4, V1_LO)
    for p in (1, 2):
        v1[p + 1] = v1[p + 1] + wt0[p] * b0[p]

    for arrived in far_in:
        arrived()
    own_rows = pl.ds(pl.multiple_of(HALO * x, HALO), half)

    def near_rows(j):
        return near.at[pl.ds(4 * core, 2), pl.ds(pl.multiple_of(half * j, half), half), :]

    across = pltpu.make_async_remote_copy(
        src_ref=reg.at[pl.ds(4 + 2 * core - 4 * x, 2), own_rows, :], dst_ref=near_rows(x),
        send_sem=side_send.at[NEAR], recv_sem=side_recv.at[NEAR], device_id=peer(at(zi, 1 - x)),
        device_id_type=pl.DeviceIdType.MESH)
    beside = pltpu.make_async_remote_copy(
        src_ref=regions, dst_ref=near.at[pl.ds(4 * core, 2)], send_sem=side_send.at[NEAR_CORE],
        recv_sem=side_recv.at[NEAR_CORE], device_id=peer(at(zi + 1 - 2 * core, x)),
        device_id_type=pl.DeviceIdType.MESH)
    within = pltpu.make_async_copy(reg.at[pl.ds(2 * core + 4 * x, 2), own_rows, :], near_rows(x),
                                   load_sem.at[2])
    for copy in (across, beside, within):
        copy.start()
    pending.append(across.wait_send)
    pending.append(beside.wait_send)
    gk_in = relay(gk, 0)
    for arrived in e1_in:
        arrived()

    @pl.when(zi == 0)
    def _():
        e1[2] = e1[3]
        e1[0] = plane1 + 1.0

    @pl.when(zi == 1)
    def _():
        e1[0] = e1[1]

    @pl.when(zi == nz - 1)
    def _():
        e1[5] = e1[4]
        e1[7] = plane1 + 1.0

    @pl.when(zi == nz - 2)
    def _():
        e1[7] = e1[6]

    s1 = 4.0
    for i in range(7):
        fz1[i] = face(e1[i], e1[i + 1], s1)
    for i in range(6):
        fx, fy, total = plane_faces(e1[i + 1], s1)
        fx1[i] = fx
        fy1[i] = fy
        diag = total + fz1[i] + fz1[i + 1] + k1[i]
        dg1[i] = diag
        weight = DAMPING / diag
        if i < 2:
            weight = jnp.where(zi > 0, weight, 0.0)
        if i > 3:
            weight = jnp.where(zi < nz - 1, weight, 0.0)
        wt1[i] = weight

    for p in (1, 2):
        v2[p + 1] = sweep0(p, v1)
    v1_halo()
    for p in (0, 3):
        v2[p + 1] = sweep0(p, v1)
    v2_halo = trade(v2, 1, 4, V2_LO)
    pack[0] = down0(fz0[4] * v2[4])
    pack[3] = down0(fz0[0] * v2[1])

    def left_over(p):
        r = b0[p] - dg0[p] * v2[p + 1] + plane_sum(fx0[p], fy0[p], v2[p + 1])
        if p > 0:
            r = r + fz0[p] * v2[p]
        if p < 3:
            r = r + fz0[p + 1] * v2[p + 2]
        return r

    for i in range(2):
        pack[1 + i] = down0(left_over(2 * i) + left_over(2 * i + 1))
    b1_in = [push(pack.at[pl.ds(0, 3)], from_lo, 1, B_P1),
             push(pack.at[pl.ds(1, 3)], from_hi, -1, B_M1),
             push(pack.at[pl.ds(0, 1)], far_lo, 2, B_P2),
             push(pack.at[pl.ds(3, 1)], far_hi, -2, B_M2)]
    gk_in()
    e2 = jnp.concatenate(in_order(gk), axis=0)
    coarse = coarse_cycle(e2, back(e2, 1, LANES // 2), nz, quarter, 16.0, 16.0,
                          dot2, times2)
    v2_halo()
    for p in (0, 3, 1, 2):
        base[p + 1] = sweep0(p, v2)
    base_halo = trade(base, 1, 4, BASE_LO)
    for arrived in b1_in:
        arrived()
    b1[0] = from_lo[1] + far_lo[0]
    b1[1] = from_lo[2] + pack[3]
    b1[2] = pack[1] + from_lo[0]
    b1[3] = pack[2] + from_hi[2]
    b1[4] = from_hi[0] + pack[0]
    b1[5] = from_hi[1] + far_hi[0]

    def beside1(i, mine, below, above):
        return plane_sum(fx1[i], fy1[i], mine) + fz1[i] * below + fz1[i + 1] * above

    def sweep1(i, mine, below, above):
        return (1.0 - DAMPING) * mine + wt1[i] * (b1[i] + beside1(i, mine, below, above))

    for i in range(6):
        a1[i] = wt1[i] * b1[i]
    for i in range(1, 5):
        a2[i - 1] = sweep1(i, a1[i], a1[i - 1], a1[i + 1])
    rest = [b1[i] - dg1[i] * a2[i - 1] + beside1(i, a2[i - 1], a2[i - 2], a2[i]) for i in (2, 3)]
    full = down1(rest[0] + rest[1])
    gb[core, chip] = full[:quarter // 4] + back(full[quarter // 4:], 1, LANES // 2)
    share(gb, 1)
    gb_in = relay(gb, 1)
    base_halo()

    def deliver(j):
        target = 4 * z + 2 * core + j
        piece = swept.at[pl.ds(2 * j, 2), pl.ds(pl.multiple_of(HALO * x, HALO), half), :]
        place = landed.at[:, pl.ds(pl.multiple_of(half * x, half), half), :]
        remote = pltpu.make_async_remote_copy(
            src_ref=piece, dst_ref=place, send_sem=spread_send.at[2, j],
            recv_sem=spread_recv.at[2, x], device_id=peer(target),
            device_id_type=pl.DeviceIdType.MESH)
        here = pltpu.make_async_copy(piece, place, spread_recv.at[2, x])
        away = target != me
        pl.when(away)(remote.start)
        pl.when(jnp.logical_not(away))(here.start)
        pending.append(lambda: pl.when(away)(remote.wait_send))

    for p in range(4):
        swept[p] = sweep0(p, base)
        if p % 2:
            deliver(p // 2)
    gb_in()
    packed = jnp.stack(in_order(gb))
    b2 = jnp.concatenate([packed, back(packed.reshape(-1, LANES), 1, LANES // 2).reshape(packed.shape)],
                         axis=1).reshape(nz * quarter, LANES)
    c2 = coarse(b2)
    for i in range(nz):
        c2_planes[i] = c2[i * quarter:(i + 1) * quarter]
    fine, mid = iota((window1, quarter), 0), iota((window1, quarter), 1)
    grow_l = jnp.where((fine + first // 2 * x) // 2 == mid, 1.0, 0.0).astype(F32)
    grow_r = spread_right(LANES, half, half)

    def up1(index):
        return dot2(grow_l, times2(c2_planes[index], grow_r))

    mine = up1(zi)
    a2[0] = a2[0] + jnp.where(zi > 0, up1(jnp.maximum(zi - 1, 0)), 0.0)
    a2[3] = a2[3] + jnp.where(zi < nz - 1, up1(jnp.minimum(zi + 1, nz - 1)), 0.0)
    a2[1] = a2[1] + mine
    a2[2] = a2[2] + mine
    for i in (1, 2):
        a3[i] = sweep1(i + 1, a2[i], a2[i - 1], a2[i + 1])
    trade(a3, 1, 2, A3_LO)()
    for i in (1, 2):
        a4[i] = sweep1(i + 1, a3[i], a3[i - 1], a3[i + 1])

    def hand(count, low, delta, slot, i):
        target = 2 * zi + delta
        exists = (target >= 0) & (target < n)
        piece = a4.at[pl.ds(low, count), pl.ds(pl.multiple_of(HALO // 2 * x, HALO // 2), quarter), :]
        place = corr.at[pl.ds(slot, count), pl.ds(pl.multiple_of(quarter * x, quarter), quarter), :]
        kind = 2 - count
        remote = pltpu.make_async_remote_copy(
            src_ref=piece, dst_ref=place, send_sem=corr_send.at[i], recv_sem=corr_recv.at[kind, x],
            device_id=peer(jnp.clip(target, 0, n - 1)), device_id_type=pl.DeviceIdType.MESH)
        here = pltpu.make_async_copy(piece, place, corr_recv.at[kind, x])
        away = exists & (target != me)
        pl.when(away)(remote.start)
        pl.when(target == me)(here.start)
        pending.append(lambda: pl.when(away)(remote.wait_send))

    hand(2, 1, 0, 1, 0)
    hand(2, 1, 1, 0, 1)
    hand(1, 1, -1, 2, 2)
    hand(1, 2, 2, 0, 3)
    big_l, big_r = spread_left(nxy, half), spread_right(half, nxy, nxy)

    def up0(c):
        return dot2(big_l, times2(c, big_r))

    load_near.wait()
    within.wait()
    across.wait_recv()
    beside.wait_recv()
    en = [dielectric(near[f]) for f in range(6)]
    fzn[0] = face(en[0], en[1], 1.0)
    fzn[1] = face(jnp.where(me > 0, en[1], en[2]), en[2], 1.0)
    fzn[2] = face(en[2], en[3], 1.0)
    fzn[3] = face(en[3], jnp.where(me < n - 1, en[4], en[3]), 1.0)
    fzn[4] = face(en[4], en[5], 1.0)
    for f in range(4):
        fx, fy, total = plane_faces(en[f + 1], 1.0)
        fxn[f] = fx
        fyn[f] = fy
        kn = jnp.where(near[f + 1] == 2, SCREEN, 0.0).astype(F32)
        wtn[f] = DAMPING / (total + kn + fzn[f] + fzn[f + 1])
    for sent in pending:
        sent()
    lax.fori_loop(0, n, sent_density, 0)
    single = jnp.where(lax.rem(me, 2) == 0, me > 0, me < n - 1)
    for j in range(2):
        both = corr.at[pl.ds(0, 2), pl.ds(quarter * j, quarter), :]
        pltpu.make_async_copy(both, both, corr_recv.at[0, j]).wait()
        one = corr.at[pl.ds(0, 1), pl.ds(quarter * j, quarter), :]
        pl.when(single)(pltpu.make_async_copy(one, one, corr_recv.at[1, j]).wait)
    for j in range(2):
        place = landed.at[:, pl.ds(half * j, half), :]
        pltpu.make_async_copy(place, place, spread_recv.at[2, j]).wait()
    below, here, above = (up0(corr[i]) for i in range(3))
    spans = [(below, below, here), (here, below, here), (here, here, above), (above, here, above)]

    def relax(f, mine, low, high):
        return (1.0 - DAMPING) * mine + wtn[f] * (
            plane_sum(fxn[f], fyn[f], mine) + fzn[f] * low + fzn[f + 1] * high)

    y = [relax(f, *spans[f]) for f in range(4)]
    y[0] = jnp.where(me > 0, y[0], 0.0)
    y[3] = jnp.where(me < n - 1, y[3], 0.0)
    for f in (1, 2):
        out[f - 1] = landed[f - 1] + relax(f, y[f], y[f - 1], y[f + 1])


def box_local(partials, regions, previous):
    n = lax.axis_size("slab")
    nxy = regions.shape[1]
    half, quarter = nxy // 2, nxy // 4
    rows = partials.shape[2]
    window, window1 = half + HALO, (half + HALO) // 2
    vmem = lambda *shape: pltpu.VMEM(shape, F32)
    big = lambda count: vmem(count, window, nxy)
    small = lambda count: vmem(count, window1, half)
    return pl.pallas_call(
        functools.partial(box_kernel, n),
        out_shape=pltpu.VMEM(previous.shape, F32),
        in_specs=[pl.BlockSpec(memory_space=pltpu.HBM)] * 3,
        out_specs=pl.BlockSpec(memory_space=pltpu.VMEM),
        scratch_shapes=[
            pltpu.VMEM(partials.shape, partials.dtype), vmem(n // 2, 4, rows, nxy),
            pltpu.VMEM((8, window, nxy), jnp.int32), big(6), big(4),
            big(4), big(4), big(5), big(4), big(4), big(6), big(6), big(6), big(4),
            pltpu.VMEM((6, nxy, nxy), jnp.int32), vmem(4, nxy, nxy), vmem(4, nxy, nxy),
            vmem(5, nxy, nxy), vmem(4, nxy, nxy), vmem(2, nxy, nxy), vmem(3, half, half),
            small(8), small(6), small(6), small(6), small(7), small(6), small(6),
            small(4), small(3), small(3), small(1), small(1),
            small(6), small(6), small(4), small(4), small(4),
            vmem(2, n // 2, quarter // 2, LANES), vmem(2, n // 2, quarter // 4, LANES),
            vmem(n // 2, quarter, LANES),
            pltpu.SemaphoreType.DMA((3,)),
            pltpu.SemaphoreType.DMA((3, 2)), pltpu.SemaphoreType.DMA((3, 2)),
            pltpu.SemaphoreType.DMA((4,)), pltpu.SemaphoreType.DMA((2, 2)),
            pltpu.SemaphoreType.DMA((n,)), pltpu.SemaphoreType.DMA((1,)),
            pltpu.SemaphoreType.DMA((MESSAGES,)), pltpu.SemaphoreType.DMA((MESSAGES,)),
            pltpu.SemaphoreType.DMA((4,)), pltpu.SemaphoreType.DMA((4,)),
        ],
        compiler_params=pltpu.CompilerParams(
            collective_id=1, has_side_effects=True, vmem_limit_bytes=60 * 1024 * 1024),
    )(partials, regions, previous)


def local(partials, regions, previous):
    n = lax.axis_size("slab")
    nxy = regions.shape[1]
    half, quarter = nxy // 2, nxy // 4
    rows = partials.shape[2]
    vmem = lambda *shape: pltpu.VMEM(shape, F32)
    spec = pl.BlockSpec(memory_space=pltpu.VMEM)
    return pl.pallas_call(
        functools.partial(kernel, n),
        out_shape=jax.ShapeDtypeStruct(previous.shape, F32),
        in_specs=[spec] * 3,
        out_specs=spec,
        scratch_shapes=[
            vmem(n, 2, rows, nxy), vmem(n, 2, rows, nxy), vmem(2, nxy, nxy),
            vmem(2, nxy, nxy), vmem(2, nxy, nxy), vmem(3, nxy, nxy), vmem(2, nxy, nxy),
            vmem(2, nxy, nxy),
            pltpu.VMEM((2, nxy, nxy), jnp.int32), pltpu.VMEM((2, nxy, nxy), jnp.int32),
            vmem(2, nxy, nxy), vmem(2, nxy, nxy), vmem(2, nxy, nxy), vmem(2, nxy, nxy),
            vmem(4, 2, nxy, nxy),
            vmem(2, nxy, nxy), vmem(2, nxy, nxy), vmem(2, nxy, nxy),
            vmem(6, 2, half, half), vmem(5, half, half), vmem(2, half, half),
            vmem(2, n // 2, quarter // 2, LANES), vmem(2, n // 2, quarter, LANES),
            pltpu.SemaphoreType.DMA((6, 2)), pltpu.SemaphoreType.DMA((6, 2)),
            pltpu.SemaphoreType.DMA((6, 2)), pltpu.SemaphoreType.DMA((6, 2)),
            pltpu.SemaphoreType.DMA((5,)), pltpu.SemaphoreType.DMA((5,)),
            vmem(n // 2, quarter, LANES),
        ],
        compiler_params=pltpu.CompilerParams(
            collective_id=0, has_side_effects=True, vmem_limit_bytes=60 * 1024 * 1024),
    )(partials, regions, previous)


def solution(mesh):
    in_specs = (
        P("job", None, "slab", None),
        P(("job", "slab"), None, None),
        P(("job", "slab"), None, None),
    )
    out_specs = P(("job", "slab"), None, None)
    size = mesh.shape["slab"]

    def fits(partials, regions):
        return (size == 16 and partials.shape[2] == 16 * size and partials.shape[1] == 2 * size
                and regions.shape[1] == 16 * size)

    def program(partials, regions, previous):
        chosen = box_local if fits(partials, regions) else local
        return jax.shard_map(chosen, mesh=mesh, in_specs=in_specs, out_specs=out_specs, check_vma=False)(
            partials, regions, previous)

    return program
```

```python
import functools

import jax
import jax.numpy as jnp
from jax import lax
from jax.experimental import pallas as pl
from jax.experimental.pallas import tpu as pltpu
from jax.sharding import PartitionSpec as P

PRE_SWEEPS = 2
POST_SWEEPS = 2
COARSE_SWEEPS = 4

DAMPING = 0.75
INSIDE = 2.0
SOLVENT = 78.4
SCREEN = 1.4
SOURCE = 16.0 * 3.141592653589793

F32 = jnp.float32
LANES = 128


def iota(shape, dim):
    return lax.broadcasted_iota(jnp.int32, shape, dim)


def face(mine, other, spacing):
    return mine * other / ((mine + other) * (0.5 * spacing))


def back(v, dim, by=1):
    return pltpu.roll(v, by, dim)


def ahead(v, dim, by=1):
    return pltpu.roll(v, v.shape[dim] - by, dim)


def terms(v):
    result = []
    for _ in range(3):
        result.append(v.astype(jnp.bfloat16))
        v = v - result[-1].astype(F32)
    return result


def product(a, b):
    return lax.dot_general(a, b, (((1,), (0,)), ((), ())), preferred_element_type=F32)


def times(v, selector):
    high, middle, low = (product(t, selector.astype(jnp.bfloat16)) for t in terms(v))
    return high + (middle + low)


def dot(selector, v):
    high, middle, low = (product(selector.astype(jnp.bfloat16), t) for t in terms(v))
    return high + (middle + low)


def halves(v):
    high = v.astype(jnp.bfloat16)
    return high, (v - high.astype(F32)).astype(jnp.bfloat16)


def times2(v, selector):
    high, low = (product(t, selector.astype(jnp.bfloat16)) for t in halves(v))
    return high + low


def dot2(selector, v):
    high, low = (product(selector.astype(jnp.bfloat16), t) for t in halves(v))
    return high + low


def pool_right(wide, narrow, valid):
    src, dst = iota((wide, narrow), 0), iota((wide, narrow), 1)
    return jnp.where((src // 2 == dst) & (src < valid), 1.0, 0.0).astype(F32)


def pool_left(narrow, wide):
    dst, src = iota((narrow, wide), 0), iota((narrow, wide), 1)
    return jnp.where(src // 2 == dst, 1.0, 0.0).astype(F32)


def spread_right(narrow, wide, valid):
    src, dst = iota((narrow, wide), 0), iota((narrow, wide), 1)
    return jnp.where((dst // 2 == src) & (dst < valid), 1.0, 0.0).astype(F32)


def spread_left(wide, narrow):
    dst, src = iota((wide, narrow), 0), iota((wide, narrow), 1)
    return jnp.where(dst // 2 == src, 1.0, 0.0).astype(F32)


def plane_faces(e, spacing):
    rows, cols = e.shape
    x, y = iota(e.shape, 0), iota(e.shape, 1)
    fx = jnp.where(x > 0, face(e, back(e, 0), spacing), 0.0)
    fy = jnp.where(y > 0, face(e, back(e, 1), spacing), 0.0)
    edges = (jnp.where((x == 0) | (x == rows - 1), 1.0, 0.0)
             + jnp.where((y == 0) | (y == cols - 1), 1.0, 0.0))
    total = fx + ahead(fx, 0) + fy + ahead(fy, 1) + edges * e * (1.0 / spacing)
    return fx, fy, total


def plane_sum(fx, fy, v):
    return fx * back(v, 0) + ahead(fx * v, 0) + fy * back(v, 1) + ahead(fy * v, 1)


def coarse_cycle(e, k, planes, nx, sz, sx, dot, times):
    rows = e.shape[0]
    row, lane = iota(e.shape, 0), iota(e.shape, 1)
    x, z = row % nx, row // nx
    valid = (row < planes * nx) & (lane < nx)
    e = jnp.where(valid, e, 1.0)
    fx = jnp.where(valid & (x > 0), face(e, back(e, 0), sx), 0.0) if nx > 1 else None
    fy = jnp.where(valid & (lane > 0), face(e, back(e, 1), sx), 0.0) if nx > 1 else None
    wrap = nx % rows
    fz = jnp.where(valid & (z > 0), face(e, back(e, 0, wrap), sz), 0.0) if planes > 1 else None
    diag = k + e * (
        (jnp.where(x == 0, 1.0, 0.0) + jnp.where(x == nx - 1, 1.0, 0.0)
         + jnp.where(lane == 0, 1.0, 0.0) + jnp.where(lane == nx - 1, 1.0, 0.0)) * (1.0 / sx)
        + (jnp.where(z == 0, 1.0, 0.0) + jnp.where(z == planes - 1, 1.0, 0.0)) * (1.0 / sz))
    if nx > 1:
        diag = diag + fx + ahead(fx, 0) + fy + ahead(fy, 1)
    if planes > 1:
        diag = diag + fz + ahead(fz, 0, wrap)
    w = jnp.where(valid, DAMPING / jnp.where(valid, diag, 1.0), 0.0)

    def beside(v):
        total = jnp.zeros_like(v)
        if nx > 1:
            total = plane_sum(fx, fy, v)
        if planes > 1:
            total = total + fz * back(v, 0, wrap) + ahead(fz * v, 0, wrap)
        return total

    def sweep(v, b):
        return (1.0 - DAMPING) * v + w * (b + beside(v))

    def coarsest(b):
        v = w * b
        for _ in range(COARSE_SWEEPS - 1):
            v = sweep(v, b)
        return v

    if planes == 1:
        return coarsest
    halve = nx > 1 and nx % 2 == 0
    nx2 = nx // 2 if halve else nx
    sx2 = sx * 4.0 if halve else sx
    step = planes
    while step * nx > 512 and step % 4 == 0:
        step //= 2
    part = step * nx
    if step == planes:
        part = rows
    real2 = planes // 2 * nx2
    rows2 = max(8, real2)
    part2 = rows2 if step == planes else step // 2 * nx2
    ratio = 2 if halve else 1

    def member(fine, coarse):
        return ((fine < step * nx) & ((fine // nx // 2) * nx2 + fine % nx // ratio == coarse))

    down = jnp.where(member(iota((part2, part), 1), iota((part2, part), 0)), 1.0, 0.0)
    up = jnp.where(member(iota((part, part2), 0), iota((part, part2), 1)), 1.0, 0.0)
    if halve:
        right = pool_right(LANES, LANES, nx)
        left = spread_right(LANES, LANES, nx)
        scale = 0.125
    else:
        scale = 0.5

    def coarsen(f):
        if halve:
            f = times(f, right)
        parts = [dot(down, f[i:i + part]) for i in range(0, rows, part)]
        return scale * (parts[0] if len(parts) == 1 else jnp.concatenate(parts, axis=0))

    def refine(f):
        if halve:
            f = times(f, left)
        parts = [dot(up, f[i:i + part2]) for i in range(0, rows2, part2)]
        return parts[0] if len(parts) == 1 else jnp.concatenate(parts, axis=0)

    below = coarse_cycle(coarsen(jnp.where(valid, e, 0.0)), coarsen(k),
                         planes // 2, nx2, sz * 4.0, sx2, dot, times)

    def run(b):
        v = w * b
        for _ in range(PRE_SWEEPS - 1):
            v = sweep(v, b)
        r = jnp.where(valid, b - diag * v + beside(v), 0.0)
        v = v + refine(below(coarsen(r)))
        for _ in range(POST_SWEEPS):
            v = sweep(v, b)
        return v

    return run


REG, V0, V1, V2, BASE, FAR = range(6)
E1, A1, A2, A3, A4, TERM = range(6)


def kernel(n, partials, regions, previous, out,
           dens, got, b0, fx0, fy0, fz0, dg0, wt0, halo_reg, far_reg, fxh, fyh, fzh, wth, halo0, v1, v2, base,
           halo1, plane1, term1, gb, gk,
           big_send, big_recv, small_send, small_recv, many_send, many_recv, c2_planes):
    me = lax.axis_index("slab")
    job = lax.axis_index("job")
    nxy = regions.shape[1]
    half = nxy // 2
    quarter = nxy // 4
    rows = partials.shape[2]
    has_lo, has_hi = me > 0, me < n - 1

    def peer(index):
        return {"slab": index}

    barrier = pltpu.get_barrier_semaphore()

    def greet(off, carry):
        pl.semaphore_signal(barrier, inc=1, device_id=peer(lax.rem(me + off, n)),
                            device_id_type=pl.DeviceIdType.MESH)
        return carry

    lax.fori_loop(1, n, greet, 0)

    @pl.when(jnp.logical_not(has_lo))
    def _():
        for i in range(4):
            halo0[i, 0] = jnp.zeros((nxy, nxy), F32)
        for i in range(6):
            halo1[i, 0] = jnp.zeros((half, half), F32)
        halo_reg[0] = jnp.zeros((nxy, nxy), jnp.int32)
        far_reg[0] = jnp.zeros((nxy, nxy), jnp.int32)

    @pl.when(jnp.logical_not(has_hi))
    def _():
        for i in range(4):
            halo0[i, 1] = jnp.zeros((nxy, nxy), F32)
        for i in range(6):
            halo1[i, 1] = jnp.zeros((half, half), F32)
        halo_reg[1] = jnp.zeros((nxy, nxy), jnp.int32)
        far_reg[1] = jnp.zeros((nxy, nxy), jnp.int32)

    density = partials[0].astype(F32)
    for g in range(1, partials.shape[0]):
        density = density + partials[g].astype(F32)
    dens[...] = (SOURCE * density).reshape(dens.shape)

    pl.semaphore_wait(barrier, n - 1)

    def copies(first, last, dst, sends, recvs, i):
        to_lo = pltpu.make_async_remote_copy(
            src_ref=first, dst_ref=dst.at[1], send_sem=sends.at[i, 0], recv_sem=recvs.at[i, 1],
            device_id=peer(jnp.maximum(me - 1, 0)), device_id_type=pl.DeviceIdType.MESH)
        to_hi = pltpu.make_async_remote_copy(
            src_ref=last, dst_ref=dst.at[0], send_sem=sends.at[i, 1], recv_sem=recvs.at[i, 0],
            device_id=peer(jnp.minimum(me + 1, n - 1)), device_id_type=pl.DeviceIdType.MESH)

        def start():
            pl.when(has_lo)(to_lo.start)
            pl.when(has_hi)(to_hi.start)

        def recv():
            pl.when(has_lo)(to_hi.wait_recv)
            pl.when(has_hi)(to_lo.wait_recv)

        def sent():
            pl.when(has_lo)(to_lo.wait_send)
            pl.when(has_hi)(to_hi.wait_send)

        return start, recv, sent

    pending = []

    def launch(first, last, dst, sends, recvs, i):
        start, recv, sent = copies(first, last, dst, sends, recvs, i)
        start()
        pending.append(sent)
        return recv

    recv_reg = launch(regions.at[0], regions.at[1], halo_reg, big_send, big_recv, REG)
    recv_v0 = launch(previous.at[0], previous.at[1], halo0.at[0], big_send, big_recv, V0)

    def scatter(step, carry):
        other = lax.rem(me + 1 + lax.rem(step + n // 2 - 1, n - 1), n)
        pltpu.make_async_remote_copy(
            src_ref=dens.at[other], dst_ref=got.at[me], send_sem=many_send.at[0],
            recv_sem=many_recv.at[0], device_id=peer(other),
            device_id_type=pl.DeviceIdType.MESH).start()
        return carry

    lax.fori_loop(0, n - 1, scatter, 0)

    def dielectric(r):
        return jnp.where(r == 0, INSIDE, SOLVENT).astype(F32)

    e = [dielectric(regions[p]) for p in range(2)]
    k = [jnp.where(regions[p] == 2, SCREEN, 0.0).astype(F32) for p in range(2)]
    right0, left0 = pool_right(nxy, half, nxy), pool_left(half, nxy)
    right1, left1 = pool_right(half, LANES, half), pool_left(quarter, half)

    def down0(a, b):
        return 0.125 * dot(left0, times(a + b, right0))

    def down1(a):
        return 0.25 * dot(left1, times(a, right1))

    e1, k1 = down0(e[0], e[1]), down0(k[0], k[1])
    plane1[E1] = e1
    recv_e1 = launch(plane1.at[E1], plane1.at[E1], halo1.at[E1], small_send, small_recv, E1)
    core, chip = lax.rem(me, 2), me // 2
    gk[core, chip] = down1(e1) + back(down1(k1), 1, LANES // 2)

    def share(ref, i):
        def one(off, carry):
            other = lax.rem(me + 2 * off, n)
            pltpu.make_async_remote_copy(
                src_ref=ref.at[core, chip], dst_ref=ref.at[core, chip], send_sem=many_send.at[i],
                recv_sem=many_recv.at[i], device_id=peer(other),
                device_id_type=pl.DeviceIdType.MESH).start()
            return carry

        lax.fori_loop(1, n // 2, one, 0)

    def relay(ref, i):
        window = ref.at[0, pl.ds(0, n // 2 - 1)]
        pltpu.make_async_copy(window, window, many_recv.at[i]).wait()
        copy = pltpu.make_async_remote_copy(
            src_ref=ref.at[core], dst_ref=ref.at[core], send_sem=many_send.at[i + 2],
            recv_sem=many_recv.at[i + 2], device_id=peer(me + 1 - 2 * core),
            device_id_type=pl.DeviceIdType.MESH)
        copy.start()
        pending.append(pltpu.make_async_copy(window, window, many_send.at[i]).wait)
        pending.append(copy.wait_send)
        return copy.wait_recv

    def all_in(ref, sems, i):
        window = ref.at[pl.ds(0, n - 1)]
        pltpu.make_async_copy(window, window, sems.at[i]).wait()

    share(gk, 1)

    totals = []
    middle = face(e[0], e[1], 1.0)
    fz0[1] = middle
    part = []
    for p in range(2):
        fx, fy, total = plane_faces(e[p], 1.0)
        fx0[p] = fx
        fy0[p] = fy
        totals.append(total + middle + k[p])
        part.append(plane_sum(fx, fy, previous[p]) + middle * previous[1 - p])
    recv_reg()
    e_side = [jnp.where(has_lo, dielectric(halo_reg[0]), e[0]),
              jnp.where(has_hi, dielectric(halo_reg[1]), e[1])]
    for p in range(2):
        outer = face(e_side[p], e[p], 1.0)
        fz0[2 * p] = outer
        total = totals[p] + outer
        dg0[p] = total
        wt0[p] = DAMPING / total

    def beside0(p, mine, below, above):
        return plane_sum(fx0[p], fy0[p], mine) + fz0[p] * below + fz0[p + 1] * above

    def sweep0(p, mine, below, above):
        return (1.0 - DAMPING) * mine + wt0[p] * (b0[p] + beside0(p, mine, below, above))

    recv_v0()
    for p in range(2):
        v1[p] = (1.0 - DAMPING) * previous[p] + wt0[p] * (part[p] + fz0[2 * p] * halo0[0, p])

    got[me] = dens[me]
    all_in(got, many_recv, 0)
    for p in range(2):
        if rows % 8 == 0:
            b0[p] = got[:, p].reshape(nxy, nxy)
        else:
            for s in range(n):
                b0[p, s * rows:(s + 1) * rows, :] = got[s, p]
    for p in range(2):
        v1[p] = v1[p] + wt0[p] * b0[p]
    recv = launch(v1.at[0], v1.at[1], halo0.at[1], big_send, big_recv, V1)
    recv_gk = relay(gk, 1)
    recv_e1()
    sz1 = sx1 = 4.0
    fx1, fy1, total1 = plane_faces(e1, sx1)
    fz1lo = face(jnp.where(has_lo, halo1[E1, 0], e1), e1, sz1)
    fz1hi = face(jnp.where(has_hi, halo1[E1, 1], e1), e1, sz1)
    dg1 = total1 + fz1lo + fz1hi + k1
    wt1 = DAMPING / dg1

    recv()
    v2[0] = sweep0(0, v1[0], halo0[1, 0], v1[1])
    v2[1] = sweep0(1, v1[1], v1[0], halo0[1, 1])
    term1[0] = 0.125 * dot(left0, times(fz0[0] * v2[0], right0))
    term1[1] = 0.125 * dot(left0, times(fz0[2] * v2[1], right0))
    recv_term = launch(term1.at[0], term1.at[1], halo1.at[TERM], small_send, small_recv, TERM)
    recv_v2 = launch(v2.at[0], v2.at[1], halo0.at[2], big_send, big_recv, V2)
    r0 = b0[0] - dg0[0] * v2[0] + plane_sum(fx0[0], fy0[0], v2[0]) + fz0[1] * v2[1]
    r1 = b0[1] - dg0[1] * v2[1] + plane_sum(fx0[1], fy0[1], v2[1]) + fz0[1] * v2[0]
    b1 = down0(r0, r1)
    recv_far = launch(regions.at[1], regions.at[0], far_reg, big_send, big_recv, FAR)
    recv_gk()
    e2 = 0.5 * (gk[0] + gk[1]).reshape(n // 2 * quarter, LANES)
    k2 = back(e2, 1, LANES // 2)
    coarse = coarse_cycle(e2, k2, n // 2, quarter, 16.0, 16.0, dot, times)
    recv_term()
    b1 = b1 + halo1[TERM, 0] + halo1[TERM, 1]

    def beside1(mine, i):
        return plane_sum(fx1, fy1, mine) + fz1lo * halo1[i, 0] + fz1hi * halo1[i, 1]

    def trade1(value, i):
        plane1[i] = value
        launch(plane1.at[i], plane1.at[i], halo1.at[i], small_send, small_recv, i)()

    a = wt1 * b1
    trade1(a, A1)
    a = (1.0 - DAMPING) * a + wt1 * (b1 + beside1(a, A1))
    trade1(a, A2)
    full = down1(b1 - dg1 * a + beside1(a, A2))
    gb[core, chip] = full[:quarter // 2] + back(full[quarter // 2:], 1, LANES // 2)
    share(gb, 2)
    recv_v2()
    base[0] = sweep0(0, v2[0], halo0[2, 0], v2[1])
    base[1] = sweep0(1, v2[1], v2[0], halo0[2, 1])
    recv_base = launch(base.at[0], base.at[1], halo0.at[3], big_send, big_recv, BASE)
    relay_gb = relay(gb, 2)
    recv_far()
    for p in range(2):
        region = halo_reg[p]
        beyond = face(e_side[p], dielectric(far_reg[p]), 1.0)
        fx, fy, total = plane_faces(e_side[p], 1.0)
        fxh[p] = fx
        fyh[p] = fy
        fzh[p] = beyond
        wth[p] = DAMPING / (total + beyond + fz0[2 * p] + jnp.where(region == 2, SCREEN, 0.0))
    relay_gb()
    packed = 0.5 * (gb[0] + gb[1]).reshape(n // 2 * quarter // 2, LANES)
    split = (n // 2, quarter // 2, LANES)
    b2 = jnp.concatenate(
        [packed.reshape(split), back(packed, 1, LANES // 2).reshape(split)], axis=1
    ).reshape(n // 2 * quarter, LANES)
    c2 = coarse(b2)

    for i in range(n // 2):
        c2_planes[i] = c2[i * quarter:(i + 1) * quarter]
    grow_l, grow_r = spread_left(half, quarter), spread_right(LANES, half, half)

    def up1(index):
        return dot(grow_l, times(c2_planes[index // 2], grow_r))

    halo1[A2, 0] = halo1[A2, 0] + jnp.where(has_lo, up1(jnp.maximum(me - 1, 0)), 0.0)
    halo1[A2, 1] = halo1[A2, 1] + jnp.where(has_hi, up1(jnp.minimum(me + 1, n - 1)), 0.0)
    a = a + up1(me)
    a = (1.0 - DAMPING) * a + wt1 * (b1 + beside1(a, A2))
    trade1(a, A3)
    a = (1.0 - DAMPING) * a + wt1 * (b1 + beside1(a, A3))
    trade1(a, A4)

    big_l, big_r = spread_left(nxy, half), spread_right(half, nxy, nxy)

    def up0(c):
        return dot(big_l, times(c, big_r))

    mine = up0(a)
    recv_base()
    v3, side = [], []
    present = [has_lo, has_hi]
    for p in range(2):
        c = up0(halo1[A4, p])
        own = plane_sum(fx0[p], fy0[p], mine) + fz0[1] * mine + fz0[2 * p] * c
        v3.append(base[p] + (1.0 - DAMPING) * mine + wt0[p] * own)
        other = plane_sum(fxh[p], fyh[p], c) + fzh[p] * c + fz0[2 * p] * mine
        swept = halo0[3, p] + (1.0 - DAMPING) * c + wth[p] * other
        side.append(jnp.where(present[p], swept, 0.0))
    out[0] = sweep0(0, v3[0], side[0], v3[1])
    out[1] = sweep0(1, v3[1], v3[0], side[1])

    for sent in pending:
        sent()
    all_in(got, many_send, 0)


HALO = 16
REG_LO, REG_HI, V0_LO, V0_HI, V1_LO, V1_HI, V2_LO, V2_HI, BASE_LO, BASE_HI = range(10)
E_M1, E_P1, E_M2, E_P2, K_M1, K_P1, B_M1, B_P1, B_M2, B_P2, A2_LO, A2_HI, NEAR, NEAR_CORE, FAR_LO, FAR_HI = range(10, 26)
MESSAGES = 26


def box_kernel(n, partials, regions, previous, out,
               parts, dens, reg, v0, b0, fx0, fy0, fz0, dg0, wt0, v1, v2, base, swept,
               near, fxn, fyn, fzn, wtn, landed, corr,
               e1, k1, fx1, fy1, fz1, dg1, wt1, pack, from_lo, from_hi, far_lo, far_hi,
               b1, a1, a2, a2c, a3, a4, gk, gb, c2_planes,
               load_sem, spread_send, spread_recv, corr_send, corr_recv, dens_send, dens_recv,
               side_send, side_recv, many_send, many_recv):
    me = lax.axis_index("slab")
    nz = n // 2
    z, x, core = me // 4, lax.rem(me // 2, 2), lax.rem(me, 2)
    zi = 2 * z + core
    nxy = regions.shape[1]
    half, quarter = nxy // 2, nxy // 4
    rows = partials.shape[2]
    window = half + HALO
    window1 = window // 2
    blocks = window // rows
    first = half - HALO

    def peer(index):
        return {"slab": index}

    def at(i, j):
        return (i // 2) * 4 + j * 2 + lax.rem(i, 2)

    load = pltpu.make_async_copy(partials, parts, load_sem.at[0])
    load.start()
    load_near = pltpu.make_async_copy(regions, near.at[pl.ds(2, 2)], load_sem.at[1])
    load_near.start()
    barrier = pltpu.get_barrier_semaphore()

    def greet(off, carry):
        pl.semaphore_signal(barrier, inc=1, device_id=peer(lax.rem(me + off, n)),
                            device_id_type=pl.DeviceIdType.MESH)
        return carry

    lax.fori_loop(1, n, greet, 0)

    plane0 = jnp.zeros((window, nxy), F32)
    plane1 = jnp.zeros((window1, half), F32)

    @pl.when(zi == 0)
    def _():
        for i in range(2):
            reg[i] = jnp.zeros((window, nxy), jnp.int32)
        for v in (v0, v1, v2, base):
            v[0] = plane0
        for i in range(3):
            from_lo[i] = plane1
        for i in range(2):
            e1[i] = plane1 + 1.0
            k1[i] = plane1
        a2[0] = plane1

    @pl.when(zi == nz - 1)
    def _():
        for i in range(2):
            reg[6 + i] = jnp.zeros((window, nxy), jnp.int32)
        for v in (v0, v1, v2, base):
            v[5] = plane0
        for i in range(3):
            from_hi[i] = plane1
        for i in range(2):
            e1[6 + i] = plane1 + 1.0
            k1[4 + i] = plane1
        a2[5] = plane1

    @pl.when(zi < 2)
    def _():
        far_lo[0] = plane1

    @pl.when(zi >= nz - 2)
    def _():
        far_hi[0] = plane1

    @pl.when(me == 0)
    def _():
        corr[0] = jnp.zeros((half, half), F32)

    @pl.when(me == n - 1)
    def _():
        corr[2] = jnp.zeros((half, half), F32)

    load.wait()
    density = parts[0].astype(F32)
    for g in range(1, partials.shape[0]):
        density = density + parts[g].astype(F32)
    dens[...] = (SOURCE * density).reshape(dens.shape)

    pl.semaphore_wait(barrier, n - 1)
    pending = []

    def spread(src, dst, low, i):
        for j in range(2):
            target = at(2 * z + x, j)
            piece = src.at[:, pl.ds(first * j, window), :]
            place = dst.at[pl.ds(low + 2 * core, 2)]
            remote = pltpu.make_async_remote_copy(
                src_ref=piece, dst_ref=place, send_sem=spread_send.at[i, j],
                recv_sem=spread_recv.at[i, core], device_id=peer(target),
                device_id_type=pl.DeviceIdType.MESH)
            here = pltpu.make_async_copy(piece, place, spread_recv.at[i, core])
            away = target != me
            pl.when(away)(remote.start)
            pl.when(jnp.logical_not(away))(here.start)
            pending.append(lambda remote=remote, away=away: pl.when(away)(remote.wait_send))

        def arrived():
            for j in range(2):
                place = dst.at[pl.ds(low + 2 * j, 2)]
                pltpu.make_async_copy(place, place, spread_recv.at[i, j]).wait()

        return arrived

    def send_density(step, carry):
        other = lax.rem(me + 1 + lax.rem(step + n // 2 - 1, n), n)
        oz, ox = 2 * (other // 4) + lax.rem(other, 2), lax.rem(other // 2, 2)
        block = me - (first // rows) * ox
        inside = (block >= 0) & (block < blocks)
        block = jnp.clip(block, 0, blocks - 1)
        place = b0.at[:, pl.ds(pl.multiple_of(block * rows, rows), rows), :]

        @pl.when(inside & (other != me))
        def _():
            pltpu.make_async_remote_copy(
                src_ref=dens.at[oz], dst_ref=place, send_sem=dens_send.at[other],
                recv_sem=dens_recv.at[0], device_id=peer(other),
                device_id_type=pl.DeviceIdType.MESH).start()

        @pl.when(inside & (other == me))
        def _():
            pltpu.make_async_copy(dens.at[oz], place, dens_recv.at[0]).start()

        return carry

    def sent_density(other, carry):
        ox = lax.rem(other // 2, 2)
        block = me - (first // rows) * ox

        @pl.when((block >= 0) & (block < blocks) & (other != me))
        def _():
            pltpu.make_async_copy(dens.at[0], dens.at[0], dens_send.at[other]).wait()

        return carry

    def push(src, dst, delta, i):
        can_send = (zi + delta >= 0) & (zi + delta < nz)
        can_recv = (zi - delta >= 0) & (zi - delta < nz)
        copy = pltpu.make_async_remote_copy(
            src_ref=src, dst_ref=dst, send_sem=side_send.at[i], recv_sem=side_recv.at[i],
            device_id=peer(at(jnp.clip(zi + delta, 0, nz - 1), x)),
            device_id_type=pl.DeviceIdType.MESH)
        pl.when(can_send)(copy.start)
        pending.append(lambda: pl.when(can_send)(copy.wait_send))
        return lambda: pl.when(can_recv)(copy.wait_recv)

    def trade(field, low, high, i):
        down = push(field.at[low], field.at[high + 1], -1, i)
        up = push(field.at[high], field.at[low - 1], 1, i + 1)

        def arrived():
            down()
            up()

        return arrived

    reg_in = spread(regions, reg, 2, 0)
    v0_in = spread(previous, v0, 1, 1)
    lax.fori_loop(0, n, send_density, 0)

    def dielectric(r):
        return jnp.where(r == 0, INSIDE, SOLVENT).astype(F32)

    right0, left0 = pool_right(nxy, half, nxy), pool_left(window1, window)
    right1 = pool_right(half, LANES, half)
    dst1, src1 = iota((quarter // 2, window1), 0), iota((quarter // 2, window1), 1)
    left1 = jnp.where((src1 - (HALO // 2) * x) // 2 == dst1, 1.0, 0.0).astype(F32)

    def down0(a):
        return 0.125 * dot2(left0, times2(a, right0))

    def down1(a):
        return 0.125 * dot2(left1, times2(a, right1))

    reg_in()
    reg_halo = trade(reg, 2, 5, REG_LO)
    e = [dielectric(reg[p]) for p in range(2, 6)]
    k = [jnp.where(reg[p] == 2, SCREEN, 0.0).astype(F32) for p in range(2, 6)]
    for i in range(2):
        e1[3 + i] = down0(e[2 * i] + e[2 * i + 1])
        k1[2 + i] = down0(k[2 * i] + k[2 * i + 1])
    e1_in = [push(e1.at[pl.ds(3, 2)], e1.at[pl.ds(1, 2)], 1, E_P1),
             push(e1.at[pl.ds(3, 2)], e1.at[pl.ds(5, 2)], -1, E_M1),
             push(e1.at[pl.ds(4, 1)], e1.at[pl.ds(0, 1)], 2, E_P2),
             push(e1.at[pl.ds(3, 1)], e1.at[pl.ds(7, 1)], -2, E_M2),
             push(k1.at[pl.ds(2, 2)], k1.at[pl.ds(0, 2)], 1, K_P1),
             push(k1.at[pl.ds(2, 2)], k1.at[pl.ds(4, 2)], -1, K_M1)]
    chip = me // 2
    gk[core, x, z] = down1(e1[3] + e1[4]) + back(down1(k1[2] + k1[3]), 1, LANES // 2)

    def share(ref, i):
        def one(off, carry):
            other = lax.rem(me + 2 * off, n)
            pltpu.make_async_remote_copy(
                src_ref=ref.at[core, chip], dst_ref=ref.at[core, chip], send_sem=many_send.at[i],
                recv_sem=many_recv.at[i], device_id=peer(other),
                device_id_type=pl.DeviceIdType.MESH).start()
            return carry

        lax.fori_loop(1, n // 2, one, 0)

    def relay(ref, i):
        seven = ref.at[0, pl.ds(0, n // 2 - 1)]
        pltpu.make_async_copy(seven, seven, many_recv.at[i]).wait()
        copy = pltpu.make_async_remote_copy(
            src_ref=ref.at[core], dst_ref=ref.at[core], send_sem=many_send.at[i + 2],
            recv_sem=many_recv.at[i + 2], device_id=peer(me + 1 - 2 * core),
            device_id_type=pl.DeviceIdType.MESH)
        copy.start()
        pending.append(pltpu.make_async_copy(seven, seven, many_send.at[i]).wait)
        pending.append(copy.wait_send)
        return copy.wait_recv

    def in_order(ref):
        return [ref[c, 2 * i + j] for i in range(n // 4) for c in range(2) for j in range(2)]

    columns = n // 4

    def along(off, carry):
        other = lax.rem(me + 4 * off, n)
        pltpu.make_async_remote_copy(
            src_ref=gk.at[core, x, z], dst_ref=gk.at[core, x, z], send_sem=many_send.at[0],
            recv_sem=many_recv.at[0], device_id=peer(other),
            device_id_type=pl.DeviceIdType.MESH).start()
        return carry

    lax.fori_loop(1, columns, along, 0)

    def gk_over():
        others = gk.at[0, 0, pl.ds(0, columns - 1)]
        pltpu.make_async_copy(others, others, many_recv.at[0]).wait()
        copy = pltpu.make_async_remote_copy(
            src_ref=gk.at[core, x], dst_ref=gk.at[core, x], send_sem=many_send.at[4],
            recv_sem=many_recv.at[4], device_id=peer(at(zi, 1 - x)),
            device_id_type=pl.DeviceIdType.MESH)
        copy.start()
        pending.append(pltpu.make_async_copy(others, others, many_send.at[0]).wait)
        pending.append(copy.wait_send)
        return copy.wait_recv

    def gk_beside():
        copy = pltpu.make_async_remote_copy(
            src_ref=gk.at[core], dst_ref=gk.at[core], send_sem=many_send.at[2],
            recv_sem=many_recv.at[2], device_id=peer(at(zi + 1 - 2 * core, x)),
            device_id_type=pl.DeviceIdType.MESH)
        copy.start()
        pending.append(copy.wait_send)
        return copy.wait_recv

    totals = []
    for p in range(4):
        fx, fy, total = plane_faces(e[p], 1.0)
        fx0[p] = fx
        fy0[p] = fy
        totals.append(total + k[p])
    for p in range(1, 4):
        fz0[p] = face(e[p - 1], e[p], 1.0)
    v0_in()
    v0_halo = trade(v0, 1, 4, V0_LO)
    far_in = [push(reg.at[3], reg.at[7], -1, FAR_LO), push(reg.at[4], reg.at[0], 1, FAR_HI)]

    def beside0(p, v):
        return (plane_sum(fx0[p], fy0[p], v[p + 1]) + fz0[p] * v[p] + fz0[p + 1] * v[p + 2])

    def sweep0(p, v):
        return (1.0 - DAMPING) * v[p + 1] + wt0[p] * (b0[p] + beside0(p, v))

    def first_part(p):
        v1[p + 1] = (1.0 - DAMPING) * v0[p + 1] + wt0[p] * beside0(p, v0)

    def weights(p):
        diag = totals[p] + fz0[p] + fz0[p + 1]
        dg0[p] = diag
        wt0[p] = DAMPING / diag

    for p in (1, 2):
        weights(p)
        first_part(p)
    reg_halo()
    fz0[0] = face(jnp.where(zi > 0, dielectric(reg[1]), e[0]), e[0], 1.0)
    fz0[4] = face(e[3], jnp.where(zi < nz - 1, dielectric(reg[6]), e[3]), 1.0)
    weights(0)
    weights(3)
    v0_halo()
    first_part(0)
    first_part(3)

    pltpu.make_async_copy(b0, b0, dens_recv.at[0]).wait()
    for p in (0, 3):
        v1[p + 1] = v1[p + 1] + wt0[p] * b0[p]
    v1_halo = trade(v1, 1, 4, V1_LO)
    for arrived in far_in:
        arrived()
    own_rows = pl.ds(pl.multiple_of(HALO * x, HALO), half)

    def near_rows(j):
        return near.at[pl.ds(4 * core, 2), pl.ds(pl.multiple_of(half * j, half), half), :]

    across = pltpu.make_async_remote_copy(
        src_ref=reg.at[pl.ds(4 + 2 * core - 4 * x, 2), own_rows, :], dst_ref=near_rows(x),
        send_sem=side_send.at[NEAR], recv_sem=side_recv.at[NEAR], device_id=peer(at(zi, 1 - x)),
        device_id_type=pl.DeviceIdType.MESH)
    beside = pltpu.make_async_remote_copy(
        src_ref=regions, dst_ref=near.at[pl.ds(4 * core, 2)], send_sem=side_send.at[NEAR_CORE],
        recv_sem=side_recv.at[NEAR_CORE], device_id=peer(at(zi + 1 - 2 * core, x)),
        device_id_type=pl.DeviceIdType.MESH)
    within = pltpu.make_async_copy(reg.at[pl.ds(2 * core + 4 * x, 2), own_rows, :], near_rows(x),
                                   load_sem.at[2])
    for copy in (across, beside, within):
        copy.start()
    pending.append(across.wait_send)
    pending.append(beside.wait_send)
    gk_across = gk_over()

    for p in (1, 2):
        v1[p + 1] = v1[p + 1] + wt0[p] * b0[p]

    for p in (1, 2):
        v2[p + 1] = sweep0(p, v1)
    v1_halo()
    for p in (0, 3):
        v2[p + 1] = sweep0(p, v1)
    v2_halo = trade(v2, 1, 4, V2_LO)
    pack[0] = down0(fz0[4] * v2[4])
    pack[3] = down0(fz0[0] * v2[1])

    def left_over(p):
        r = b0[p] - dg0[p] * v2[p + 1] + plane_sum(fx0[p], fy0[p], v2[p + 1])
        if p > 0:
            r = r + fz0[p] * v2[p]
        if p < 3:
            r = r + fz0[p + 1] * v2[p + 2]
        return r

    for i in range(2):
        pack[1 + i] = down0(left_over(2 * i) + left_over(2 * i + 1))
    b1_in = [push(pack.at[pl.ds(0, 3)], from_lo, 1, B_P1),
             push(pack.at[pl.ds(1, 3)], from_hi, -1, B_M1),
             push(pack.at[pl.ds(0, 1)], far_lo, 2, B_P2),
             push(pack.at[pl.ds(3, 1)], far_hi, -2, B_M2)]
    for arrived in e1_in:
        arrived()

    @pl.when(zi == 0)
    def _():
        e1[2] = e1[3]
        e1[0] = plane1 + 1.0

    @pl.when(zi == 1)
    def _():
        e1[0] = e1[1]

    @pl.when(zi == nz - 1)
    def _():
        e1[5] = e1[4]
        e1[7] = plane1 + 1.0

    @pl.when(zi == nz - 2)
    def _():
        e1[7] = e1[6]

    s1 = 4.0
    for i in range(7):
        fz1[i] = face(e1[i], e1[i + 1], s1)
    for i in range(6):
        fx, fy, total = plane_faces(e1[i + 1], s1)
        fx1[i] = fx
        fy1[i] = fy
        diag = total + fz1[i] + fz1[i + 1] + k1[i]
        dg1[i] = diag
        weight = DAMPING / diag
        if i < 2:
            weight = jnp.where(zi > 0, weight, 0.0)
        if i > 3:
            weight = jnp.where(zi < nz - 1, weight, 0.0)
        wt1[i] = weight

    v2_halo()
    for p in (0, 3, 1, 2):
        base[p + 1] = sweep0(p, v2)
    base_halo = trade(base, 1, 4, BASE_LO)
    for arrived in b1_in:
        arrived()
    b1[0] = from_lo[1] + far_lo[0]
    b1[1] = from_lo[2] + pack[3]
    b1[2] = pack[1] + from_lo[0]
    b1[3] = pack[2] + from_hi[2]
    b1[4] = from_hi[0] + pack[0]
    b1[5] = from_hi[1] + far_hi[0]

    def beside1(i, mine, below, above):
        return plane_sum(fx1[i], fy1[i], mine) + fz1[i] * below + fz1[i + 1] * above

    def sweep1(i, mine, below, above):
        return (1.0 - DAMPING) * mine + wt1[i] * (b1[i] + beside1(i, mine, below, above))

    for i in range(6):
        a1[i] = wt1[i] * b1[i]
    for i in range(1, 5):
        a2[i] = sweep1(i, a1[i], a1[i - 1], a1[i + 1])
    rest = [b1[i] - dg1[i] * a2[i] + beside1(i, a2[i], a2[i - 1], a2[i + 1]) for i in (2, 3)]
    full = down1(rest[0] + rest[1])
    gb[core, chip] = full[:quarter // 4] + back(full[quarter // 4:], 1, LANES // 2)
    share(gb, 1)
    a2_in = [push(a2.at[2], a2.at[0], 1, A2_HI), push(a2.at[3], a2.at[5], -1, A2_LO)]
    gk_across()
    gk_in = gk_beside()
    gk_in()
    e2 = jnp.concatenate([gk[i, j, m] for m in range(n // 4) for i in range(2) for j in range(2)], axis=0)
    coarse = coarse_cycle(e2, back(e2, 1, LANES // 2), nz, quarter, 16.0, 16.0,
                          dot2, times2)
    base_halo()

    def deliver(j):
        target = 4 * z + 2 * core + j
        piece = swept.at[pl.ds(2 * j, 2), pl.ds(pl.multiple_of(HALO * x, HALO), half), :]
        place = landed.at[:, pl.ds(pl.multiple_of(half * x, half), half), :]
        remote = pltpu.make_async_remote_copy(
            src_ref=piece, dst_ref=place, send_sem=spread_send.at[2, j],
            recv_sem=spread_recv.at[2, x], device_id=peer(target),
            device_id_type=pl.DeviceIdType.MESH)
        here = pltpu.make_async_copy(piece, place, spread_recv.at[2, x])
        away = target != me
        pl.when(away)(remote.start)
        pl.when(jnp.logical_not(away))(here.start)
        pending.append(lambda: pl.when(away)(remote.wait_send))

    for p in range(4):
        swept[p] = sweep0(p, base)
        if p % 2:
            deliver(p // 2)
    gb_in = relay(gb, 1)
    gb_in()
    packed = jnp.stack(in_order(gb))
    b2 = jnp.concatenate([packed, back(packed.reshape(-1, LANES), 1, LANES // 2).reshape(packed.shape)],
                         axis=1).reshape(nz * quarter, LANES)
    c2 = coarse(b2)
    for i in range(nz):
        c2_planes[i] = c2[i * quarter:(i + 1) * quarter]
    fine, mid = iota((window1, quarter), 0), iota((window1, quarter), 1)
    grow_l = jnp.where((fine + first // 2 * x) // 2 == mid, 1.0, 0.0).astype(F32)
    grow_r = spread_right(LANES, half, half)

    def up1(index):
        return dot2(grow_l, times2(c2_planes[index], grow_r))


    for arrived in a2_in:
        arrived()
    mine = up1(zi)
    lower = jnp.where(zi > 0, up1(jnp.maximum(zi - 1, 0)), 0.0)
    upper = jnp.where(zi < nz - 1, up1(jnp.minimum(zi + 1, nz - 1)), 0.0)
    for i, c in enumerate((lower, lower, mine, mine, upper, upper)):
        a2c[i] = a2[i] + c
    for i in range(1, 5):
        a3[i - 1] = sweep1(i, a2c[i], a2c[i - 1], a2c[i + 1])
    for i in (1, 2):
        a4[i] = sweep1(i + 1, a3[i], a3[i - 1], a3[i + 1])

    def hand(count, low, delta, slot, i):
        target = 2 * zi + delta
        exists = (target >= 0) & (target < n)
        piece = a4.at[pl.ds(low, count), pl.ds(pl.multiple_of(HALO // 2 * x, HALO // 2), quarter), :]
        place = corr.at[pl.ds(slot, count), pl.ds(pl.multiple_of(quarter * x, quarter), quarter), :]
        kind = 2 - count
        remote = pltpu.make_async_remote_copy(
            src_ref=piece, dst_ref=place, send_sem=corr_send.at[i], recv_sem=corr_recv.at[kind, x],
            device_id=peer(jnp.clip(target, 0, n - 1)), device_id_type=pl.DeviceIdType.MESH)
        here = pltpu.make_async_copy(piece, place, corr_recv.at[kind, x])
        away = exists & (target != me)
        pl.when(away)(remote.start)
        pl.when(target == me)(here.start)
        pending.append(lambda: pl.when(away)(remote.wait_send))

    hand(2, 1, 0, 1, 0)
    hand(2, 1, 1, 0, 1)
    hand(1, 1, -1, 2, 2)
    hand(1, 2, 2, 0, 3)
    big_l, big_r = spread_left(nxy, half), spread_right(half, nxy, nxy)

    def up0(c):
        return dot2(big_l, times2(c, big_r))

    load_near.wait()
    within.wait()
    across.wait_recv()
    beside.wait_recv()
    en = [dielectric(near[f]) for f in range(6)]
    fzn[0] = face(en[0], en[1], 1.0)
    fzn[1] = face(jnp.where(me > 0, en[1], en[2]), en[2], 1.0)
    fzn[2] = face(en[2], en[3], 1.0)
    fzn[3] = face(en[3], jnp.where(me < n - 1, en[4], en[3]), 1.0)
    fzn[4] = face(en[4], en[5], 1.0)
    for f in range(4):
        fx, fy, total = plane_faces(en[f + 1], 1.0)
        fxn[f] = fx
        fyn[f] = fy
        kn = jnp.where(near[f + 1] == 2, SCREEN, 0.0).astype(F32)
        wtn[f] = DAMPING / (total + kn + fzn[f] + fzn[f + 1])
    for sent in pending:
        sent()
    lax.fori_loop(0, n, sent_density, 0)
    single = jnp.where(lax.rem(me, 2) == 0, me > 0, me < n - 1)
    for j in range(2):
        both = corr.at[pl.ds(0, 2), pl.ds(quarter * j, quarter), :]
        pltpu.make_async_copy(both, both, corr_recv.at[0, j]).wait()
        one = corr.at[pl.ds(0, 1), pl.ds(quarter * j, quarter), :]
        pl.when(single)(pltpu.make_async_copy(one, one, corr_recv.at[1, j]).wait)
    for j in range(2):
        place = landed.at[:, pl.ds(half * j, half), :]
        pltpu.make_async_copy(place, place, spread_recv.at[2, j]).wait()
    below, here, above = (up0(corr[i]) for i in range(3))
    spans = [(below, below, here), (here, below, here), (here, here, above), (above, here, above)]

    def relax(f, mine, low, high):
        return (1.0 - DAMPING) * mine + wtn[f] * (
            plane_sum(fxn[f], fyn[f], mine) + fzn[f] * low + fzn[f + 1] * high)

    y = [relax(f, *spans[f]) for f in range(4)]
    y[0] = jnp.where(me > 0, y[0], 0.0)
    y[3] = jnp.where(me < n - 1, y[3], 0.0)
    for f in (1, 2):
        out[f - 1] = landed[f - 1] + relax(f, y[f], y[f - 1], y[f + 1])


def box_local(partials, regions, previous):
    n = lax.axis_size("slab")
    nxy = regions.shape[1]
    half, quarter = nxy // 2, nxy // 4
    rows = partials.shape[2]
    window, window1 = half + HALO, (half + HALO) // 2
    vmem = lambda *shape: pltpu.VMEM(shape, F32)
    big = lambda count: vmem(count, window, nxy)
    small = lambda count: vmem(count, window1, half)
    return pl.pallas_call(
        functools.partial(box_kernel, n),
        out_shape=pltpu.VMEM(previous.shape, F32),
        in_specs=[pl.BlockSpec(memory_space=pltpu.HBM)] * 3,
        out_specs=pl.BlockSpec(memory_space=pltpu.VMEM),
        scratch_shapes=[
            pltpu.VMEM(partials.shape, partials.dtype), vmem(n // 2, 4, rows, nxy),
            pltpu.VMEM((8, window, nxy), jnp.int32), big(6), big(4),
            big(4), big(4), big(5), big(4), big(4), big(6), big(6), big(6), big(4),
            pltpu.VMEM((6, nxy, nxy), jnp.int32), vmem(4, nxy, nxy), vmem(4, nxy, nxy),
            vmem(5, nxy, nxy), vmem(4, nxy, nxy), vmem(2, nxy, nxy), vmem(3, half, half),
            small(8), small(6), small(6), small(6), small(7), small(6), small(6),
            small(4), small(3), small(3), small(1), small(1),
            small(6), small(6), small(6), small(6), small(4), small(4),
            vmem(2, 2, n // 4, quarter // 2, LANES), vmem(2, n // 2, quarter // 4, LANES),
            vmem(n // 2, quarter, LANES),
            pltpu.SemaphoreType.DMA((3,)),
            pltpu.SemaphoreType.DMA((3, 2)), pltpu.SemaphoreType.DMA((3, 2)),
            pltpu.SemaphoreType.DMA((4,)), pltpu.SemaphoreType.DMA((2, 2)),
            pltpu.SemaphoreType.DMA((n,)), pltpu.SemaphoreType.DMA((1,)),
            pltpu.SemaphoreType.DMA((MESSAGES,)), pltpu.SemaphoreType.DMA((MESSAGES,)),
            pltpu.SemaphoreType.DMA((5,)), pltpu.SemaphoreType.DMA((5,)),
        ],
        compiler_params=pltpu.CompilerParams(
            collective_id=1, has_side_effects=True, vmem_limit_bytes=60 * 1024 * 1024),
    )(partials, regions, previous)


def local(partials, regions, previous):
    n = lax.axis_size("slab")
    nxy = regions.shape[1]
    half, quarter = nxy // 2, nxy // 4
    rows = partials.shape[2]
    vmem = lambda *shape: pltpu.VMEM(shape, F32)
    spec = pl.BlockSpec(memory_space=pltpu.VMEM)
    return pl.pallas_call(
        functools.partial(kernel, n),
        out_shape=jax.ShapeDtypeStruct(previous.shape, F32),
        in_specs=[spec] * 3,
        out_specs=spec,
        scratch_shapes=[
            vmem(n, 2, rows, nxy), vmem(n, 2, rows, nxy), vmem(2, nxy, nxy),
            vmem(2, nxy, nxy), vmem(2, nxy, nxy), vmem(3, nxy, nxy), vmem(2, nxy, nxy),
            vmem(2, nxy, nxy),
            pltpu.VMEM((2, nxy, nxy), jnp.int32), pltpu.VMEM((2, nxy, nxy), jnp.int32),
            vmem(2, nxy, nxy), vmem(2, nxy, nxy), vmem(2, nxy, nxy), vmem(2, nxy, nxy),
            vmem(4, 2, nxy, nxy),
            vmem(2, nxy, nxy), vmem(2, nxy, nxy), vmem(2, nxy, nxy),
            vmem(6, 2, half, half), vmem(5, half, half), vmem(2, half, half),
            vmem(2, n // 2, quarter // 2, LANES), vmem(2, n // 2, quarter, LANES),
            pltpu.SemaphoreType.DMA((6, 2)), pltpu.SemaphoreType.DMA((6, 2)),
            pltpu.SemaphoreType.DMA((6, 2)), pltpu.SemaphoreType.DMA((6, 2)),
            pltpu.SemaphoreType.DMA((5,)), pltpu.SemaphoreType.DMA((5,)),
            vmem(n // 2, quarter, LANES),
        ],
        compiler_params=pltpu.CompilerParams(
            collective_id=0, has_side_effects=True, vmem_limit_bytes=60 * 1024 * 1024),
    )(partials, regions, previous)


def solution(mesh):
    in_specs = (
        P("job", None, "slab", None),
        P(("job", "slab"), None, None),
        P(("job", "slab"), None, None),
    )
    out_specs = P(("job", "slab"), None, None)
    size = mesh.shape["slab"]

    def fits(partials, regions):
        return (size == 16 and partials.shape[2] == 16 * size and partials.shape[1] == 2 * size
                and regions.shape[1] == 16 * size)

    def program(partials, regions, previous):
        chosen = box_local if fits(partials, regions) else local
        return jax.shard_map(chosen, mesh=mesh, in_specs=in_specs, out_specs=out_specs, check_vma=False)(
            partials, regions, previous)

    return program
```

```python
import functools

import jax
import jax.numpy as jnp
from jax import lax
from jax.experimental import pallas as pl
from jax.experimental.pallas import tpu as pltpu
from jax.sharding import PartitionSpec as P

PRE_SWEEPS = 2
POST_SWEEPS = 2
COARSE_SWEEPS = 4

DAMPING = 0.75
INSIDE = 2.0
SOLVENT = 78.4
SCREEN = 1.4
SOURCE = 16.0 * 3.141592653589793

F32 = jnp.float32
LANES = 128


def iota(shape, dim):
    return lax.broadcasted_iota(jnp.int32, shape, dim)


def face(mine, other, spacing):
    return mine * other / ((mine + other) * (0.5 * spacing))


def back(v, dim, by=1):
    return pltpu.roll(v, by, dim)


def ahead(v, dim, by=1):
    return pltpu.roll(v, v.shape[dim] - by, dim)


def terms(v):
    result = []
    for _ in range(3):
        result.append(v.astype(jnp.bfloat16))
        v = v - result[-1].astype(F32)
    return result


def product(a, b):
    return lax.dot_general(a, b, (((1,), (0,)), ((), ())), preferred_element_type=F32)


def times(v, selector):
    high, middle, low = (product(t, selector.astype(jnp.bfloat16)) for t in terms(v))
    return high + (middle + low)


def dot(selector, v):
    high, middle, low = (product(selector.astype(jnp.bfloat16), t) for t in terms(v))
    return high + (middle + low)


def halves(v):
    high = v.astype(jnp.bfloat16)
    return high, (v - high.astype(F32)).astype(jnp.bfloat16)


def times2(v, selector):
    high, low = (product(t, selector.astype(jnp.bfloat16)) for t in halves(v))
    return high + low


def dot2(selector, v):
    high, low = (product(selector.astype(jnp.bfloat16), t) for t in halves(v))
    return high + low


def pool_right(wide, narrow, valid):
    src, dst = iota((wide, narrow), 0), iota((wide, narrow), 1)
    return jnp.where((src // 2 == dst) & (src < valid), 1.0, 0.0).astype(F32)


def pool_left(narrow, wide):
    dst, src = iota((narrow, wide), 0), iota((narrow, wide), 1)
    return jnp.where(src // 2 == dst, 1.0, 0.0).astype(F32)


def spread_right(narrow, wide, valid):
    src, dst = iota((narrow, wide), 0), iota((narrow, wide), 1)
    return jnp.where((dst // 2 == src) & (dst < valid), 1.0, 0.0).astype(F32)


def spread_left(wide, narrow):
    dst, src = iota((wide, narrow), 0), iota((wide, narrow), 1)
    return jnp.where(dst // 2 == src, 1.0, 0.0).astype(F32)


def plane_faces(e, spacing):
    rows, cols = e.shape
    x, y = iota(e.shape, 0), iota(e.shape, 1)
    fx = jnp.where(x > 0, face(e, back(e, 0), spacing), 0.0)
    fy = jnp.where(y > 0, face(e, back(e, 1), spacing), 0.0)
    edges = (jnp.where((x == 0) | (x == rows - 1), 1.0, 0.0)
             + jnp.where((y == 0) | (y == cols - 1), 1.0, 0.0))
    total = fx + ahead(fx, 0) + fy + ahead(fy, 1) + edges * e * (1.0 / spacing)
    return fx, fy, total


def plane_sum(fx, fy, v):
    return fx * back(v, 0) + ahead(fx * v, 0) + fy * back(v, 1) + ahead(fy * v, 1)


def coarse_cycle(e, k, planes, nx, sz, sx, dot, times, pairs=None):
    rows = e.shape[0]
    row, lane = iota(e.shape, 0), iota(e.shape, 1)
    x, z = row % nx, row // nx
    valid = (row < planes * nx) & (lane < nx)
    e = jnp.where(valid, e, 1.0)
    fx = jnp.where(valid & (x > 0), face(e, back(e, 0), sx), 0.0) if nx > 1 else None
    fy = jnp.where(valid & (lane > 0), face(e, back(e, 1), sx), 0.0) if nx > 1 else None
    wrap = nx % rows
    fz = jnp.where(valid & (z > 0), face(e, back(e, 0, wrap), sz), 0.0) if planes > 1 else None
    diag = k + e * (
        (jnp.where(x == 0, 1.0, 0.0) + jnp.where(x == nx - 1, 1.0, 0.0)
         + jnp.where(lane == 0, 1.0, 0.0) + jnp.where(lane == nx - 1, 1.0, 0.0)) * (1.0 / sx)
        + (jnp.where(z == 0, 1.0, 0.0) + jnp.where(z == planes - 1, 1.0, 0.0)) * (1.0 / sz))
    if nx > 1:
        diag = diag + fx + ahead(fx, 0) + fy + ahead(fy, 1)
    if planes > 1:
        diag = diag + fz + ahead(fz, 0, wrap)
    w = jnp.where(valid, DAMPING / jnp.where(valid, diag, 1.0), 0.0)

    def beside(v):
        total = jnp.zeros_like(v)
        if nx > 1:
            total = plane_sum(fx, fy, v)
        if planes > 1:
            total = total + fz * back(v, 0, wrap) + ahead(fz * v, 0, wrap)
        return total

    def sweep(v, b):
        return (1.0 - DAMPING) * v + w * (b + beside(v))

    def coarsest(b):
        v = w * b
        for _ in range(COARSE_SWEEPS - 1):
            v = sweep(v, b)
        return v

    if planes == 1:
        return coarsest
    halve = nx > 1 and nx % 2 == 0
    nx2 = nx // 2 if halve else nx
    sx2 = sx * 4.0 if halve else sx
    step = planes
    while step * nx > 512 and step % 4 == 0:
        step //= 2
    part = step * nx
    if step == planes:
        part = rows
    real2 = planes // 2 * nx2
    rows2 = max(8, real2)
    part2 = rows2 if step == planes else step // 2 * nx2
    ratio = 2 if halve else 1

    def member(fine, coarse):
        return ((fine < step * nx) & ((fine // nx // 2) * nx2 + fine % nx // ratio == coarse))

    down = jnp.where(member(iota((part2, part), 1), iota((part2, part), 0)), 1.0, 0.0)
    up = jnp.where(member(iota((part, part2), 0), iota((part, part2), 1)), 1.0, 0.0)
    if halve:
        right = pool_right(LANES, LANES, nx)
        left = spread_right(LANES, LANES, nx)
        scale = 0.125
    else:
        scale = 0.5

    def coarsen(f):
        if pairs is not None:
            f = jnp.sum(f.reshape(planes // 2, 2, nx, LANES), axis=1).reshape(planes // 2 * nx, LANES)
            return scale * times(pairs[0](f), right)
        if halve:
            f = times(f, right)
        parts = [dot(down, f[i:i + part]) for i in range(0, rows, part)]
        return scale * (parts[0] if len(parts) == 1 else jnp.concatenate(parts, axis=0))

    def refine(f):
        if pairs is not None:
            f = pairs[1](times(f, left)).reshape(planes // 2, 1, nx, LANES)
            return jnp.broadcast_to(f, (planes // 2, 2, nx, LANES)).reshape(planes * nx, LANES)
        if halve:
            f = times(f, left)
        parts = [dot(up, f[i:i + part2]) for i in range(0, rows2, part2)]
        return parts[0] if len(parts) == 1 else jnp.concatenate(parts, axis=0)

    below = coarse_cycle(coarsen(jnp.where(valid, e, 0.0)), coarsen(k),
                         planes // 2, nx2, sz * 4.0, sx2, dot, times, pairs)

    def run(b):
        v = w * b
        for _ in range(PRE_SWEEPS - 1):
            v = sweep(v, b)
        r = jnp.where(valid, b - diag * v + beside(v), 0.0)
        v = v + refine(below(coarsen(r)))
        for _ in range(POST_SWEEPS):
            v = sweep(v, b)
        return v

    return run


REG, V0, V1, V2, BASE, FAR = range(6)
E1, A1, A2, A3, A4, TERM = range(6)


def kernel(n, partials, regions, previous, out,
           dens, got, b0, fx0, fy0, fz0, dg0, wt0, halo_reg, far_reg, fxh, fyh, fzh, wth, halo0, v1, v2, base,
           halo1, plane1, term1, gb, gk,
           big_send, big_recv, small_send, small_recv, many_send, many_recv, c2_planes):
    me = lax.axis_index("slab")
    job = lax.axis_index("job")
    nxy = regions.shape[1]
    half = nxy // 2
    quarter = nxy // 4
    rows = partials.shape[2]
    has_lo, has_hi = me > 0, me < n - 1

    def peer(index):
        return {"slab": index}

    barrier = pltpu.get_barrier_semaphore()

    def greet(off, carry):
        pl.semaphore_signal(barrier, inc=1, device_id=peer(lax.rem(me + off, n)),
                            device_id_type=pl.DeviceIdType.MESH)
        return carry

    lax.fori_loop(1, n, greet, 0)

    @pl.when(jnp.logical_not(has_lo))
    def _():
        for i in range(4):
            halo0[i, 0] = jnp.zeros((nxy, nxy), F32)
        for i in range(6):
            halo1[i, 0] = jnp.zeros((half, half), F32)
        halo_reg[0] = jnp.zeros((nxy, nxy), jnp.int32)
        far_reg[0] = jnp.zeros((nxy, nxy), jnp.int32)

    @pl.when(jnp.logical_not(has_hi))
    def _():
        for i in range(4):
            halo0[i, 1] = jnp.zeros((nxy, nxy), F32)
        for i in range(6):
            halo1[i, 1] = jnp.zeros((half, half), F32)
        halo_reg[1] = jnp.zeros((nxy, nxy), jnp.int32)
        far_reg[1] = jnp.zeros((nxy, nxy), jnp.int32)

    density = partials[0].astype(F32)
    for g in range(1, partials.shape[0]):
        density = density + partials[g].astype(F32)
    dens[...] = (SOURCE * density).reshape(dens.shape)

    pl.semaphore_wait(barrier, n - 1)

    def copies(first, last, dst, sends, recvs, i):
        to_lo = pltpu.make_async_remote_copy(
            src_ref=first, dst_ref=dst.at[1], send_sem=sends.at[i, 0], recv_sem=recvs.at[i, 1],
            device_id=peer(jnp.maximum(me - 1, 0)), device_id_type=pl.DeviceIdType.MESH)
        to_hi = pltpu.make_async_remote_copy(
            src_ref=last, dst_ref=dst.at[0], send_sem=sends.at[i, 1], recv_sem=recvs.at[i, 0],
            device_id=peer(jnp.minimum(me + 1, n - 1)), device_id_type=pl.DeviceIdType.MESH)

        def start():
            pl.when(has_lo)(to_lo.start)
            pl.when(has_hi)(to_hi.start)

        def recv():
            pl.when(has_lo)(to_hi.wait_recv)
            pl.when(has_hi)(to_lo.wait_recv)

        def sent():
            pl.when(has_lo)(to_lo.wait_send)
            pl.when(has_hi)(to_hi.wait_send)

        return start, recv, sent

    pending = []

    def launch(first, last, dst, sends, recvs, i):
        start, recv, sent = copies(first, last, dst, sends, recvs, i)
        start()
        pending.append(sent)
        return recv

    recv_reg = launch(regions.at[0], regions.at[1], halo_reg, big_send, big_recv, REG)
    recv_v0 = launch(previous.at[0], previous.at[1], halo0.at[0], big_send, big_recv, V0)

    def scatter(step, carry):
        other = lax.rem(me + 1 + lax.rem(step + n // 2 - 1, n - 1), n)
        pltpu.make_async_remote_copy(
            src_ref=dens.at[other], dst_ref=got.at[me], send_sem=many_send.at[0],
            recv_sem=many_recv.at[0], device_id=peer(other),
            device_id_type=pl.DeviceIdType.MESH).start()
        return carry

    lax.fori_loop(0, n - 1, scatter, 0)

    def dielectric(r):
        return jnp.where(r == 0, INSIDE, SOLVENT).astype(F32)

    e = [dielectric(regions[p]) for p in range(2)]
    k = [jnp.where(regions[p] == 2, SCREEN, 0.0).astype(F32) for p in range(2)]
    right0, left0 = pool_right(nxy, half, nxy), pool_left(half, nxy)
    right1, left1 = pool_right(half, LANES, half), pool_left(quarter, half)

    def down0(a, b):
        return 0.125 * dot(left0, times(a + b, right0))

    def down1(a):
        return 0.25 * dot(left1, times(a, right1))

    e1, k1 = down0(e[0], e[1]), down0(k[0], k[1])
    plane1[E1] = e1
    recv_e1 = launch(plane1.at[E1], plane1.at[E1], halo1.at[E1], small_send, small_recv, E1)
    core, chip = lax.rem(me, 2), me // 2
    gk[core, chip] = down1(e1) + back(down1(k1), 1, LANES // 2)

    def share(ref, i):
        def one(off, carry):
            other = lax.rem(me + 2 * off, n)
            pltpu.make_async_remote_copy(
                src_ref=ref.at[core, chip], dst_ref=ref.at[core, chip], send_sem=many_send.at[i],
                recv_sem=many_recv.at[i], device_id=peer(other),
                device_id_type=pl.DeviceIdType.MESH).start()
            return carry

        lax.fori_loop(1, n // 2, one, 0)

    def relay(ref, i):
        window = ref.at[0, pl.ds(0, n // 2 - 1)]
        pltpu.make_async_copy(window, window, many_recv.at[i]).wait()
        copy = pltpu.make_async_remote_copy(
            src_ref=ref.at[core], dst_ref=ref.at[core], send_sem=many_send.at[i + 2],
            recv_sem=many_recv.at[i + 2], device_id=peer(me + 1 - 2 * core),
            device_id_type=pl.DeviceIdType.MESH)
        copy.start()
        pending.append(pltpu.make_async_copy(window, window, many_send.at[i]).wait)
        pending.append(copy.wait_send)
        return copy.wait_recv

    def all_in(ref, sems, i):
        window = ref.at[pl.ds(0, n - 1)]
        pltpu.make_async_copy(window, window, sems.at[i]).wait()

    share(gk, 1)

    totals = []
    middle = face(e[0], e[1], 1.0)
    fz0[1] = middle
    part = []
    for p in range(2):
        fx, fy, total = plane_faces(e[p], 1.0)
        fx0[p] = fx
        fy0[p] = fy
        totals.append(total + middle + k[p])
        part.append(plane_sum(fx, fy, previous[p]) + middle * previous[1 - p])
    recv_reg()
    e_side = [jnp.where(has_lo, dielectric(halo_reg[0]), e[0]),
              jnp.where(has_hi, dielectric(halo_reg[1]), e[1])]
    for p in range(2):
        outer = face(e_side[p], e[p], 1.0)
        fz0[2 * p] = outer
        total = totals[p] + outer
        dg0[p] = total
        wt0[p] = DAMPING / total

    def beside0(p, mine, below, above):
        return plane_sum(fx0[p], fy0[p], mine) + fz0[p] * below + fz0[p + 1] * above

    def sweep0(p, mine, below, above):
        return (1.0 - DAMPING) * mine + wt0[p] * (b0[p] + beside0(p, mine, below, above))

    recv_v0()
    for p in range(2):
        v1[p] = (1.0 - DAMPING) * previous[p] + wt0[p] * (part[p] + fz0[2 * p] * halo0[0, p])

    got[me] = dens[me]
    all_in(got, many_recv, 0)
    for p in range(2):
        if rows % 8 == 0:
            b0[p] = got[:, p].reshape(nxy, nxy)
        else:
            for s in range(n):
                b0[p, s * rows:(s + 1) * rows, :] = got[s, p]
    for p in range(2):
        v1[p] = v1[p] + wt0[p] * b0[p]
    recv = launch(v1.at[0], v1.at[1], halo0.at[1], big_send, big_recv, V1)
    recv_gk = relay(gk, 1)
    recv_e1()
    sz1 = sx1 = 4.0
    fx1, fy1, total1 = plane_faces(e1, sx1)
    fz1lo = face(jnp.where(has_lo, halo1[E1, 0], e1), e1, sz1)
    fz1hi = face(jnp.where(has_hi, halo1[E1, 1], e1), e1, sz1)
    dg1 = total1 + fz1lo + fz1hi + k1
    wt1 = DAMPING / dg1

    recv()
    v2[0] = sweep0(0, v1[0], halo0[1, 0], v1[1])
    v2[1] = sweep0(1, v1[1], v1[0], halo0[1, 1])
    term1[0] = 0.125 * dot(left0, times(fz0[0] * v2[0], right0))
    term1[1] = 0.125 * dot(left0, times(fz0[2] * v2[1], right0))
    recv_term = launch(term1.at[0], term1.at[1], halo1.at[TERM], small_send, small_recv, TERM)
    recv_v2 = launch(v2.at[0], v2.at[1], halo0.at[2], big_send, big_recv, V2)
    r0 = b0[0] - dg0[0] * v2[0] + plane_sum(fx0[0], fy0[0], v2[0]) + fz0[1] * v2[1]
    r1 = b0[1] - dg0[1] * v2[1] + plane_sum(fx0[1], fy0[1], v2[1]) + fz0[1] * v2[0]
    b1 = down0(r0, r1)
    recv_far = launch(regions.at[1], regions.at[0], far_reg, big_send, big_recv, FAR)
    recv_gk()
    e2 = 0.5 * (gk[0] + gk[1]).reshape(n // 2 * quarter, LANES)
    k2 = back(e2, 1, LANES // 2)
    coarse = coarse_cycle(e2, k2, n // 2, quarter, 16.0, 16.0, dot, times)
    recv_term()
    b1 = b1 + halo1[TERM, 0] + halo1[TERM, 1]

    def beside1(mine, i):
        return plane_sum(fx1, fy1, mine) + fz1lo * halo1[i, 0] + fz1hi * halo1[i, 1]

    def trade1(value, i):
        plane1[i] = value
        launch(plane1.at[i], plane1.at[i], halo1.at[i], small_send, small_recv, i)()

    a = wt1 * b1
    trade1(a, A1)
    a = (1.0 - DAMPING) * a + wt1 * (b1 + beside1(a, A1))
    trade1(a, A2)
    full = down1(b1 - dg1 * a + beside1(a, A2))
    gb[core, chip] = full[:quarter // 2] + back(full[quarter // 2:], 1, LANES // 2)
    share(gb, 2)
    recv_v2()
    base[0] = sweep0(0, v2[0], halo0[2, 0], v2[1])
    base[1] = sweep0(1, v2[1], v2[0], halo0[2, 1])
    recv_base = launch(base.at[0], base.at[1], halo0.at[3], big_send, big_recv, BASE)
    relay_gb = relay(gb, 2)
    recv_far()
    for p in range(2):
        region = halo_reg[p]
        beyond = face(e_side[p], dielectric(far_reg[p]), 1.0)
        fx, fy, total = plane_faces(e_side[p], 1.0)
        fxh[p] = fx
        fyh[p] = fy
        fzh[p] = beyond
        wth[p] = DAMPING / (total + beyond + fz0[2 * p] + jnp.where(region == 2, SCREEN, 0.0))
    relay_gb()
    packed = 0.5 * (gb[0] + gb[1]).reshape(n // 2 * quarter // 2, LANES)
    split = (n // 2, quarter // 2, LANES)
    b2 = jnp.concatenate(
        [packed.reshape(split), back(packed, 1, LANES // 2).reshape(split)], axis=1
    ).reshape(n // 2 * quarter, LANES)
    c2 = coarse(b2)

    for i in range(n // 2):
        c2_planes[i] = c2[i * quarter:(i + 1) * quarter]
    grow_l, grow_r = spread_left(half, quarter), spread_right(LANES, half, half)

    def up1(index):
        return dot(grow_l, times(c2_planes[index // 2], grow_r))

    halo1[A2, 0] = halo1[A2, 0] + jnp.where(has_lo, up1(jnp.maximum(me - 1, 0)), 0.0)
    halo1[A2, 1] = halo1[A2, 1] + jnp.where(has_hi, up1(jnp.minimum(me + 1, n - 1)), 0.0)
    a = a + up1(me)
    a = (1.0 - DAMPING) * a + wt1 * (b1 + beside1(a, A2))
    trade1(a, A3)
    a = (1.0 - DAMPING) * a + wt1 * (b1 + beside1(a, A3))
    trade1(a, A4)

    big_l, big_r = spread_left(nxy, half), spread_right(half, nxy, nxy)

    def up0(c):
        return dot(big_l, times(c, big_r))

    mine = up0(a)
    recv_base()
    v3, side = [], []
    present = [has_lo, has_hi]
    for p in range(2):
        c = up0(halo1[A4, p])
        own = plane_sum(fx0[p], fy0[p], mine) + fz0[1] * mine + fz0[2 * p] * c
        v3.append(base[p] + (1.0 - DAMPING) * mine + wt0[p] * own)
        other = plane_sum(fxh[p], fyh[p], c) + fzh[p] * c + fz0[2 * p] * mine
        swept = halo0[3, p] + (1.0 - DAMPING) * c + wth[p] * other
        side.append(jnp.where(present[p], swept, 0.0))
    out[0] = sweep0(0, v3[0], side[0], v3[1])
    out[1] = sweep0(1, v3[1], v3[0], side[1])

    for sent in pending:
        sent()
    all_in(got, many_send, 0)


HALO = 16
REG_LO, REG_HI, V0_LO, V0_HI, V1_LO, V1_HI, V2_LO, V2_HI, BASE_LO, BASE_HI = range(10)
E_M1, E_P1, E_M2, E_P2, K_M1, K_P1, B_M1, B_P1, B_M2, B_P2, A2_LO, A2_HI, NEAR, NEAR_CORE, FAR_LO, FAR_HI = range(10, 26)
MESSAGES = 26


def box_kernel(n, partials, regions, previous, out,
               parts, dens, reg, v0, b0, fx0, fy0, fz0, dg0, wt0, v1, v2, base, swept,
               near, fxn, fyn, fzn, wtn, landed, corr,
               e1, k1, fx1, fy1, fz1, dg1, wt1, pack, from_lo, from_hi, far_lo, far_hi,
               b1, a1, a2, a2c, a3, a4, gk, gb, c2_planes, rows_tmp,
               load_sem, spread_send, spread_recv, corr_send, corr_recv, dens_send, dens_recv,
               side_send, side_recv, many_send, many_recv):
    me = lax.axis_index("slab")
    nz = n // 2
    z, x, core = me // 4, lax.rem(me // 2, 2), lax.rem(me, 2)
    zi = 2 * z + core
    nxy = regions.shape[1]
    half, quarter = nxy // 2, nxy // 4
    rows = partials.shape[2]
    window = half + HALO
    window1 = window // 2
    blocks = window // rows
    first = half - HALO

    def peer(index):
        return {"slab": index}

    def at(i, j):
        return (i // 2) * 4 + j * 2 + lax.rem(i, 2)

    load = pltpu.make_async_copy(partials, parts, load_sem.at[0])
    load.start()
    load_near = pltpu.make_async_copy(regions, near.at[pl.ds(2, 2)], load_sem.at[1])
    load_near.start()
    barrier = pltpu.get_barrier_semaphore()

    def greet(off, carry):
        pl.semaphore_signal(barrier, inc=1, device_id=peer(lax.rem(me + off, n)),
                            device_id_type=pl.DeviceIdType.MESH)
        return carry

    lax.fori_loop(1, n, greet, 0)

    plane0 = jnp.zeros((window, nxy), F32)
    plane1 = jnp.zeros((window1, half), F32)

    @pl.when(zi == 0)
    def _():
        for i in range(2):
            reg[i] = jnp.zeros((window, nxy), jnp.int32)
        for v in (v0, v1, v2, base):
            v[0] = plane0
        for i in range(3):
            from_lo[i] = plane1
        for i in range(2):
            e1[i] = plane1 + 1.0
            k1[i] = plane1
        a2[0] = plane1

    @pl.when(zi == nz - 1)
    def _():
        for i in range(2):
            reg[6 + i] = jnp.zeros((window, nxy), jnp.int32)
        for v in (v0, v1, v2, base):
            v[5] = plane0
        for i in range(3):
            from_hi[i] = plane1
        for i in range(2):
            e1[6 + i] = plane1 + 1.0
            k1[4 + i] = plane1
        a2[5] = plane1

    @pl.when(zi < 2)
    def _():
        far_lo[0] = plane1

    @pl.when(zi >= nz - 2)
    def _():
        far_hi[0] = plane1

    @pl.when(me == 0)
    def _():
        corr[0] = jnp.zeros((half, half), F32)

    @pl.when(me == n - 1)
    def _():
        corr[2] = jnp.zeros((half, half), F32)

    load.wait()
    density = parts[0].astype(F32)
    for g in range(1, partials.shape[0]):
        density = density + parts[g].astype(F32)
    dens[...] = (SOURCE * density).reshape(dens.shape)

    pl.semaphore_wait(barrier, n - 1)
    pending = []

    def spread(src, dst, low, i):
        for j in range(2):
            target = at(2 * z + x, j)
            piece = src.at[:, pl.ds(first * j, window), :]
            place = dst.at[pl.ds(low + 2 * core, 2)]
            remote = pltpu.make_async_remote_copy(
                src_ref=piece, dst_ref=place, send_sem=spread_send.at[i, j],
                recv_sem=spread_recv.at[i, core], device_id=peer(target),
                device_id_type=pl.DeviceIdType.MESH)
            here = pltpu.make_async_copy(piece, place, spread_recv.at[i, core])
            away = target != me
            pl.when(away)(remote.start)
            pl.when(jnp.logical_not(away))(here.start)
            pending.append(lambda remote=remote, away=away: pl.when(away)(remote.wait_send))

        def arrived():
            for j in range(2):
                place = dst.at[pl.ds(low + 2 * j, 2)]
                pltpu.make_async_copy(place, place, spread_recv.at[i, j]).wait()

        return arrived

    def send_density(step, carry):
        other = lax.rem(me + 1 + lax.rem(step + n // 2 - 1, n), n)
        oz, ox = 2 * (other // 4) + lax.rem(other, 2), lax.rem(other // 2, 2)
        block = me - (first // rows) * ox
        inside = (block >= 0) & (block < blocks)
        block = jnp.clip(block, 0, blocks - 1)
        place = b0.at[:, pl.ds(pl.multiple_of(block * rows, rows), rows), :]

        @pl.when(inside & (other != me))
        def _():
            pltpu.make_async_remote_copy(
                src_ref=dens.at[oz], dst_ref=place, send_sem=dens_send.at[other],
                recv_sem=dens_recv.at[0], device_id=peer(other),
                device_id_type=pl.DeviceIdType.MESH).start()

        @pl.when(inside & (other == me))
        def _():
            pltpu.make_async_copy(dens.at[oz], place, dens_recv.at[0]).start()

        return carry

    def sent_density(other, carry):
        ox = lax.rem(other // 2, 2)
        block = me - (first // rows) * ox

        @pl.when((block >= 0) & (block < blocks) & (other != me))
        def _():
            pltpu.make_async_copy(dens.at[0], dens.at[0], dens_send.at[other]).wait()

        return carry

    def push(src, dst, delta, i):
        can_send = (zi + delta >= 0) & (zi + delta < nz)
        can_recv = (zi - delta >= 0) & (zi - delta < nz)
        copy = pltpu.make_async_remote_copy(
            src_ref=src, dst_ref=dst, send_sem=side_send.at[i], recv_sem=side_recv.at[i],
            device_id=peer(at(jnp.clip(zi + delta, 0, nz - 1), x)),
            device_id_type=pl.DeviceIdType.MESH)
        pl.when(can_send)(copy.start)
        pending.append(lambda: pl.when(can_send)(copy.wait_send))
        return lambda: pl.when(can_recv)(copy.wait_recv)

    def trade(field, low, high, i):
        down = push(field.at[low], field.at[high + 1], -1, i)
        up = push(field.at[high], field.at[low - 1], 1, i + 1)

        def arrived():
            down()
            up()

        return arrived

    reg_in = spread(regions, reg, 2, 0)
    v0_in = spread(previous, v0, 1, 1)
    lax.fori_loop(0, n, send_density, 0)

    def dielectric(r):
        return jnp.where(r == 0, INSIDE, SOLVENT).astype(F32)

    right0 = pool_right(nxy, half, nxy)
    right1 = pool_right(half, LANES, half)
    dst1, src1 = iota((quarter // 2, window1), 0), iota((quarter // 2, window1), 1)
    left1 = jnp.where((src1 - (HALO // 2) * x) // 2 == dst1, 1.0, 0.0).astype(F32)

    turn = [0]

    def strips(v):
        return [v[:, i:i + LANES] for i in range(0, v.shape[1], LANES)]

    def scratch():
        turn[0] = (turn[0] + 1) % 8
        return rows_tmp.at[turn[0]]

    def pool_rows(v):
        count = v.shape[0] // 2
        done = []
        for strip in strips(v):
            tmp = scratch()
            tmp[:2 * count] = strip
            done.append(tmp[pl.ds(0, count, stride=2), :] + tmp[pl.ds(1, count, stride=2), :])
        return done[0] if len(done) == 1 else jnp.concatenate(done, axis=1)

    def grow_rows(v):
        count = v.shape[0]
        done = []
        for strip in strips(v):
            tmp = scratch()
            tmp[pl.ds(0, count, stride=2), :] = strip
            tmp[pl.ds(1, count, stride=2), :] = strip
            done.append(tmp[:2 * count])
        return done[0] if len(done) == 1 else jnp.concatenate(done, axis=1)

    def down0(a):
        return 0.125 * times2(pool_rows(a), right0)

    def down1(a):
        return 0.125 * dot2(left1, times2(a, right1))

    reg_in()
    reg_halo = trade(reg, 2, 5, REG_LO)
    e = [dielectric(reg[p]) for p in range(2, 6)]
    k = [jnp.where(reg[p] == 2, SCREEN, 0.0).astype(F32) for p in range(2, 6)]
    for i in range(2):
        e1[3 + i] = down0(e[2 * i] + e[2 * i + 1])
        k1[2 + i] = down0(k[2 * i] + k[2 * i + 1])
    e1_in = [push(e1.at[pl.ds(3, 2)], e1.at[pl.ds(1, 2)], 1, E_P1),
             push(e1.at[pl.ds(3, 2)], e1.at[pl.ds(5, 2)], -1, E_M1),
             push(e1.at[pl.ds(4, 1)], e1.at[pl.ds(0, 1)], 2, E_P2),
             push(e1.at[pl.ds(3, 1)], e1.at[pl.ds(7, 1)], -2, E_M2),
             push(k1.at[pl.ds(2, 2)], k1.at[pl.ds(0, 2)], 1, K_P1),
             push(k1.at[pl.ds(2, 2)], k1.at[pl.ds(4, 2)], -1, K_M1)]
    chip = me // 2
    gk[core, x, z] = down1(e1[3] + e1[4]) + back(down1(k1[2] + k1[3]), 1, LANES // 2)

    def share(ref, i):
        def one(off, carry):
            other = lax.rem(me + 2 * off, n)
            pltpu.make_async_remote_copy(
                src_ref=ref.at[core, chip], dst_ref=ref.at[core, chip], send_sem=many_send.at[i],
                recv_sem=many_recv.at[i], device_id=peer(other),
                device_id_type=pl.DeviceIdType.MESH).start()
            return carry

        lax.fori_loop(1, n // 2, one, 0)

    def relay(ref, i):
        seven = ref.at[0, pl.ds(0, n // 2 - 1)]
        pltpu.make_async_copy(seven, seven, many_recv.at[i]).wait()
        copy = pltpu.make_async_remote_copy(
            src_ref=ref.at[core], dst_ref=ref.at[core], send_sem=many_send.at[i + 2],
            recv_sem=many_recv.at[i + 2], device_id=peer(me + 1 - 2 * core),
            device_id_type=pl.DeviceIdType.MESH)
        copy.start()
        pending.append(pltpu.make_async_copy(seven, seven, many_send.at[i]).wait)
        pending.append(copy.wait_send)
        return copy.wait_recv

    def in_order(ref):
        return [ref[c, 2 * i + j] for i in range(n // 4) for c in range(2) for j in range(2)]

    columns = n // 4

    def along(off, carry):
        other = lax.rem(me + 4 * off, n)
        pltpu.make_async_remote_copy(
            src_ref=gk.at[core, x, z], dst_ref=gk.at[core, x, z], send_sem=many_send.at[0],
            recv_sem=many_recv.at[0], device_id=peer(other),
            device_id_type=pl.DeviceIdType.MESH).start()
        return carry

    lax.fori_loop(1, columns, along, 0)

    def gk_over():
        others = gk.at[0, 0, pl.ds(0, columns - 1)]
        pltpu.make_async_copy(others, others, many_recv.at[0]).wait()
        copy = pltpu.make_async_remote_copy(
            src_ref=gk.at[core, x], dst_ref=gk.at[core, x], send_sem=many_send.at[4],
            recv_sem=many_recv.at[4], device_id=peer(at(zi, 1 - x)),
            device_id_type=pl.DeviceIdType.MESH)
        copy.start()
        pending.append(pltpu.make_async_copy(others, others, many_send.at[0]).wait)
        pending.append(copy.wait_send)
        return copy.wait_recv

    def gk_beside():
        copy = pltpu.make_async_remote_copy(
            src_ref=gk.at[core], dst_ref=gk.at[core], send_sem=many_send.at[2],
            recv_sem=many_recv.at[2], device_id=peer(at(zi + 1 - 2 * core, x)),
            device_id_type=pl.DeviceIdType.MESH)
        copy.start()
        pending.append(copy.wait_send)
        return copy.wait_recv

    totals = []
    for p in range(4):
        fx, fy, total = plane_faces(e[p], 1.0)
        fx0[p] = fx
        fy0[p] = fy
        totals.append(total + k[p])
    for p in range(1, 4):
        fz0[p] = face(e[p - 1], e[p], 1.0)
    v0_in()
    v0_halo = trade(v0, 1, 4, V0_LO)
    far_in = [push(reg.at[3], reg.at[7], -1, FAR_LO), push(reg.at[4], reg.at[0], 1, FAR_HI)]

    def beside0(p, v):
        return (plane_sum(fx0[p], fy0[p], v[p + 1]) + fz0[p] * v[p] + fz0[p + 1] * v[p + 2])

    def sweep0(p, v):
        return (1.0 - DAMPING) * v[p + 1] + wt0[p] * (b0[p] + beside0(p, v))

    def first_part(p):
        v1[p + 1] = (1.0 - DAMPING) * v0[p + 1] + wt0[p] * beside0(p, v0)

    def weights(p):
        diag = totals[p] + fz0[p] + fz0[p + 1]
        dg0[p] = diag
        wt0[p] = DAMPING / diag

    for p in (1, 2):
        weights(p)
        first_part(p)
    reg_halo()
    fz0[0] = face(jnp.where(zi > 0, dielectric(reg[1]), e[0]), e[0], 1.0)
    fz0[4] = face(e[3], jnp.where(zi < nz - 1, dielectric(reg[6]), e[3]), 1.0)
    weights(0)
    weights(3)
    v0_halo()
    first_part(0)
    first_part(3)

    pltpu.make_async_copy(b0, b0, dens_recv.at[0]).wait()
    for p in (0, 3):
        v1[p + 1] = v1[p + 1] + wt0[p] * b0[p]
    v1_halo = trade(v1, 1, 4, V1_LO)
    for arrived in far_in:
        arrived()
    own_rows = pl.ds(pl.multiple_of(HALO * x, HALO), half)

    def near_rows(j):
        return near.at[pl.ds(4 * core, 2), pl.ds(pl.multiple_of(half * j, half), half), :]

    across = pltpu.make_async_remote_copy(
        src_ref=reg.at[pl.ds(4 + 2 * core - 4 * x, 2), own_rows, :], dst_ref=near_rows(x),
        send_sem=side_send.at[NEAR], recv_sem=side_recv.at[NEAR], device_id=peer(at(zi, 1 - x)),
        device_id_type=pl.DeviceIdType.MESH)
    beside = pltpu.make_async_remote_copy(
        src_ref=regions, dst_ref=near.at[pl.ds(4 * core, 2)], send_sem=side_send.at[NEAR_CORE],
        recv_sem=side_recv.at[NEAR_CORE], device_id=peer(at(zi + 1 - 2 * core, x)),
        device_id_type=pl.DeviceIdType.MESH)
    within = pltpu.make_async_copy(reg.at[pl.ds(2 * core + 4 * x, 2), own_rows, :], near_rows(x),
                                   load_sem.at[2])
    for copy in (across, beside, within):
        copy.start()
    pending.append(across.wait_send)
    pending.append(beside.wait_send)
    gk_across = gk_over()

    for p in (1, 2):
        v1[p + 1] = v1[p + 1] + wt0[p] * b0[p]

    for p in (1, 2):
        v2[p + 1] = sweep0(p, v1)
    v1_halo()
    for p in (0, 3):
        v2[p + 1] = sweep0(p, v1)
    v2_halo = trade(v2, 1, 4, V2_LO)
    pack[0] = down0(fz0[4] * v2[4])
    pack[3] = down0(fz0[0] * v2[1])

    def left_over(p):
        r = b0[p] - dg0[p] * v2[p + 1] + plane_sum(fx0[p], fy0[p], v2[p + 1])
        if p > 0:
            r = r + fz0[p] * v2[p]
        if p < 3:
            r = r + fz0[p + 1] * v2[p + 2]
        return r

    for i in range(2):
        pack[1 + i] = down0(left_over(2 * i) + left_over(2 * i + 1))
    b1_in = [push(pack.at[pl.ds(0, 3)], from_lo, 1, B_P1),
             push(pack.at[pl.ds(1, 3)], from_hi, -1, B_M1),
             push(pack.at[pl.ds(0, 1)], far_lo, 2, B_P2),
             push(pack.at[pl.ds(3, 1)], far_hi, -2, B_M2)]
    for arrived in e1_in:
        arrived()

    @pl.when(zi == 0)
    def _():
        e1[2] = e1[3]
        e1[0] = plane1 + 1.0

    @pl.when(zi == 1)
    def _():
        e1[0] = e1[1]

    @pl.when(zi == nz - 1)
    def _():
        e1[5] = e1[4]
        e1[7] = plane1 + 1.0

    @pl.when(zi == nz - 2)
    def _():
        e1[7] = e1[6]

    s1 = 4.0
    for i in range(7):
        fz1[i] = face(e1[i], e1[i + 1], s1)
    for i in range(6):
        fx, fy, total = plane_faces(e1[i + 1], s1)
        fx1[i] = fx
        fy1[i] = fy
        diag = total + fz1[i] + fz1[i + 1] + k1[i]
        dg1[i] = diag
        weight = DAMPING / diag
        if i < 2:
            weight = jnp.where(zi > 0, weight, 0.0)
        if i > 3:
            weight = jnp.where(zi < nz - 1, weight, 0.0)
        wt1[i] = weight

    v2_halo()
    for p in (0, 3, 1, 2):
        base[p + 1] = sweep0(p, v2)
    base_halo = trade(base, 1, 4, BASE_LO)
    for arrived in b1_in:
        arrived()
    b1[0] = from_lo[1] + far_lo[0]
    b1[1] = from_lo[2] + pack[3]
    b1[2] = pack[1] + from_lo[0]
    b1[3] = pack[2] + from_hi[2]
    b1[4] = from_hi[0] + pack[0]
    b1[5] = from_hi[1] + far_hi[0]

    def beside1(i, mine, below, above):
        return plane_sum(fx1[i], fy1[i], mine) + fz1[i] * below + fz1[i + 1] * above

    def sweep1(i, mine, below, above):
        return (1.0 - DAMPING) * mine + wt1[i] * (b1[i] + beside1(i, mine, below, above))

    for i in range(6):
        a1[i] = wt1[i] * b1[i]
    for i in range(1, 5):
        a2[i] = sweep1(i, a1[i], a1[i - 1], a1[i + 1])
    rest = [b1[i] - dg1[i] * a2[i] + beside1(i, a2[i], a2[i - 1], a2[i + 1]) for i in (2, 3)]
    full = down1(rest[0] + rest[1])
    gb[core, chip] = full[:quarter // 4] + back(full[quarter // 4:], 1, LANES // 2)
    share(gb, 1)
    a2_in = [push(a2.at[2], a2.at[0], 1, A2_HI), push(a2.at[3], a2.at[5], -1, A2_LO)]
    gk_across()
    gk_in = gk_beside()
    gk_in()
    e2 = jnp.concatenate([gk[i, j, m] for m in range(n // 4) for i in range(2) for j in range(2)], axis=0)
    coarse = coarse_cycle(e2, back(e2, 1, LANES // 2), nz, quarter, 16.0, 16.0,
                          dot2, times2, (pool_rows, grow_rows))
    base_halo()

    def deliver(j):
        target = 4 * z + 2 * core + j
        piece = swept.at[pl.ds(2 * j, 2), pl.ds(pl.multiple_of(HALO * x, HALO), half), :]
        place = landed.at[:, pl.ds(pl.multiple_of(half * x, half), half), :]
        remote = pltpu.make_async_remote_copy(
            src_ref=piece, dst_ref=place, send_sem=spread_send.at[2, j],
            recv_sem=spread_recv.at[2, x], device_id=peer(target),
            device_id_type=pl.DeviceIdType.MESH)
        here = pltpu.make_async_copy(piece, place, spread_recv.at[2, x])
        away = target != me
        pl.when(away)(remote.start)
        pl.when(jnp.logical_not(away))(here.start)
        pending.append(lambda: pl.when(away)(remote.wait_send))

    for p in range(4):
        swept[p] = sweep0(p, base)
        if p % 2:
            deliver(p // 2)
    gb_in = relay(gb, 1)
    gb_in()
    packed = jnp.stack(in_order(gb))
    b2 = jnp.concatenate([packed, back(packed.reshape(-1, LANES), 1, LANES // 2).reshape(packed.shape)],
                         axis=1).reshape(nz * quarter, LANES)
    c2 = coarse(b2)
    for i in range(nz):
        c2_planes[i] = c2[i * quarter:(i + 1) * quarter]
    fine, mid = iota((window1, quarter), 0), iota((window1, quarter), 1)
    grow_l = jnp.where((fine + first // 2 * x) // 2 == mid, 1.0, 0.0).astype(F32)
    grow_r = spread_right(LANES, half, half)

    def up1(index):
        return dot2(grow_l, times2(c2_planes[index], grow_r))


    for arrived in a2_in:
        arrived()
    mine = up1(zi)
    lower = jnp.where(zi > 0, up1(jnp.maximum(zi - 1, 0)), 0.0)
    upper = jnp.where(zi < nz - 1, up1(jnp.minimum(zi + 1, nz - 1)), 0.0)
    for i, c in enumerate((lower, lower, mine, mine, upper, upper)):
        a2c[i] = a2[i] + c
    for i in range(1, 5):
        a3[i - 1] = sweep1(i, a2c[i], a2c[i - 1], a2c[i + 1])
    for i in (1, 2):
        a4[i] = sweep1(i + 1, a3[i], a3[i - 1], a3[i + 1])

    def hand(count, low, delta, slot, i):
        target = 2 * zi + delta
        exists = (target >= 0) & (target < n)
        piece = a4.at[pl.ds(low, count), pl.ds(pl.multiple_of(HALO // 2 * x, HALO // 2), quarter), :]
        place = corr.at[pl.ds(slot, count), pl.ds(pl.multiple_of(quarter * x, quarter), quarter), :]
        kind = 2 - count
        remote = pltpu.make_async_remote_copy(
            src_ref=piece, dst_ref=place, send_sem=corr_send.at[i], recv_sem=corr_recv.at[kind, x],
            device_id=peer(jnp.clip(target, 0, n - 1)), device_id_type=pl.DeviceIdType.MESH)
        here = pltpu.make_async_copy(piece, place, corr_recv.at[kind, x])
        away = exists & (target != me)
        pl.when(away)(remote.start)
        pl.when(target == me)(here.start)
        pending.append(lambda: pl.when(away)(remote.wait_send))

    hand(2, 1, 0, 1, 0)
    hand(2, 1, 1, 0, 1)
    hand(1, 1, -1, 2, 2)
    hand(1, 2, 2, 0, 3)
    big_l, big_r = spread_left(nxy, half), spread_right(half, nxy, nxy)

    def up0(c):
        return dot2(big_l, times2(c, big_r))

    load_near.wait()
    within.wait()
    across.wait_recv()
    beside.wait_recv()
    en = [dielectric(near[f]) for f in range(6)]
    fzn[0] = face(en[0], en[1], 1.0)
    fzn[1] = face(jnp.where(me > 0, en[1], en[2]), en[2], 1.0)
    fzn[2] = face(en[2], en[3], 1.0)
    fzn[3] = face(en[3], jnp.where(me < n - 1, en[4], en[3]), 1.0)
    fzn[4] = face(en[4], en[5], 1.0)
    for f in range(4):
        fx, fy, total = plane_faces(en[f + 1], 1.0)
        fxn[f] = fx
        fyn[f] = fy
        kn = jnp.where(near[f + 1] == 2, SCREEN, 0.0).astype(F32)
        wtn[f] = DAMPING / (total + kn + fzn[f] + fzn[f + 1])
    for sent in pending:
        sent()
    lax.fori_loop(0, n, sent_density, 0)
    single = jnp.where(lax.rem(me, 2) == 0, me > 0, me < n - 1)
    for j in range(2):
        both = corr.at[pl.ds(0, 2), pl.ds(quarter * j, quarter), :]
        pltpu.make_async_copy(both, both, corr_recv.at[0, j]).wait()
        one = corr.at[pl.ds(0, 1), pl.ds(quarter * j, quarter), :]
        pl.when(single)(pltpu.make_async_copy(one, one, corr_recv.at[1, j]).wait)
    for j in range(2):
        place = landed.at[:, pl.ds(half * j, half), :]
        pltpu.make_async_copy(place, place, spread_recv.at[2, j]).wait()
    below, here, above = (up0(corr[i]) for i in range(3))
    spans = [(below, below, here), (here, below, here), (here, here, above), (above, here, above)]

    def relax(f, mine, low, high):
        return (1.0 - DAMPING) * mine + wtn[f] * (
            plane_sum(fxn[f], fyn[f], mine) + fzn[f] * low + fzn[f + 1] * high)

    y = [relax(f, *spans[f]) for f in range(4)]
    y[0] = jnp.where(me > 0, y[0], 0.0)
    y[3] = jnp.where(me < n - 1, y[3], 0.0)
    for f in (1, 2):
        out[f - 1] = landed[f - 1] + relax(f, y[f], y[f - 1], y[f + 1])


def box_local(partials, regions, previous):
    n = lax.axis_size("slab")
    nxy = regions.shape[1]
    half, quarter = nxy // 2, nxy // 4
    rows = partials.shape[2]
    window, window1 = half + HALO, (half + HALO) // 2
    vmem = lambda *shape: pltpu.VMEM(shape, F32)
    big = lambda count: vmem(count, window, nxy)
    small = lambda count: vmem(count, window1, half)
    return pl.pallas_call(
        functools.partial(box_kernel, n),
        out_shape=pltpu.VMEM(previous.shape, F32),
        in_specs=[pl.BlockSpec(memory_space=pltpu.HBM)] * 3,
        out_specs=pl.BlockSpec(memory_space=pltpu.VMEM),
        scratch_shapes=[
            pltpu.VMEM(partials.shape, partials.dtype), vmem(n // 2, 4, rows, nxy),
            pltpu.VMEM((8, window, nxy), jnp.int32), big(6), big(4),
            big(4), big(4), big(5), big(4), big(4), big(6), big(6), big(6), big(4),
            pltpu.VMEM((6, nxy, nxy), jnp.int32), vmem(4, nxy, nxy), vmem(4, nxy, nxy),
            vmem(5, nxy, nxy), vmem(4, nxy, nxy), vmem(2, nxy, nxy), vmem(3, half, half),
            small(8), small(6), small(6), small(6), small(7), small(6), small(6),
            small(4), small(3), small(3), small(1), small(1),
            small(6), small(6), small(6), small(6), small(4), small(4),
            vmem(2, 2, n // 4, quarter // 2, LANES), vmem(2, n // 2, quarter // 4, LANES),
            vmem(n // 2, quarter, LANES), vmem(8, 2 * nxy, LANES),
            pltpu.SemaphoreType.DMA((3,)),
            pltpu.SemaphoreType.DMA((3, 2)), pltpu.SemaphoreType.DMA((3, 2)),
            pltpu.SemaphoreType.DMA((4,)), pltpu.SemaphoreType.DMA((2, 2)),
            pltpu.SemaphoreType.DMA((n,)), pltpu.SemaphoreType.DMA((1,)),
            pltpu.SemaphoreType.DMA((MESSAGES,)), pltpu.SemaphoreType.DMA((MESSAGES,)),
            pltpu.SemaphoreType.DMA((5,)), pltpu.SemaphoreType.DMA((5,)),
        ],
        compiler_params=pltpu.CompilerParams(
            collective_id=1, has_side_effects=True, vmem_limit_bytes=60 * 1024 * 1024),
    )(partials, regions, previous)


def local(partials, regions, previous):
    n = lax.axis_size("slab")
    nxy = regions.shape[1]
    half, quarter = nxy // 2, nxy // 4
    rows = partials.shape[2]
    vmem = lambda *shape: pltpu.VMEM(shape, F32)
    spec = pl.BlockSpec(memory_space=pltpu.VMEM)
    return pl.pallas_call(
        functools.partial(kernel, n),
        out_shape=jax.ShapeDtypeStruct(previous.shape, F32),
        in_specs=[spec] * 3,
        out_specs=spec,
        scratch_shapes=[
            vmem(n, 2, rows, nxy), vmem(n, 2, rows, nxy), vmem(2, nxy, nxy),
            vmem(2, nxy, nxy), vmem(2, nxy, nxy), vmem(3, nxy, nxy), vmem(2, nxy, nxy),
            vmem(2, nxy, nxy),
            pltpu.VMEM((2, nxy, nxy), jnp.int32), pltpu.VMEM((2, nxy, nxy), jnp.int32),
            vmem(2, nxy, nxy), vmem(2, nxy, nxy), vmem(2, nxy, nxy), vmem(2, nxy, nxy),
            vmem(4, 2, nxy, nxy),
            vmem(2, nxy, nxy), vmem(2, nxy, nxy), vmem(2, nxy, nxy),
            vmem(6, 2, half, half), vmem(5, half, half), vmem(2, half, half),
            vmem(2, n // 2, quarter // 2, LANES), vmem(2, n // 2, quarter, LANES),
            pltpu.SemaphoreType.DMA((6, 2)), pltpu.SemaphoreType.DMA((6, 2)),
            pltpu.SemaphoreType.DMA((6, 2)), pltpu.SemaphoreType.DMA((6, 2)),
            pltpu.SemaphoreType.DMA((5,)), pltpu.SemaphoreType.DMA((5,)),
            vmem(n // 2, quarter, LANES),
        ],
        compiler_params=pltpu.CompilerParams(
            collective_id=0, has_side_effects=True, vmem_limit_bytes=60 * 1024 * 1024),
    )(partials, regions, previous)


def solution(mesh):
    in_specs = (
        P("job", None, "slab", None),
        P(("job", "slab"), None, None),
        P(("job", "slab"), None, None),
    )
    out_specs = P(("job", "slab"), None, None)
    size = mesh.shape["slab"]

    def fits(partials, regions):
        return (size == 16 and partials.shape[2] == 16 * size and partials.shape[1] == 2 * size
                and regions.shape[1] == 16 * size)

    def program(partials, regions, previous):
        chosen = box_local if fits(partials, regions) else local
        return jax.shard_map(chosen, mesh=mesh, in_specs=in_specs, out_specs=out_specs, check_vma=False)(
            partials, regions, previous)

    return program
```

```python
import functools

import jax
import jax.numpy as jnp
from jax import lax
from jax.experimental import pallas as pl
from jax.experimental.pallas import tpu as pltpu
from jax.sharding import PartitionSpec as P

PRE_SWEEPS = 2
POST_SWEEPS = 2
COARSE_SWEEPS = 4

DAMPING = 0.75
INSIDE = 2.0
SOLVENT = 78.4
SCREEN = 1.4
SOURCE = 16.0 * 3.141592653589793

F32 = jnp.float32
LANES = 128


def iota(shape, dim):
    return lax.broadcasted_iota(jnp.int32, shape, dim)


def face(mine, other, spacing):
    return mine * other / ((mine + other) * (0.5 * spacing))


def back(v, dim, by=1):
    return pltpu.roll(v, by, dim)


def ahead(v, dim, by=1):
    return pltpu.roll(v, v.shape[dim] - by, dim)


def terms(v):
    result = []
    for _ in range(3):
        result.append(v.astype(jnp.bfloat16))
        v = v - result[-1].astype(F32)
    return result


def product(a, b):
    return lax.dot_general(a, b, (((1,), (0,)), ((), ())), preferred_element_type=F32)


def times(v, selector):
    high, middle, low = (product(t, selector.astype(jnp.bfloat16)) for t in terms(v))
    return high + (middle + low)


def dot(selector, v):
    high, middle, low = (product(selector.astype(jnp.bfloat16), t) for t in terms(v))
    return high + (middle + low)


def halves(v):
    high = v.astype(jnp.bfloat16)
    return high, (v - high.astype(F32)).astype(jnp.bfloat16)


def times2(v, selector):
    high, low = (product(t, selector.astype(jnp.bfloat16)) for t in halves(v))
    return high + low


def dot2(selector, v):
    high, low = (product(selector.astype(jnp.bfloat16), t) for t in halves(v))
    return high + low


def pool_right(wide, narrow, valid):
    src, dst = iota((wide, narrow), 0), iota((wide, narrow), 1)
    return jnp.where((src // 2 == dst) & (src < valid), 1.0, 0.0).astype(F32)


def pool_left(narrow, wide):
    dst, src = iota((narrow, wide), 0), iota((narrow, wide), 1)
    return jnp.where(src // 2 == dst, 1.0, 0.0).astype(F32)


def spread_right(narrow, wide, valid):
    src, dst = iota((narrow, wide), 0), iota((narrow, wide), 1)
    return jnp.where((dst // 2 == src) & (dst < valid), 1.0, 0.0).astype(F32)


def spread_left(wide, narrow):
    dst, src = iota((wide, narrow), 0), iota((wide, narrow), 1)
    return jnp.where(dst // 2 == src, 1.0, 0.0).astype(F32)


def plane_faces(e, spacing):
    rows, cols = e.shape
    x, y = iota(e.shape, 0), iota(e.shape, 1)
    fx = jnp.where(x > 0, face(e, back(e, 0), spacing), 0.0)
    fy = jnp.where(y > 0, face(e, back(e, 1), spacing), 0.0)
    edges = (jnp.where((x == 0) | (x == rows - 1), 1.0, 0.0)
             + jnp.where((y == 0) | (y == cols - 1), 1.0, 0.0))
    total = fx + ahead(fx, 0) + fy + ahead(fy, 1) + edges * e * (1.0 / spacing)
    return fx, fy, total


def plane_sum(fx, fy, v):
    return fx * back(v, 0) + ahead(fx * v, 0) + fy * back(v, 1) + ahead(fy * v, 1)


def coarse_cycle(e, k, planes, nx, sz, sx, dot, times, pairs=None):
    rows = e.shape[0]
    row, lane = iota(e.shape, 0), iota(e.shape, 1)
    x, z = row % nx, row // nx
    valid = (row < planes * nx) & (lane < nx)
    e = jnp.where(valid, e, 1.0)
    fx = jnp.where(valid & (x > 0), face(e, back(e, 0), sx), 0.0) if nx > 1 else None
    fy = jnp.where(valid & (lane > 0), face(e, back(e, 1), sx), 0.0) if nx > 1 else None
    wrap = nx % rows
    fz = jnp.where(valid & (z > 0), face(e, back(e, 0, wrap), sz), 0.0) if planes > 1 else None
    diag = k + e * (
        (jnp.where(x == 0, 1.0, 0.0) + jnp.where(x == nx - 1, 1.0, 0.0)
         + jnp.where(lane == 0, 1.0, 0.0) + jnp.where(lane == nx - 1, 1.0, 0.0)) * (1.0 / sx)
        + (jnp.where(z == 0, 1.0, 0.0) + jnp.where(z == planes - 1, 1.0, 0.0)) * (1.0 / sz))
    if nx > 1:
        diag = diag + fx + ahead(fx, 0) + fy + ahead(fy, 1)
    if planes > 1:
        diag = diag + fz + ahead(fz, 0, wrap)
    w = jnp.where(valid, DAMPING / jnp.where(valid, diag, 1.0), 0.0)

    def beside(v):
        total = jnp.zeros_like(v)
        if nx > 1:
            total = plane_sum(fx, fy, v)
        if planes > 1:
            total = total + fz * back(v, 0, wrap) + ahead(fz * v, 0, wrap)
        return total

    def sweep(v, b):
        return (1.0 - DAMPING) * v + w * (b + beside(v))

    def coarsest(b):
        v = w * b
        for _ in range(COARSE_SWEEPS - 1):
            v = sweep(v, b)
        return v

    if planes == 1:
        return coarsest
    halve = nx > 1 and nx % 2 == 0
    nx2 = nx // 2 if halve else nx
    sx2 = sx * 4.0 if halve else sx
    step = planes
    while step * nx > 512 and step % 4 == 0:
        step //= 2
    part = step * nx
    if step == planes:
        part = rows
    real2 = planes // 2 * nx2
    rows2 = max(8, real2)
    part2 = rows2 if step == planes else step // 2 * nx2
    ratio = 2 if halve else 1

    def member(fine, coarse):
        return ((fine < step * nx) & ((fine // nx // 2) * nx2 + fine % nx // ratio == coarse))

    down = jnp.where(member(iota((part2, part), 1), iota((part2, part), 0)), 1.0, 0.0)
    up = jnp.where(member(iota((part, part2), 0), iota((part, part2), 1)), 1.0, 0.0)
    if halve:
        right = pool_right(LANES, LANES, nx)
        left = spread_right(LANES, LANES, nx)
        scale = 0.125
    else:
        scale = 0.5

    def coarsen(f):
        if pairs is not None:
            f = jnp.sum(f.reshape(planes // 2, 2, nx, LANES), axis=1).reshape(planes // 2 * nx, LANES)
            return scale * times(pairs[0](f), right)
        if halve:
            f = times(f, right)
        parts = [dot(down, f[i:i + part]) for i in range(0, rows, part)]
        return scale * (parts[0] if len(parts) == 1 else jnp.concatenate(parts, axis=0))

    def refine(f):
        if pairs is not None:
            f = pairs[1](times(f, left)).reshape(planes // 2, 1, nx, LANES)
            return jnp.broadcast_to(f, (planes // 2, 2, nx, LANES)).reshape(planes * nx, LANES)
        if halve:
            f = times(f, left)
        parts = [dot(up, f[i:i + part2]) for i in range(0, rows2, part2)]
        return parts[0] if len(parts) == 1 else jnp.concatenate(parts, axis=0)

    below = coarse_cycle(coarsen(jnp.where(valid, e, 0.0)), coarsen(k),
                         planes // 2, nx2, sz * 4.0, sx2, dot, times, pairs)

    def run(b):
        v = w * b
        for _ in range(PRE_SWEEPS - 1):
            v = sweep(v, b)
        r = jnp.where(valid, b - diag * v + beside(v), 0.0)
        v = v + refine(below(coarsen(r)))
        for _ in range(POST_SWEEPS):
            v = sweep(v, b)
        return v

    return run


REG, V0, V1, V2, BASE, FAR = range(6)
E1, A1, A2, A3, A4, TERM = range(6)


def kernel(n, partials, regions, previous, out,
           dens, got, b0, fx0, fy0, fz0, dg0, wt0, halo_reg, far_reg, fxh, fyh, fzh, wth, halo0, v1, v2, base,
           halo1, plane1, term1, gb, gk,
           big_send, big_recv, small_send, small_recv, many_send, many_recv, c2_planes):
    me = lax.axis_index("slab")
    job = lax.axis_index("job")
    nxy = regions.shape[1]
    half = nxy // 2
    quarter = nxy // 4
    rows = partials.shape[2]
    has_lo, has_hi = me > 0, me < n - 1

    def peer(index):
        return {"slab": index}

    barrier = pltpu.get_barrier_semaphore()

    def greet(off, carry):
        pl.semaphore_signal(barrier, inc=1, device_id=peer(lax.rem(me + off, n)),
                            device_id_type=pl.DeviceIdType.MESH)
        return carry

    lax.fori_loop(1, n, greet, 0)

    @pl.when(jnp.logical_not(has_lo))
    def _():
        for i in range(4):
            halo0[i, 0] = jnp.zeros((nxy, nxy), F32)
        for i in range(6):
            halo1[i, 0] = jnp.zeros((half, half), F32)
        halo_reg[0] = jnp.zeros((nxy, nxy), jnp.int32)
        far_reg[0] = jnp.zeros((nxy, nxy), jnp.int32)

    @pl.when(jnp.logical_not(has_hi))
    def _():
        for i in range(4):
            halo0[i, 1] = jnp.zeros((nxy, nxy), F32)
        for i in range(6):
            halo1[i, 1] = jnp.zeros((half, half), F32)
        halo_reg[1] = jnp.zeros((nxy, nxy), jnp.int32)
        far_reg[1] = jnp.zeros((nxy, nxy), jnp.int32)

    density = partials[0].astype(F32)
    for g in range(1, partials.shape[0]):
        density = density + partials[g].astype(F32)
    dens[...] = (SOURCE * density).reshape(dens.shape)

    pl.semaphore_wait(barrier, n - 1)

    def copies(first, last, dst, sends, recvs, i):
        to_lo = pltpu.make_async_remote_copy(
            src_ref=first, dst_ref=dst.at[1], send_sem=sends.at[i, 0], recv_sem=recvs.at[i, 1],
            device_id=peer(jnp.maximum(me - 1, 0)), device_id_type=pl.DeviceIdType.MESH)
        to_hi = pltpu.make_async_remote_copy(
            src_ref=last, dst_ref=dst.at[0], send_sem=sends.at[i, 1], recv_sem=recvs.at[i, 0],
            device_id=peer(jnp.minimum(me + 1, n - 1)), device_id_type=pl.DeviceIdType.MESH)

        def start():
            pl.when(has_lo)(to_lo.start)
            pl.when(has_hi)(to_hi.start)

        def recv():
            pl.when(has_lo)(to_hi.wait_recv)
            pl.when(has_hi)(to_lo.wait_recv)

        def sent():
            pl.when(has_lo)(to_lo.wait_send)
            pl.when(has_hi)(to_hi.wait_send)

        return start, recv, sent

    pending = []

    def launch(first, last, dst, sends, recvs, i):
        start, recv, sent = copies(first, last, dst, sends, recvs, i)
        start()
        pending.append(sent)
        return recv

    recv_reg = launch(regions.at[0], regions.at[1], halo_reg, big_send, big_recv, REG)
    recv_v0 = launch(previous.at[0], previous.at[1], halo0.at[0], big_send, big_recv, V0)

    def scatter(step, carry):
        other = lax.rem(me + 1 + lax.rem(step + n // 2 - 1, n - 1), n)
        pltpu.make_async_remote_copy(
            src_ref=dens.at[other], dst_ref=got.at[me], send_sem=many_send.at[0],
            recv_sem=many_recv.at[0], device_id=peer(other),
            device_id_type=pl.DeviceIdType.MESH).start()
        return carry

    lax.fori_loop(0, n - 1, scatter, 0)

    def dielectric(r):
        return jnp.where(r == 0, INSIDE, SOLVENT).astype(F32)

    e = [dielectric(regions[p]) for p in range(2)]
    k = [jnp.where(regions[p] == 2, SCREEN, 0.0).astype(F32) for p in range(2)]
    right0, left0 = pool_right(nxy, half, nxy), pool_left(half, nxy)
    right1, left1 = pool_right(half, LANES, half), pool_left(quarter, half)

    def down0(a, b):
        return 0.125 * dot(left0, times(a + b, right0))

    def down1(a):
        return 0.25 * dot(left1, times(a, right1))

    e1, k1 = down0(e[0], e[1]), down0(k[0], k[1])
    plane1[E1] = e1
    recv_e1 = launch(plane1.at[E1], plane1.at[E1], halo1.at[E1], small_send, small_recv, E1)
    core, chip = lax.rem(me, 2), me // 2
    gk[core, chip] = down1(e1) + back(down1(k1), 1, LANES // 2)

    def share(ref, i):
        def one(off, carry):
            other = lax.rem(me + 2 * off, n)
            pltpu.make_async_remote_copy(
                src_ref=ref.at[core, chip], dst_ref=ref.at[core, chip], send_sem=many_send.at[i],
                recv_sem=many_recv.at[i], device_id=peer(other),
                device_id_type=pl.DeviceIdType.MESH).start()
            return carry

        lax.fori_loop(1, n // 2, one, 0)

    def relay(ref, i):
        window = ref.at[0, pl.ds(0, n // 2 - 1)]
        pltpu.make_async_copy(window, window, many_recv.at[i]).wait()
        copy = pltpu.make_async_remote_copy(
            src_ref=ref.at[core], dst_ref=ref.at[core], send_sem=many_send.at[i + 2],
            recv_sem=many_recv.at[i + 2], device_id=peer(me + 1 - 2 * core),
            device_id_type=pl.DeviceIdType.MESH)
        copy.start()
        pending.append(pltpu.make_async_copy(window, window, many_send.at[i]).wait)
        pending.append(copy.wait_send)
        return copy.wait_recv

    def all_in(ref, sems, i):
        window = ref.at[pl.ds(0, n - 1)]
        pltpu.make_async_copy(window, window, sems.at[i]).wait()

    share(gk, 1)

    totals = []
    middle = face(e[0], e[1], 1.0)
    fz0[1] = middle
    part = []
    for p in range(2):
        fx, fy, total = plane_faces(e[p], 1.0)
        fx0[p] = fx
        fy0[p] = fy
        totals.append(total + middle + k[p])
        part.append(plane_sum(fx, fy, previous[p]) + middle * previous[1 - p])
    recv_reg()
    e_side = [jnp.where(has_lo, dielectric(halo_reg[0]), e[0]),
              jnp.where(has_hi, dielectric(halo_reg[1]), e[1])]
    for p in range(2):
        outer = face(e_side[p], e[p], 1.0)
        fz0[2 * p] = outer
        total = totals[p] + outer
        dg0[p] = total
        wt0[p] = DAMPING / total

    def beside0(p, mine, below, above):
        return plane_sum(fx0[p], fy0[p], mine) + fz0[p] * below + fz0[p + 1] * above

    def sweep0(p, mine, below, above):
        return (1.0 - DAMPING) * mine + wt0[p] * (b0[p] + beside0(p, mine, below, above))

    recv_v0()
    for p in range(2):
        v1[p] = (1.0 - DAMPING) * previous[p] + wt0[p] * (part[p] + fz0[2 * p] * halo0[0, p])

    got[me] = dens[me]
    all_in(got, many_recv, 0)
    for p in range(2):
        if rows % 8 == 0:
            b0[p] = got[:, p].reshape(nxy, nxy)
        else:
            for s in range(n):
                b0[p, s * rows:(s + 1) * rows, :] = got[s, p]
    for p in range(2):
        v1[p] = v1[p] + wt0[p] * b0[p]
    recv = launch(v1.at[0], v1.at[1], halo0.at[1], big_send, big_recv, V1)
    recv_gk = relay(gk, 1)
    recv_e1()
    sz1 = sx1 = 4.0
    fx1, fy1, total1 = plane_faces(e1, sx1)
    fz1lo = face(jnp.where(has_lo, halo1[E1, 0], e1), e1, sz1)
    fz1hi = face(jnp.where(has_hi, halo1[E1, 1], e1), e1, sz1)
    dg1 = total1 + fz1lo + fz1hi + k1
    wt1 = DAMPING / dg1

    recv()
    v2[0] = sweep0(0, v1[0], halo0[1, 0], v1[1])
    v2[1] = sweep0(1, v1[1], v1[0], halo0[1, 1])
    term1[0] = 0.125 * dot(left0, times(fz0[0] * v2[0], right0))
    term1[1] = 0.125 * dot(left0, times(fz0[2] * v2[1], right0))
    recv_term = launch(term1.at[0], term1.at[1], halo1.at[TERM], small_send, small_recv, TERM)
    recv_v2 = launch(v2.at[0], v2.at[1], halo0.at[2], big_send, big_recv, V2)
    r0 = b0[0] - dg0[0] * v2[0] + plane_sum(fx0[0], fy0[0], v2[0]) + fz0[1] * v2[1]
    r1 = b0[1] - dg0[1] * v2[1] + plane_sum(fx0[1], fy0[1], v2[1]) + fz0[1] * v2[0]
    b1 = down0(r0, r1)
    recv_far = launch(regions.at[1], regions.at[0], far_reg, big_send, big_recv, FAR)
    recv_gk()
    e2 = 0.5 * (gk[0] + gk[1]).reshape(n // 2 * quarter, LANES)
    k2 = back(e2, 1, LANES // 2)
    coarse = coarse_cycle(e2, k2, n // 2, quarter, 16.0, 16.0, dot, times)
    recv_term()
    b1 = b1 + halo1[TERM, 0] + halo1[TERM, 1]

    def beside1(mine, i):
        return plane_sum(fx1, fy1, mine) + fz1lo * halo1[i, 0] + fz1hi * halo1[i, 1]

    def trade1(value, i):
        plane1[i] = value
        launch(plane1.at[i], plane1.at[i], halo1.at[i], small_send, small_recv, i)()

    a = wt1 * b1
    trade1(a, A1)
    a = (1.0 - DAMPING) * a + wt1 * (b1 + beside1(a, A1))
    trade1(a, A2)
    full = down1(b1 - dg1 * a + beside1(a, A2))
    gb[core, chip] = full[:quarter // 2] + back(full[quarter // 2:], 1, LANES // 2)
    share(gb, 2)
    recv_v2()
    base[0] = sweep0(0, v2[0], halo0[2, 0], v2[1])
    base[1] = sweep0(1, v2[1], v2[0], halo0[2, 1])
    recv_base = launch(base.at[0], base.at[1], halo0.at[3], big_send, big_recv, BASE)
    relay_gb = relay(gb, 2)
    recv_far()
    for p in range(2):
        region = halo_reg[p]
        beyond = face(e_side[p], dielectric(far_reg[p]), 1.0)
        fx, fy, total = plane_faces(e_side[p], 1.0)
        fxh[p] = fx
        fyh[p] = fy
        fzh[p] = beyond
        wth[p] = DAMPING / (total + beyond + fz0[2 * p] + jnp.where(region == 2, SCREEN, 0.0))
    relay_gb()
    packed = 0.5 * (gb[0] + gb[1]).reshape(n // 2 * quarter // 2, LANES)
    split = (n // 2, quarter // 2, LANES)
    b2 = jnp.concatenate(
        [packed.reshape(split), back(packed, 1, LANES // 2).reshape(split)], axis=1
    ).reshape(n // 2 * quarter, LANES)
    c2 = coarse(b2)

    for i in range(n // 2):
        c2_planes[i] = c2[i * quarter:(i + 1) * quarter]
    grow_l, grow_r = spread_left(half, quarter), spread_right(LANES, half, half)

    def up1(index):
        return dot(grow_l, times(c2_planes[index // 2], grow_r))

    halo1[A2, 0] = halo1[A2, 0] + jnp.where(has_lo, up1(jnp.maximum(me - 1, 0)), 0.0)
    halo1[A2, 1] = halo1[A2, 1] + jnp.where(has_hi, up1(jnp.minimum(me + 1, n - 1)), 0.0)
    a = a + up1(me)
    a = (1.0 - DAMPING) * a + wt1 * (b1 + beside1(a, A2))
    trade1(a, A3)
    a = (1.0 - DAMPING) * a + wt1 * (b1 + beside1(a, A3))
    trade1(a, A4)

    big_l, big_r = spread_left(nxy, half), spread_right(half, nxy, nxy)

    def up0(c):
        return dot(big_l, times(c, big_r))

    mine = up0(a)
    recv_base()
    v3, side = [], []
    present = [has_lo, has_hi]
    for p in range(2):
        c = up0(halo1[A4, p])
        own = plane_sum(fx0[p], fy0[p], mine) + fz0[1] * mine + fz0[2 * p] * c
        v3.append(base[p] + (1.0 - DAMPING) * mine + wt0[p] * own)
        other = plane_sum(fxh[p], fyh[p], c) + fzh[p] * c + fz0[2 * p] * mine
        swept = halo0[3, p] + (1.0 - DAMPING) * c + wth[p] * other
        side.append(jnp.where(present[p], swept, 0.0))
    out[0] = sweep0(0, v3[0], side[0], v3[1])
    out[1] = sweep0(1, v3[1], v3[0], side[1])

    for sent in pending:
        sent()
    all_in(got, many_send, 0)


HALO = 16
REG_LO, REG_HI, V0_LO, V0_HI, V1_LO, V1_HI, V2_LO, V2_HI, BASE_LO, BASE_HI = range(10)
E_M1, E_P1, E_M2, E_P2, K_M1, K_P1, B_M1, B_P1, B_M2, B_P2, A2_LO, A2_HI, NEAR, NEAR_CORE, FAR_LO, FAR_HI = range(10, 26)
MESSAGES = 26


def box_kernel(n, partials, regions, previous, out,
               parts, dens, reg, v0, b0, fx0, fy0, fz0, dg0, wt0, v1, v2, base, swept,
               near, fxn, fyn, fzn, wtn, landed, corr,
               e1, k1, fx1, fy1, fz1, dg1, wt1, pack, from_lo, from_hi, far_lo, far_hi,
               b1, a1, a2, a2c, a3, a4, gk, gb, c2_planes, rows_tmp,
               load_sem, spread_send, spread_recv, corr_send, corr_recv, dens_send, dens_recv,
               side_send, side_recv, many_send, many_recv):
    me = lax.axis_index("slab")
    nz = n // 2
    z, x, core = me // 4, lax.rem(me // 2, 2), lax.rem(me, 2)
    zi = 2 * z + core
    nxy = regions.shape[1]
    half, quarter = nxy // 2, nxy // 4
    rows = partials.shape[2]
    window = half + HALO
    window1 = window // 2
    blocks = window // rows
    first = half - HALO

    def peer(index):
        return {"slab": index}

    def at(i, j):
        return (i // 2) * 4 + j * 2 + lax.rem(i, 2)

    load = pltpu.make_async_copy(partials, parts, load_sem.at[0])
    load.start()
    load_near = pltpu.make_async_copy(regions, near.at[pl.ds(2, 2)], load_sem.at[1])
    load_near.start()
    barrier = pltpu.get_barrier_semaphore()

    def greet(off, carry):
        pl.semaphore_signal(barrier, inc=1, device_id=peer(lax.rem(me + off, n)),
                            device_id_type=pl.DeviceIdType.MESH)
        return carry

    lax.fori_loop(1, n, greet, 0)

    plane0 = jnp.zeros((window, nxy), F32)
    plane1 = jnp.zeros((window1, half), F32)

    @pl.when(zi == 0)
    def _():
        for i in range(2):
            reg[i] = jnp.zeros((window, nxy), jnp.int32)
        for v in (v0, v1, v2, base):
            v[0] = plane0
        for i in range(3):
            from_lo[i] = plane1
        for i in range(2):
            e1[i] = plane1 + 1.0
            k1[i] = plane1
        a2[0] = plane1

    @pl.when(zi == nz - 1)
    def _():
        for i in range(2):
            reg[6 + i] = jnp.zeros((window, nxy), jnp.int32)
        for v in (v0, v1, v2, base):
            v[5] = plane0
        for i in range(3):
            from_hi[i] = plane1
        for i in range(2):
            e1[6 + i] = plane1 + 1.0
            k1[4 + i] = plane1
        a2[5] = plane1

    @pl.when(zi < 2)
    def _():
        far_lo[0] = plane1

    @pl.when(zi >= nz - 2)
    def _():
        far_hi[0] = plane1

    @pl.when(me == 0)
    def _():
        corr[0] = jnp.zeros((half, half), F32)

    @pl.when(me == n - 1)
    def _():
        corr[2] = jnp.zeros((half, half), F32)

    load.wait()
    density = parts[0].astype(F32)
    for g in range(1, partials.shape[0]):
        density = density + parts[g].astype(F32)
    dens[...] = (SOURCE * density).reshape(dens.shape)

    pl.semaphore_wait(barrier, n - 1)
    pending = []

    def spread(src, dst, mine, first_slot, step, i):
        for j in range(2):
            target = at(2 * z + x, j)
            piece = src.at[pl.ds(mine, 1), pl.ds(first * j, window), :]
            place = dst.at[pl.ds(first_slot + step * core, 1)]
            remote = pltpu.make_async_remote_copy(
                src_ref=piece, dst_ref=place, send_sem=spread_send.at[i, j],
                recv_sem=spread_recv.at[i, core], device_id=peer(target),
                device_id_type=pl.DeviceIdType.MESH)
            here = pltpu.make_async_copy(piece, place, spread_recv.at[i, core])
            away = target != me
            pl.when(away)(remote.start)
            pl.when(jnp.logical_not(away))(here.start)
            pending.append(lambda remote=remote, away=away: pl.when(away)(remote.wait_send))

        def arrived():
            for j in range(2):
                place = dst.at[pl.ds(first_slot + step * j, 1)]
                pltpu.make_async_copy(place, place, spread_recv.at[i, j]).wait()

        return arrived

    def send_density(step, carry):
        other = lax.rem(me + 1 + lax.rem(step + n // 2 - 1, n), n)
        oz, ox = 2 * (other // 4) + lax.rem(other, 2), lax.rem(other // 2, 2)
        block = me - (first // rows) * ox
        inside = (block >= 0) & (block < blocks)
        block = jnp.clip(block, 0, blocks - 1)
        place = b0.at[:, pl.ds(pl.multiple_of(block * rows, rows), rows), :]

        @pl.when(inside & (other != me))
        def _():
            pltpu.make_async_remote_copy(
                src_ref=dens.at[oz], dst_ref=place, send_sem=dens_send.at[other],
                recv_sem=dens_recv.at[0], device_id=peer(other),
                device_id_type=pl.DeviceIdType.MESH).start()

        @pl.when(inside & (other == me))
        def _():
            pltpu.make_async_copy(dens.at[oz], place, dens_recv.at[0]).start()

        return carry

    def sent_density(other, carry):
        ox = lax.rem(other // 2, 2)
        block = me - (first // rows) * ox

        @pl.when((block >= 0) & (block < blocks) & (other != me))
        def _():
            pltpu.make_async_copy(dens.at[0], dens.at[0], dens_send.at[other]).wait()

        return carry

    def push(src, dst, delta, i):
        can_send = (zi + delta >= 0) & (zi + delta < nz)
        can_recv = (zi - delta >= 0) & (zi - delta < nz)
        copy = pltpu.make_async_remote_copy(
            src_ref=src, dst_ref=dst, send_sem=side_send.at[i], recv_sem=side_recv.at[i],
            device_id=peer(at(jnp.clip(zi + delta, 0, nz - 1), x)),
            device_id_type=pl.DeviceIdType.MESH)
        pl.when(can_send)(copy.start)
        pending.append(lambda: pl.when(can_send)(copy.wait_send))
        return lambda: pl.when(can_recv)(copy.wait_recv)

    def trade(field, low, high, i):
        down = push(field.at[low], field.at[high + 1], -1, i)
        up = push(field.at[high], field.at[low - 1], 1, i + 1)

        def arrived():
            down()
            up()

        return arrived

    lax.fori_loop(0, n, send_density, 0)
    reg_edge = spread(regions, reg, core, 2, 3, 0)
    v0_edge = spread(previous, v0, core, 1, 3, 1)
    reg_in = spread(regions, reg, 1 - core, 3, 1, 3)
    v0_in = spread(previous, v0, 1 - core, 2, 1, 4)

    def dielectric(r):
        return jnp.where(r == 0, INSIDE, SOLVENT).astype(F32)

    right0 = pool_right(nxy, half, nxy)
    right1 = pool_right(half, LANES, half)
    dst1, src1 = iota((quarter // 2, window1), 0), iota((quarter // 2, window1), 1)
    left1 = jnp.where((src1 - (HALO // 2) * x) // 2 == dst1, 1.0, 0.0).astype(F32)

    turn = [0]

    def strips(v):
        return [v[:, i:i + LANES] for i in range(0, v.shape[1], LANES)]

    def scratch():
        turn[0] = (turn[0] + 1) % 8
        return rows_tmp.at[turn[0]]

    def pool_rows(v):
        count = v.shape[0] // 2
        done = []
        for strip in strips(v):
            tmp = scratch()
            tmp[:2 * count] = strip
            done.append(tmp[pl.ds(0, count, stride=2), :] + tmp[pl.ds(1, count, stride=2), :])
        return done[0] if len(done) == 1 else jnp.concatenate(done, axis=1)

    def grow_rows(v):
        count = v.shape[0]
        done = []
        for strip in strips(v):
            tmp = scratch()
            tmp[pl.ds(0, count, stride=2), :] = strip
            tmp[pl.ds(1, count, stride=2), :] = strip
            done.append(tmp[:2 * count])
        return done[0] if len(done) == 1 else jnp.concatenate(done, axis=1)

    def down0(a):
        return 0.125 * times2(pool_rows(a), right0)

    def down1(a):
        return 0.125 * dot2(left1, times2(a, right1))

    reg_edge()
    reg_halo = trade(reg, 2, 5, REG_LO)
    v0_edge()
    v0_halo = trade(v0, 1, 4, V0_LO)
    reg_in()
    far_in = [push(reg.at[3], reg.at[7], -1, FAR_LO), push(reg.at[4], reg.at[0], 1, FAR_HI)]
    e = [dielectric(reg[p]) for p in range(2, 6)]
    k = [jnp.where(reg[p] == 2, SCREEN, 0.0).astype(F32) for p in range(2, 6)]
    for i in range(2):
        e1[3 + i] = down0(e[2 * i] + e[2 * i + 1])
        k1[2 + i] = down0(k[2 * i] + k[2 * i + 1])
    e1_in = [push(e1.at[pl.ds(3, 2)], e1.at[pl.ds(1, 2)], 1, E_P1),
             push(e1.at[pl.ds(3, 2)], e1.at[pl.ds(5, 2)], -1, E_M1),
             push(e1.at[pl.ds(4, 1)], e1.at[pl.ds(0, 1)], 2, E_P2),
             push(e1.at[pl.ds(3, 1)], e1.at[pl.ds(7, 1)], -2, E_M2),
             push(k1.at[pl.ds(2, 2)], k1.at[pl.ds(0, 2)], 1, K_P1),
             push(k1.at[pl.ds(2, 2)], k1.at[pl.ds(4, 2)], -1, K_M1)]
    chip = me // 2
    gk[core, x, z] = down1(e1[3] + e1[4]) + back(down1(k1[2] + k1[3]), 1, LANES // 2)

    def share(ref, i):
        def one(off, carry):
            other = lax.rem(me + 2 * off, n)
            pltpu.make_async_remote_copy(
                src_ref=ref.at[core, chip], dst_ref=ref.at[core, chip], send_sem=many_send.at[i],
                recv_sem=many_recv.at[i], device_id=peer(other),
                device_id_type=pl.DeviceIdType.MESH).start()
            return carry

        lax.fori_loop(1, n // 2, one, 0)

    def relay(ref, i):
        seven = ref.at[0, pl.ds(0, n // 2 - 1)]
        pltpu.make_async_copy(seven, seven, many_recv.at[i]).wait()
        copy = pltpu.make_async_remote_copy(
            src_ref=ref.at[core], dst_ref=ref.at[core], send_sem=many_send.at[i + 2],
            recv_sem=many_recv.at[i + 2], device_id=peer(me + 1 - 2 * core),
            device_id_type=pl.DeviceIdType.MESH)
        copy.start()
        pending.append(pltpu.make_async_copy(seven, seven, many_send.at[i]).wait)
        pending.append(copy.wait_send)
        return copy.wait_recv

    def in_order(ref):
        return [ref[c, 2 * i + j] for i in range(n // 4) for c in range(2) for j in range(2)]

    columns = n // 4

    def along(off, carry):
        other = lax.rem(me + 4 * off, n)
        pltpu.make_async_remote_copy(
            src_ref=gk.at[core, x, z], dst_ref=gk.at[core, x, z], send_sem=many_send.at[0],
            recv_sem=many_recv.at[0], device_id=peer(other),
            device_id_type=pl.DeviceIdType.MESH).start()
        return carry

    lax.fori_loop(1, columns, along, 0)

    def gk_over():
        others = gk.at[0, 0, pl.ds(0, columns - 1)]
        pltpu.make_async_copy(others, others, many_recv.at[0]).wait()
        copy = pltpu.make_async_remote_copy(
            src_ref=gk.at[core, x], dst_ref=gk.at[core, x], send_sem=many_send.at[4],
            recv_sem=many_recv.at[4], device_id=peer(at(zi, 1 - x)),
            device_id_type=pl.DeviceIdType.MESH)
        copy.start()
        pending.append(pltpu.make_async_copy(others, others, many_send.at[0]).wait)
        pending.append(copy.wait_send)
        return copy.wait_recv

    def gk_beside():
        copy = pltpu.make_async_remote_copy(
            src_ref=gk.at[core], dst_ref=gk.at[core], send_sem=many_send.at[2],
            recv_sem=many_recv.at[2], device_id=peer(at(zi + 1 - 2 * core, x)),
            device_id_type=pl.DeviceIdType.MESH)
        copy.start()
        pending.append(copy.wait_send)
        return copy.wait_recv

    totals = []
    for p in range(4):
        fx, fy, total = plane_faces(e[p], 1.0)
        fx0[p] = fx
        fy0[p] = fy
        totals.append(total + k[p])
    for p in range(1, 4):
        fz0[p] = face(e[p - 1], e[p], 1.0)
    v0_in()

    def beside0(p, v):
        return (plane_sum(fx0[p], fy0[p], v[p + 1]) + fz0[p] * v[p] + fz0[p + 1] * v[p + 2])

    def sweep0(p, v):
        return (1.0 - DAMPING) * v[p + 1] + wt0[p] * (b0[p] + beside0(p, v))

    def first_part(p):
        v1[p + 1] = (1.0 - DAMPING) * v0[p + 1] + wt0[p] * beside0(p, v0)

    def weights(p):
        diag = totals[p] + fz0[p] + fz0[p + 1]
        dg0[p] = diag
        wt0[p] = DAMPING / diag

    for p in (1, 2):
        weights(p)
        first_part(p)
    reg_halo()
    fz0[0] = face(jnp.where(zi > 0, dielectric(reg[1]), e[0]), e[0], 1.0)
    fz0[4] = face(e[3], jnp.where(zi < nz - 1, dielectric(reg[6]), e[3]), 1.0)
    weights(0)
    weights(3)
    v0_halo()
    first_part(0)
    first_part(3)

    pltpu.make_async_copy(b0, b0, dens_recv.at[0]).wait()
    for p in (0, 3):
        v1[p + 1] = v1[p + 1] + wt0[p] * b0[p]
    v1_halo = trade(v1, 1, 4, V1_LO)
    for arrived in far_in:
        arrived()
    own_rows = pl.ds(pl.multiple_of(HALO * x, HALO), half)

    def near_rows(j):
        return near.at[pl.ds(4 * core, 2), pl.ds(pl.multiple_of(half * j, half), half), :]

    across = pltpu.make_async_remote_copy(
        src_ref=reg.at[pl.ds(4 + 2 * core - 4 * x, 2), own_rows, :], dst_ref=near_rows(x),
        send_sem=side_send.at[NEAR], recv_sem=side_recv.at[NEAR], device_id=peer(at(zi, 1 - x)),
        device_id_type=pl.DeviceIdType.MESH)
    beside = pltpu.make_async_remote_copy(
        src_ref=regions, dst_ref=near.at[pl.ds(4 * core, 2)], send_sem=side_send.at[NEAR_CORE],
        recv_sem=side_recv.at[NEAR_CORE], device_id=peer(at(zi + 1 - 2 * core, x)),
        device_id_type=pl.DeviceIdType.MESH)
    within = pltpu.make_async_copy(reg.at[pl.ds(2 * core + 4 * x, 2), own_rows, :], near_rows(x),
                                   load_sem.at[2])
    for copy in (across, beside, within):
        copy.start()
    pending.append(across.wait_send)
    pending.append(beside.wait_send)
    gk_across = gk_over()

    for p in (1, 2):
        v1[p + 1] = v1[p + 1] + wt0[p] * b0[p]

    for p in (1, 2):
        v2[p + 1] = sweep0(p, v1)
    v1_halo()
    for p in (0, 3):
        v2[p + 1] = sweep0(p, v1)
    v2_halo = trade(v2, 1, 4, V2_LO)
    pack[0] = down0(fz0[4] * v2[4])
    pack[3] = down0(fz0[0] * v2[1])

    def left_over(p):
        r = b0[p] - dg0[p] * v2[p + 1] + plane_sum(fx0[p], fy0[p], v2[p + 1])
        if p > 0:
            r = r + fz0[p] * v2[p]
        if p < 3:
            r = r + fz0[p + 1] * v2[p + 2]
        return r

    for i in range(2):
        pack[1 + i] = down0(left_over(2 * i) + left_over(2 * i + 1))
    b1_in = [push(pack.at[pl.ds(0, 3)], from_lo, 1, B_P1),
             push(pack.at[pl.ds(1, 3)], from_hi, -1, B_M1),
             push(pack.at[pl.ds(0, 1)], far_lo, 2, B_P2),
             push(pack.at[pl.ds(3, 1)], far_hi, -2, B_M2)]
    for arrived in e1_in:
        arrived()

    @pl.when(zi == 0)
    def _():
        e1[2] = e1[3]
        e1[0] = plane1 + 1.0

    @pl.when(zi == 1)
    def _():
        e1[0] = e1[1]

    @pl.when(zi == nz - 1)
    def _():
        e1[5] = e1[4]
        e1[7] = plane1 + 1.0

    @pl.when(zi == nz - 2)
    def _():
        e1[7] = e1[6]

    s1 = 4.0
    for i in range(7):
        fz1[i] = face(e1[i], e1[i + 1], s1)
    for i in range(6):
        fx, fy, total = plane_faces(e1[i + 1], s1)
        fx1[i] = fx
        fy1[i] = fy
        diag = total + fz1[i] + fz1[i + 1] + k1[i]
        dg1[i] = diag
        weight = DAMPING / diag
        if i < 2:
            weight = jnp.where(zi > 0, weight, 0.0)
        if i > 3:
            weight = jnp.where(zi < nz - 1, weight, 0.0)
        wt1[i] = weight

    v2_halo()
    for p in (0, 3, 1, 2):
        base[p + 1] = sweep0(p, v2)
    base_halo = trade(base, 1, 4, BASE_LO)
    for arrived in b1_in:
        arrived()
    b1[0] = from_lo[1] + far_lo[0]
    b1[1] = from_lo[2] + pack[3]
    b1[2] = pack[1] + from_lo[0]
    b1[3] = pack[2] + from_hi[2]
    b1[4] = from_hi[0] + pack[0]
    b1[5] = from_hi[1] + far_hi[0]

    def beside1(i, mine, below, above):
        return plane_sum(fx1[i], fy1[i], mine) + fz1[i] * below + fz1[i + 1] * above

    def sweep1(i, mine, below, above):
        return (1.0 - DAMPING) * mine + wt1[i] * (b1[i] + beside1(i, mine, below, above))

    for i in range(6):
        a1[i] = wt1[i] * b1[i]
    for i in range(1, 5):
        a2[i] = sweep1(i, a1[i], a1[i - 1], a1[i + 1])
    rest = [b1[i] - dg1[i] * a2[i] + beside1(i, a2[i], a2[i - 1], a2[i + 1]) for i in (2, 3)]
    full = down1(rest[0] + rest[1])
    gb[core, chip] = full[:quarter // 4] + back(full[quarter // 4:], 1, LANES // 2)
    share(gb, 1)
    a2_in = [push(a2.at[2], a2.at[0], 1, A2_HI), push(a2.at[3], a2.at[5], -1, A2_LO)]
    gk_across()
    gk_in = gk_beside()
    gk_in()
    e2 = jnp.concatenate([gk[i, j, m] for m in range(n // 4) for i in range(2) for j in range(2)], axis=0)
    coarse = coarse_cycle(e2, back(e2, 1, LANES // 2), nz, quarter, 16.0, 16.0,
                          dot2, times2, (pool_rows, grow_rows))
    base_halo()

    def deliver(j):
        target = 4 * z + 2 * core + j
        piece = swept.at[pl.ds(2 * j, 2), pl.ds(pl.multiple_of(HALO * x, HALO), half), :]
        place = landed.at[:, pl.ds(pl.multiple_of(half * x, half), half), :]
        remote = pltpu.make_async_remote_copy(
            src_ref=piece, dst_ref=place, send_sem=spread_send.at[2, j],
            recv_sem=spread_recv.at[2, x], device_id=peer(target),
            device_id_type=pl.DeviceIdType.MESH)
        here = pltpu.make_async_copy(piece, place, spread_recv.at[2, x])
        away = target != me
        pl.when(away)(remote.start)
        pl.when(jnp.logical_not(away))(here.start)
        pending.append(lambda: pl.when(away)(remote.wait_send))

    for p in range(4):
        swept[p] = sweep0(p, base)
        if p % 2:
            deliver(p // 2)
    gb_in = relay(gb, 1)
    gb_in()
    packed = jnp.stack(in_order(gb))
    b2 = jnp.concatenate([packed, back(packed.reshape(-1, LANES), 1, LANES // 2).reshape(packed.shape)],
                         axis=1).reshape(nz * quarter, LANES)
    c2 = coarse(b2)
    for i in range(nz):
        c2_planes[i] = c2[i * quarter:(i + 1) * quarter]
    fine, mid = iota((window1, quarter), 0), iota((window1, quarter), 1)
    grow_l = jnp.where((fine + first // 2 * x) // 2 == mid, 1.0, 0.0).astype(F32)
    grow_r = spread_right(LANES, half, half)

    def up1(index):
        return dot2(grow_l, times2(c2_planes[index], grow_r))


    for arrived in a2_in:
        arrived()
    mine = up1(zi)
    lower = jnp.where(zi > 0, up1(jnp.maximum(zi - 1, 0)), 0.0)
    upper = jnp.where(zi < nz - 1, up1(jnp.minimum(zi + 1, nz - 1)), 0.0)
    for i, c in enumerate((lower, lower, mine, mine, upper, upper)):
        a2c[i] = a2[i] + c
    for i in range(1, 5):
        a3[i - 1] = sweep1(i, a2c[i], a2c[i - 1], a2c[i + 1])
    for i in (1, 2):
        a4[i] = sweep1(i + 1, a3[i], a3[i - 1], a3[i + 1])

    def hand(count, low, delta, slot, i):
        target = 2 * zi + delta
        exists = (target >= 0) & (target < n)
        piece = a4.at[pl.ds(low, count), pl.ds(pl.multiple_of(HALO // 2 * x, HALO // 2), quarter), :]
        place = corr.at[pl.ds(slot, count), pl.ds(pl.multiple_of(quarter * x, quarter), quarter), :]
        kind = 2 - count
        remote = pltpu.make_async_remote_copy(
            src_ref=piece, dst_ref=place, send_sem=corr_send.at[i], recv_sem=corr_recv.at[kind, x],
            device_id=peer(jnp.clip(target, 0, n - 1)), device_id_type=pl.DeviceIdType.MESH)
        here = pltpu.make_async_copy(piece, place, corr_recv.at[kind, x])
        away = exists & (target != me)
        pl.when(away)(remote.start)
        pl.when(target == me)(here.start)
        pending.append(lambda: pl.when(away)(remote.wait_send))

    hand(2, 1, 0, 1, 0)
    hand(2, 1, 1, 0, 1)
    hand(1, 1, -1, 2, 2)
    hand(1, 2, 2, 0, 3)
    big_l, big_r = spread_left(nxy, half), spread_right(half, nxy, nxy)

    def up0(c):
        return dot2(big_l, times2(c, big_r))

    load_near.wait()
    within.wait()
    across.wait_recv()
    beside.wait_recv()
    en = [dielectric(near[f]) for f in range(6)]
    fzn[0] = face(en[0], en[1], 1.0)
    fzn[1] = face(jnp.where(me > 0, en[1], en[2]), en[2], 1.0)
    fzn[2] = face(en[2], en[3], 1.0)
    fzn[3] = face(en[3], jnp.where(me < n - 1, en[4], en[3]), 1.0)
    fzn[4] = face(en[4], en[5], 1.0)
    for f in range(4):
        fx, fy, total = plane_faces(en[f + 1], 1.0)
        fxn[f] = fx
        fyn[f] = fy
        kn = jnp.where(near[f + 1] == 2, SCREEN, 0.0).astype(F32)
        wtn[f] = DAMPING / (total + kn + fzn[f] + fzn[f + 1])
    for sent in pending:
        sent()
    lax.fori_loop(0, n, sent_density, 0)
    single = jnp.where(lax.rem(me, 2) == 0, me > 0, me < n - 1)
    for j in range(2):
        both = corr.at[pl.ds(0, 2), pl.ds(quarter * j, quarter), :]
        pltpu.make_async_copy(both, both, corr_recv.at[0, j]).wait()
        one = corr.at[pl.ds(0, 1), pl.ds(quarter * j, quarter), :]
        pl.when(single)(pltpu.make_async_copy(one, one, corr_recv.at[1, j]).wait)
    for j in range(2):
        place = landed.at[:, pl.ds(half * j, half), :]
        pltpu.make_async_copy(place, place, spread_recv.at[2, j]).wait()
    below, here, above = (up0(corr[i]) for i in range(3))
    spans = [(below, below, here), (here, below, here), (here, here, above), (above, here, above)]

    def relax(f, mine, low, high):
        return (1.0 - DAMPING) * mine + wtn[f] * (
            plane_sum(fxn[f], fyn[f], mine) + fzn[f] * low + fzn[f + 1] * high)

    y = [relax(f, *spans[f]) for f in range(4)]
    y[0] = jnp.where(me > 0, y[0], 0.0)
    y[3] = jnp.where(me < n - 1, y[3], 0.0)
    for f in (1, 2):
        out[f - 1] = landed[f - 1] + relax(f, y[f], y[f - 1], y[f + 1])


def box_local(partials, regions, previous):
    n = lax.axis_size("slab")
    nxy = regions.shape[1]
    half, quarter = nxy // 2, nxy // 4
    rows = partials.shape[2]
    window, window1 = half + HALO, (half + HALO) // 2
    vmem = lambda *shape: pltpu.VMEM(shape, F32)
    big = lambda count: vmem(count, window, nxy)
    small = lambda count: vmem(count, window1, half)
    return pl.pallas_call(
        functools.partial(box_kernel, n),
        out_shape=pltpu.VMEM(previous.shape, F32),
        in_specs=[pl.BlockSpec(memory_space=pltpu.HBM)] * 3,
        out_specs=pl.BlockSpec(memory_space=pltpu.VMEM),
        scratch_shapes=[
            pltpu.VMEM(partials.shape, partials.dtype), vmem(n // 2, 4, rows, nxy),
            pltpu.VMEM((8, window, nxy), jnp.int32), big(6), big(4),
            big(4), big(4), big(5), big(4), big(4), big(6), big(6), big(6), big(4),
            pltpu.VMEM((6, nxy, nxy), jnp.int32), vmem(4, nxy, nxy), vmem(4, nxy, nxy),
            vmem(5, nxy, nxy), vmem(4, nxy, nxy), vmem(2, nxy, nxy), vmem(3, half, half),
            small(8), small(6), small(6), small(6), small(7), small(6), small(6),
            small(4), small(3), small(3), small(1), small(1),
            small(6), small(6), small(6), small(6), small(4), small(4),
            vmem(2, 2, n // 4, quarter // 2, LANES), vmem(2, n // 2, quarter // 4, LANES),
            vmem(n // 2, quarter, LANES), vmem(8, 2 * nxy, LANES),
            pltpu.SemaphoreType.DMA((3,)),
            pltpu.SemaphoreType.DMA((5, 2)), pltpu.SemaphoreType.DMA((5, 2)),
            pltpu.SemaphoreType.DMA((4,)), pltpu.SemaphoreType.DMA((2, 2)),
            pltpu.SemaphoreType.DMA((n,)), pltpu.SemaphoreType.DMA((1,)),
            pltpu.SemaphoreType.DMA((MESSAGES,)), pltpu.SemaphoreType.DMA((MESSAGES,)),
            pltpu.SemaphoreType.DMA((5,)), pltpu.SemaphoreType.DMA((5,)),
        ],
        compiler_params=pltpu.CompilerParams(
            collective_id=1, has_side_effects=True, vmem_limit_bytes=60 * 1024 * 1024),
    )(partials, regions, previous)


def local(partials, regions, previous):
    n = lax.axis_size("slab")
    nxy = regions.shape[1]
    half, quarter = nxy // 2, nxy // 4
    rows = partials.shape[2]
    vmem = lambda *shape: pltpu.VMEM(shape, F32)
    spec = pl.BlockSpec(memory_space=pltpu.VMEM)
    return pl.pallas_call(
        functools.partial(kernel, n),
        out_shape=jax.ShapeDtypeStruct(previous.shape, F32),
        in_specs=[spec] * 3,
        out_specs=spec,
        scratch_shapes=[
            vmem(n, 2, rows, nxy), vmem(n, 2, rows, nxy), vmem(2, nxy, nxy),
            vmem(2, nxy, nxy), vmem(2, nxy, nxy), vmem(3, nxy, nxy), vmem(2, nxy, nxy),
            vmem(2, nxy, nxy),
            pltpu.VMEM((2, nxy, nxy), jnp.int32), pltpu.VMEM((2, nxy, nxy), jnp.int32),
            vmem(2, nxy, nxy), vmem(2, nxy, nxy), vmem(2, nxy, nxy), vmem(2, nxy, nxy),
            vmem(4, 2, nxy, nxy),
            vmem(2, nxy, nxy), vmem(2, nxy, nxy), vmem(2, nxy, nxy),
            vmem(6, 2, half, half), vmem(5, half, half), vmem(2, half, half),
            vmem(2, n // 2, quarter // 2, LANES), vmem(2, n // 2, quarter, LANES),
            pltpu.SemaphoreType.DMA((6, 2)), pltpu.SemaphoreType.DMA((6, 2)),
            pltpu.SemaphoreType.DMA((6, 2)), pltpu.SemaphoreType.DMA((6, 2)),
            pltpu.SemaphoreType.DMA((5,)), pltpu.SemaphoreType.DMA((5,)),
            vmem(n // 2, quarter, LANES),
        ],
        compiler_params=pltpu.CompilerParams(
            collective_id=0, has_side_effects=True, vmem_limit_bytes=60 * 1024 * 1024),
    )(partials, regions, previous)


def solution(mesh):
    in_specs = (
        P("job", None, "slab", None),
        P(("job", "slab"), None, None),
        P(("job", "slab"), None, None),
    )
    out_specs = P(("job", "slab"), None, None)
    size = mesh.shape["slab"]

    def fits(partials, regions):
        return (size == 16 and partials.shape[2] == 16 * size and partials.shape[1] == 2 * size
                and regions.shape[1] == 16 * size)

    def program(partials, regions, previous):
        chosen = box_local if fits(partials, regions) else local
        return jax.shard_map(chosen, mesh=mesh, in_specs=in_specs, out_specs=out_specs, check_vma=False)(
            partials, regions, previous)

    return program
```

```python
import functools

import jax
import jax.numpy as jnp
from jax import lax
from jax.experimental import pallas as pl
from jax.experimental.pallas import tpu as pltpu
from jax.sharding import PartitionSpec as P

PRE_SWEEPS = 2
POST_SWEEPS = 2
COARSE_SWEEPS = 4

DAMPING = 0.75
INSIDE = 2.0
SOLVENT = 78.4
SCREEN = 1.4
SOURCE = 16.0 * 3.141592653589793

F32 = jnp.float32
LANES = 128


def iota(shape, dim):
    return lax.broadcasted_iota(jnp.int32, shape, dim)


def face(mine, other, spacing):
    return mine * other / ((mine + other) * (0.5 * spacing))


def back(v, dim, by=1):
    return pltpu.roll(v, by, dim)


def ahead(v, dim, by=1):
    return pltpu.roll(v, v.shape[dim] - by, dim)


def terms(v):
    result = []
    for _ in range(3):
        result.append(v.astype(jnp.bfloat16))
        v = v - result[-1].astype(F32)
    return result


def product(a, b):
    return lax.dot_general(a, b, (((1,), (0,)), ((), ())), preferred_element_type=F32)


def times(v, selector):
    high, middle, low = (product(t, selector.astype(jnp.bfloat16)) for t in terms(v))
    return high + (middle + low)


def dot(selector, v):
    high, middle, low = (product(selector.astype(jnp.bfloat16), t) for t in terms(v))
    return high + (middle + low)


def halves(v):
    high = v.astype(jnp.bfloat16)
    return high, (v - high.astype(F32)).astype(jnp.bfloat16)


def times2(v, selector):
    high, low = (product(t, selector.astype(jnp.bfloat16)) for t in halves(v))
    return high + low


def dot2(selector, v):
    high, low = (product(selector.astype(jnp.bfloat16), t) for t in halves(v))
    return high + low


def pool_right(wide, narrow, valid):
    src, dst = iota((wide, narrow), 0), iota((wide, narrow), 1)
    return jnp.where((src // 2 == dst) & (src < valid), 1.0, 0.0).astype(F32)


def pool_left(narrow, wide):
    dst, src = iota((narrow, wide), 0), iota((narrow, wide), 1)
    return jnp.where(src // 2 == dst, 1.0, 0.0).astype(F32)


def spread_right(narrow, wide, valid):
    src, dst = iota((narrow, wide), 0), iota((narrow, wide), 1)
    return jnp.where((dst // 2 == src) & (dst < valid), 1.0, 0.0).astype(F32)


def spread_left(wide, narrow):
    dst, src = iota((wide, narrow), 0), iota((wide, narrow), 1)
    return jnp.where(dst // 2 == src, 1.0, 0.0).astype(F32)


def plane_faces(e, spacing):
    rows, cols = e.shape
    x, y = iota(e.shape, 0), iota(e.shape, 1)
    fx = jnp.where(x > 0, face(e, back(e, 0), spacing), 0.0)
    fy = jnp.where(y > 0, face(e, back(e, 1), spacing), 0.0)
    edges = (jnp.where((x == 0) | (x == rows - 1), 1.0, 0.0)
             + jnp.where((y == 0) | (y == cols - 1), 1.0, 0.0))
    total = fx + ahead(fx, 0) + fy + ahead(fy, 1) + edges * e * (1.0 / spacing)
    return fx, fy, total


def plane_sum(fx, fy, v):
    return fx * back(v, 0) + ahead(fx * v, 0) + fy * back(v, 1) + ahead(fy * v, 1)


def coarse_cycle(e, k, planes, nx, sz, sx, dot, times, pairs=None):
    rows = e.shape[0]
    row, lane = iota(e.shape, 0), iota(e.shape, 1)
    x, z = row % nx, row // nx
    valid = (row < planes * nx) & (lane < nx)
    e = jnp.where(valid, e, 1.0)
    fx = jnp.where(valid & (x > 0), face(e, back(e, 0), sx), 0.0) if nx > 1 else None
    fy = jnp.where(valid & (lane > 0), face(e, back(e, 1), sx), 0.0) if nx > 1 else None
    wrap = nx % rows
    fz = jnp.where(valid & (z > 0), face(e, back(e, 0, wrap), sz), 0.0) if planes > 1 else None
    diag = k + e * (
        (jnp.where(x == 0, 1.0, 0.0) + jnp.where(x == nx - 1, 1.0, 0.0)
         + jnp.where(lane == 0, 1.0, 0.0) + jnp.where(lane == nx - 1, 1.0, 0.0)) * (1.0 / sx)
        + (jnp.where(z == 0, 1.0, 0.0) + jnp.where(z == planes - 1, 1.0, 0.0)) * (1.0 / sz))
    if nx > 1:
        diag = diag + fx + ahead(fx, 0) + fy + ahead(fy, 1)
    if planes > 1:
        diag = diag + fz + ahead(fz, 0, wrap)
    w = jnp.where(valid, DAMPING / jnp.where(valid, diag, 1.0), 0.0)

    def beside(v):
        total = jnp.zeros_like(v)
        if nx > 1:
            total = plane_sum(fx, fy, v)
        if planes > 1:
            total = total + fz * back(v, 0, wrap) + ahead(fz * v, 0, wrap)
        return total

    def sweep(v, b):
        return (1.0 - DAMPING) * v + w * (b + beside(v))

    def coarsest(b):
        v = w * b
        for _ in range(COARSE_SWEEPS - 1):
            v = sweep(v, b)
        return v

    if planes == 1:
        return coarsest
    halve = nx > 1 and nx % 2 == 0
    nx2 = nx // 2 if halve else nx
    sx2 = sx * 4.0 if halve else sx
    step = planes
    while step * nx > 512 and step % 4 == 0:
        step //= 2
    part = step * nx
    if step == planes:
        part = rows
    real2 = planes // 2 * nx2
    rows2 = max(8, real2)
    part2 = rows2 if step == planes else step // 2 * nx2
    ratio = 2 if halve else 1

    def member(fine, coarse):
        return ((fine < step * nx) & ((fine // nx // 2) * nx2 + fine % nx // ratio == coarse))

    down = jnp.where(member(iota((part2, part), 1), iota((part2, part), 0)), 1.0, 0.0)
    up = jnp.where(member(iota((part, part2), 0), iota((part, part2), 1)), 1.0, 0.0)
    if halve:
        right = pool_right(LANES, LANES, nx)
        left = spread_right(LANES, LANES, nx)
        scale = 0.125
    else:
        scale = 0.5

    def coarsen(f):
        if pairs is not None:
            f = jnp.sum(f.reshape(planes // 2, 2, nx, LANES), axis=1).reshape(planes // 2 * nx, LANES)
            return scale * times(pairs[0](f), right)
        if halve:
            f = times(f, right)
        parts = [dot(down, f[i:i + part]) for i in range(0, rows, part)]
        return scale * (parts[0] if len(parts) == 1 else jnp.concatenate(parts, axis=0))

    def refine(f):
        if pairs is not None:
            f = pairs[1](times(f, left)).reshape(planes // 2, 1, nx, LANES)
            return jnp.broadcast_to(f, (planes // 2, 2, nx, LANES)).reshape(planes * nx, LANES)
        if halve:
            f = times(f, left)
        parts = [dot(up, f[i:i + part2]) for i in range(0, rows2, part2)]
        return parts[0] if len(parts) == 1 else jnp.concatenate(parts, axis=0)

    below = coarse_cycle(coarsen(jnp.where(valid, e, 0.0)), coarsen(k),
                         planes // 2, nx2, sz * 4.0, sx2, dot, times, pairs)

    def run(b):
        v = w * b
        for _ in range(PRE_SWEEPS - 1):
            v = sweep(v, b)
        r = jnp.where(valid, b - diag * v + beside(v), 0.0)
        v = v + refine(below(coarsen(r)))
        for _ in range(POST_SWEEPS):
            v = sweep(v, b)
        return v

    return run


REG, V0, V1, V2, BASE, FAR = range(6)
E1, A1, A2, A3, A4, TERM = range(6)


def kernel(n, partials, regions, previous, out,
           dens, got, b0, fx0, fy0, fz0, dg0, wt0, halo_reg, far_reg, fxh, fyh, fzh, wth, halo0, v1, v2, base,
           halo1, plane1, term1, gb, gk,
           big_send, big_recv, small_send, small_recv, many_send, many_recv, c2_planes):
    me = lax.axis_index("slab")
    job = lax.axis_index("job")
    nxy = regions.shape[1]
    half = nxy // 2
    quarter = nxy // 4
    rows = partials.shape[2]
    has_lo, has_hi = me > 0, me < n - 1

    def peer(index):
        return {"slab": index}

    barrier = pltpu.get_barrier_semaphore()

    def greet(off, carry):
        pl.semaphore_signal(barrier, inc=1, device_id=peer(lax.rem(me + off, n)),
                            device_id_type=pl.DeviceIdType.MESH)
        return carry

    lax.fori_loop(1, n, greet, 0)

    @pl.when(jnp.logical_not(has_lo))
    def _():
        for i in range(4):
            halo0[i, 0] = jnp.zeros((nxy, nxy), F32)
        for i in range(6):
            halo1[i, 0] = jnp.zeros((half, half), F32)
        halo_reg[0] = jnp.zeros((nxy, nxy), jnp.int32)
        far_reg[0] = jnp.zeros((nxy, nxy), jnp.int32)

    @pl.when(jnp.logical_not(has_hi))
    def _():
        for i in range(4):
            halo0[i, 1] = jnp.zeros((nxy, nxy), F32)
        for i in range(6):
            halo1[i, 1] = jnp.zeros((half, half), F32)
        halo_reg[1] = jnp.zeros((nxy, nxy), jnp.int32)
        far_reg[1] = jnp.zeros((nxy, nxy), jnp.int32)

    density = partials[0].astype(F32)
    for g in range(1, partials.shape[0]):
        density = density + partials[g].astype(F32)
    dens[...] = (SOURCE * density).reshape(dens.shape)

    pl.semaphore_wait(barrier, n - 1)

    def copies(first, last, dst, sends, recvs, i):
        to_lo = pltpu.make_async_remote_copy(
            src_ref=first, dst_ref=dst.at[1], send_sem=sends.at[i, 0], recv_sem=recvs.at[i, 1],
            device_id=peer(jnp.maximum(me - 1, 0)), device_id_type=pl.DeviceIdType.MESH)
        to_hi = pltpu.make_async_remote_copy(
            src_ref=last, dst_ref=dst.at[0], send_sem=sends.at[i, 1], recv_sem=recvs.at[i, 0],
            device_id=peer(jnp.minimum(me + 1, n - 1)), device_id_type=pl.DeviceIdType.MESH)

        def start():
            pl.when(has_lo)(to_lo.start)
            pl.when(has_hi)(to_hi.start)

        def recv():
            pl.when(has_lo)(to_hi.wait_recv)
            pl.when(has_hi)(to_lo.wait_recv)

        def sent():
            pl.when(has_lo)(to_lo.wait_send)
            pl.when(has_hi)(to_hi.wait_send)

        return start, recv, sent

    pending = []

    def launch(first, last, dst, sends, recvs, i):
        start, recv, sent = copies(first, last, dst, sends, recvs, i)
        start()
        pending.append(sent)
        return recv

    recv_reg = launch(regions.at[0], regions.at[1], halo_reg, big_send, big_recv, REG)
    recv_v0 = launch(previous.at[0], previous.at[1], halo0.at[0], big_send, big_recv, V0)

    def scatter(step, carry):
        other = lax.rem(me + 1 + lax.rem(step + n // 2 - 1, n - 1), n)
        pltpu.make_async_remote_copy(
            src_ref=dens.at[other], dst_ref=got.at[me], send_sem=many_send.at[0],
            recv_sem=many_recv.at[0], device_id=peer(other),
            device_id_type=pl.DeviceIdType.MESH).start()
        return carry

    lax.fori_loop(0, n - 1, scatter, 0)

    def dielectric(r):
        return jnp.where(r == 0, INSIDE, SOLVENT).astype(F32)

    e = [dielectric(regions[p]) for p in range(2)]
    k = [jnp.where(regions[p] == 2, SCREEN, 0.0).astype(F32) for p in range(2)]
    right0, left0 = pool_right(nxy, half, nxy), pool_left(half, nxy)
    right1, left1 = pool_right(half, LANES, half), pool_left(quarter, half)

    def down0(a, b):
        return 0.125 * dot(left0, times(a + b, right0))

    def down1(a):
        return 0.25 * dot(left1, times(a, right1))

    e1, k1 = down0(e[0], e[1]), down0(k[0], k[1])
    plane1[E1] = e1
    recv_e1 = launch(plane1.at[E1], plane1.at[E1], halo1.at[E1], small_send, small_recv, E1)
    core, chip = lax.rem(me, 2), me // 2
    gk[core, chip] = down1(e1) + back(down1(k1), 1, LANES // 2)

    def share(ref, i):
        def one(off, carry):
            other = lax.rem(me + 2 * off, n)
            pltpu.make_async_remote_copy(
                src_ref=ref.at[core, chip], dst_ref=ref.at[core, chip], send_sem=many_send.at[i],
                recv_sem=many_recv.at[i], device_id=peer(other),
                device_id_type=pl.DeviceIdType.MESH).start()
            return carry

        lax.fori_loop(1, n // 2, one, 0)

    def relay(ref, i):
        window = ref.at[0, pl.ds(0, n // 2 - 1)]
        pltpu.make_async_copy(window, window, many_recv.at[i]).wait()
        copy = pltpu.make_async_remote_copy(
            src_ref=ref.at[core], dst_ref=ref.at[core], send_sem=many_send.at[i + 2],
            recv_sem=many_recv.at[i + 2], device_id=peer(me + 1 - 2 * core),
            device_id_type=pl.DeviceIdType.MESH)
        copy.start()
        pending.append(pltpu.make_async_copy(window, window, many_send.at[i]).wait)
        pending.append(copy.wait_send)
        return copy.wait_recv

    def all_in(ref, sems, i):
        window = ref.at[pl.ds(0, n - 1)]
        pltpu.make_async_copy(window, window, sems.at[i]).wait()

    share(gk, 1)

    totals = []
    middle = face(e[0], e[1], 1.0)
    fz0[1] = middle
    part = []
    for p in range(2):
        fx, fy, total = plane_faces(e[p], 1.0)
        fx0[p] = fx
        fy0[p] = fy
        totals.append(total + middle + k[p])
        part.append(plane_sum(fx, fy, previous[p]) + middle * previous[1 - p])
    recv_reg()
    e_side = [jnp.where(has_lo, dielectric(halo_reg[0]), e[0]),
              jnp.where(has_hi, dielectric(halo_reg[1]), e[1])]
    for p in range(2):
        outer = face(e_side[p], e[p], 1.0)
        fz0[2 * p] = outer
        total = totals[p] + outer
        dg0[p] = total
        wt0[p] = DAMPING / total

    def beside0(p, mine, below, above):
        return plane_sum(fx0[p], fy0[p], mine) + fz0[p] * below + fz0[p + 1] * above

    def sweep0(p, mine, below, above):
        return (1.0 - DAMPING) * mine + wt0[p] * (b0[p] + beside0(p, mine, below, above))

    recv_v0()
    for p in range(2):
        v1[p] = (1.0 - DAMPING) * previous[p] + wt0[p] * (part[p] + fz0[2 * p] * halo0[0, p])

    got[me] = dens[me]
    all_in(got, many_recv, 0)
    for p in range(2):
        if rows % 8 == 0:
            b0[p] = got[:, p].reshape(nxy, nxy)
        else:
            for s in range(n):
                b0[p, s * rows:(s + 1) * rows, :] = got[s, p]
    for p in range(2):
        v1[p] = v1[p] + wt0[p] * b0[p]
    recv = launch(v1.at[0], v1.at[1], halo0.at[1], big_send, big_recv, V1)
    recv_gk = relay(gk, 1)
    recv_e1()
    sz1 = sx1 = 4.0
    fx1, fy1, total1 = plane_faces(e1, sx1)
    fz1lo = face(jnp.where(has_lo, halo1[E1, 0], e1), e1, sz1)
    fz1hi = face(jnp.where(has_hi, halo1[E1, 1], e1), e1, sz1)
    dg1 = total1 + fz1lo + fz1hi + k1
    wt1 = DAMPING / dg1

    recv()
    v2[0] = sweep0(0, v1[0], halo0[1, 0], v1[1])
    v2[1] = sweep0(1, v1[1], v1[0], halo0[1, 1])
    term1[0] = 0.125 * dot(left0, times(fz0[0] * v2[0], right0))
    term1[1] = 0.125 * dot(left0, times(fz0[2] * v2[1], right0))
    recv_term = launch(term1.at[0], term1.at[1], halo1.at[TERM], small_send, small_recv, TERM)
    recv_v2 = launch(v2.at[0], v2.at[1], halo0.at[2], big_send, big_recv, V2)
    r0 = b0[0] - dg0[0] * v2[0] + plane_sum(fx0[0], fy0[0], v2[0]) + fz0[1] * v2[1]
    r1 = b0[1] - dg0[1] * v2[1] + plane_sum(fx0[1], fy0[1], v2[1]) + fz0[1] * v2[0]
    b1 = down0(r0, r1)
    recv_far = launch(regions.at[1], regions.at[0], far_reg, big_send, big_recv, FAR)
    recv_gk()
    e2 = 0.5 * (gk[0] + gk[1]).reshape(n // 2 * quarter, LANES)
    k2 = back(e2, 1, LANES // 2)
    coarse = coarse_cycle(e2, k2, n // 2, quarter, 16.0, 16.0, dot, times)
    recv_term()
    b1 = b1 + halo1[TERM, 0] + halo1[TERM, 1]

    def beside1(mine, i):
        return plane_sum(fx1, fy1, mine) + fz1lo * halo1[i, 0] + fz1hi * halo1[i, 1]

    def trade1(value, i):
        plane1[i] = value
        launch(plane1.at[i], plane1.at[i], halo1.at[i], small_send, small_recv, i)()

    a = wt1 * b1
    trade1(a, A1)
    a = (1.0 - DAMPING) * a + wt1 * (b1 + beside1(a, A1))
    trade1(a, A2)
    full = down1(b1 - dg1 * a + beside1(a, A2))
    gb[core, chip] = full[:quarter // 2] + back(full[quarter // 2:], 1, LANES // 2)
    share(gb, 2)
    recv_v2()
    base[0] = sweep0(0, v2[0], halo0[2, 0], v2[1])
    base[1] = sweep0(1, v2[1], v2[0], halo0[2, 1])
    recv_base = launch(base.at[0], base.at[1], halo0.at[3], big_send, big_recv, BASE)
    relay_gb = relay(gb, 2)
    recv_far()
    for p in range(2):
        region = halo_reg[p]
        beyond = face(e_side[p], dielectric(far_reg[p]), 1.0)
        fx, fy, total = plane_faces(e_side[p], 1.0)
        fxh[p] = fx
        fyh[p] = fy
        fzh[p] = beyond
        wth[p] = DAMPING / (total + beyond + fz0[2 * p] + jnp.where(region == 2, SCREEN, 0.0))
    relay_gb()
    packed = 0.5 * (gb[0] + gb[1]).reshape(n // 2 * quarter // 2, LANES)
    split = (n // 2, quarter // 2, LANES)
    b2 = jnp.concatenate(
        [packed.reshape(split), back(packed, 1, LANES // 2).reshape(split)], axis=1
    ).reshape(n // 2 * quarter, LANES)
    c2 = coarse(b2)

    for i in range(n // 2):
        c2_planes[i] = c2[i * quarter:(i + 1) * quarter]
    grow_l, grow_r = spread_left(half, quarter), spread_right(LANES, half, half)

    def up1(index):
        return dot(grow_l, times(c2_planes[index // 2], grow_r))

    halo1[A2, 0] = halo1[A2, 0] + jnp.where(has_lo, up1(jnp.maximum(me - 1, 0)), 0.0)
    halo1[A2, 1] = halo1[A2, 1] + jnp.where(has_hi, up1(jnp.minimum(me + 1, n - 1)), 0.0)
    a = a + up1(me)
    a = (1.0 - DAMPING) * a + wt1 * (b1 + beside1(a, A2))
    trade1(a, A3)
    a = (1.0 - DAMPING) * a + wt1 * (b1 + beside1(a, A3))
    trade1(a, A4)

    big_l, big_r = spread_left(nxy, half), spread_right(half, nxy, nxy)

    def up0(c):
        return dot(big_l, times(c, big_r))

    mine = up0(a)
    recv_base()
    v3, side = [], []
    present = [has_lo, has_hi]
    for p in range(2):
        c = up0(halo1[A4, p])
        own = plane_sum(fx0[p], fy0[p], mine) + fz0[1] * mine + fz0[2 * p] * c
        v3.append(base[p] + (1.0 - DAMPING) * mine + wt0[p] * own)
        other = plane_sum(fxh[p], fyh[p], c) + fzh[p] * c + fz0[2 * p] * mine
        swept = halo0[3, p] + (1.0 - DAMPING) * c + wth[p] * other
        side.append(jnp.where(present[p], swept, 0.0))
    out[0] = sweep0(0, v3[0], side[0], v3[1])
    out[1] = sweep0(1, v3[1], v3[0], side[1])

    for sent in pending:
        sent()
    all_in(got, many_send, 0)


HALO = 16
REG_LO, REG_HI, V0_LO, V0_HI, V1_LO, V1_HI, V2_LO, V2_HI, BASE_LO, BASE_HI = range(10)
E_M1, E_P1, E_M2, E_P2, K_M1, K_P1, B_M1, B_P1, B_M2, B_P2, A2_LO, A2_HI, NEAR, NEAR_CORE, FAR_LO, FAR_HI = range(10, 26)
MESSAGES = 26


def box_kernel(n, partials, regions, previous, out,
               parts, dens, reg, v0, b0, fx0, fy0, fz0, dg0, wt0, v1, v2, base, swept,
               near, fxn, fyn, fzn, wtn, landed, corr,
               e1, k1, fx1, fy1, fz1, dg1, wt1, pack, from_lo, from_hi, far_lo, far_hi,
               b1, a1, a2, a2c, a3, a4, gk, gb, c2_planes, rows_tmp,
               load_sem, spread_send, spread_recv, corr_send, corr_recv, dens_send, dens_recv,
               side_send, side_recv, many_send, many_recv):
    me = lax.axis_index("slab")
    nz = n // 2
    z, x, core = me // 4, lax.rem(me // 2, 2), lax.rem(me, 2)
    zi = 2 * z + core
    nxy = regions.shape[1]
    half, quarter = nxy // 2, nxy // 4
    rows = partials.shape[2]
    window = half + HALO
    window1 = window // 2
    blocks = window // rows
    first = half - HALO

    def peer(index):
        return {"slab": index}

    def at(i, j):
        return (i // 2) * 4 + j * 2 + lax.rem(i, 2)

    load = pltpu.make_async_copy(partials, parts, load_sem.at[0])
    load.start()
    load_near = pltpu.make_async_copy(regions, near.at[pl.ds(2, 2)], load_sem.at[1])
    load_near.start()
    barrier = pltpu.get_barrier_semaphore()

    def greet(off, carry):
        pl.semaphore_signal(barrier, inc=1, device_id=peer(lax.rem(me + off, n)),
                            device_id_type=pl.DeviceIdType.MESH)
        return carry

    lax.fori_loop(1, n, greet, 0)

    plane0 = jnp.zeros((window, nxy), F32)
    plane1 = jnp.zeros((window1, half), F32)

    @pl.when(zi == 0)
    def _():
        for i in range(2):
            reg[i] = jnp.zeros((window, nxy), jnp.int32)
        for v in (v0, v1, v2, base):
            v[0] = plane0
        for i in range(3):
            from_lo[i] = plane1
        for i in range(2):
            e1[i] = plane1 + 1.0
            k1[i] = plane1
        a2[0] = plane1

    @pl.when(zi == nz - 1)
    def _():
        for i in range(2):
            reg[6 + i] = jnp.zeros((window, nxy), jnp.int32)
        for v in (v0, v1, v2, base):
            v[5] = plane0
        for i in range(3):
            from_hi[i] = plane1
        for i in range(2):
            e1[6 + i] = plane1 + 1.0
            k1[4 + i] = plane1
        a2[5] = plane1

    @pl.when(zi < 2)
    def _():
        far_lo[0] = plane1

    @pl.when(zi >= nz - 2)
    def _():
        far_hi[0] = plane1

    @pl.when(me == 0)
    def _():
        corr[0] = jnp.zeros((half, half), F32)

    @pl.when(me == n - 1)
    def _():
        corr[2] = jnp.zeros((half, half), F32)

    load.wait()
    density = parts[0].astype(F32)
    for g in range(1, partials.shape[0]):
        density = density + parts[g].astype(F32)
    dens[...] = (SOURCE * density).reshape(dens.shape)

    pl.semaphore_wait(barrier, n - 1)
    pending = []

    def spread(src, dst, mine, first_slot, step, i):
        for j in range(2):
            target = at(2 * z + x, j)
            piece = src.at[pl.ds(mine, 1), pl.ds(first * j, window), :]
            place = dst.at[pl.ds(first_slot + step * core, 1)]
            remote = pltpu.make_async_remote_copy(
                src_ref=piece, dst_ref=place, send_sem=spread_send.at[i, j],
                recv_sem=spread_recv.at[i, core], device_id=peer(target),
                device_id_type=pl.DeviceIdType.MESH)
            here = pltpu.make_async_copy(piece, place, spread_recv.at[i, core])
            away = target != me
            pl.when(away)(remote.start)
            pl.when(jnp.logical_not(away))(here.start)
            pending.append(lambda remote=remote, away=away: pl.when(away)(remote.wait_send))

        def arrived():
            for j in range(2):
                place = dst.at[pl.ds(first_slot + step * j, 1)]
                pltpu.make_async_copy(place, place, spread_recv.at[i, j]).wait()

        return arrived

    def send_density(step, carry):
        other = lax.rem(me + 1 + lax.rem(step + n // 2 - 1, n), n)
        oz, ox = 2 * (other // 4) + lax.rem(other, 2), lax.rem(other // 2, 2)
        block = me - (first // rows) * ox
        inside = (block >= 0) & (block < blocks)
        block = jnp.clip(block, 0, blocks - 1)
        place = b0.at[:, pl.ds(pl.multiple_of(block * rows, rows), rows), :]

        @pl.when(inside & (other != me))
        def _():
            pltpu.make_async_remote_copy(
                src_ref=dens.at[oz], dst_ref=place, send_sem=dens_send.at[other],
                recv_sem=dens_recv.at[0], device_id=peer(other),
                device_id_type=pl.DeviceIdType.MESH).start()

        @pl.when(inside & (other == me))
        def _():
            pltpu.make_async_copy(dens.at[oz], place, dens_recv.at[0]).start()

        return carry

    def sent_density(other, carry):
        ox = lax.rem(other // 2, 2)
        block = me - (first // rows) * ox

        @pl.when((block >= 0) & (block < blocks) & (other != me))
        def _():
            pltpu.make_async_copy(dens.at[0], dens.at[0], dens_send.at[other]).wait()

        return carry

    deferred = []
    soon = core == x

    def push(src, dst, delta, i, split=False):
        can_send = (zi + delta >= 0) & (zi + delta < nz)
        can_recv = (zi - delta >= 0) & (zi - delta < nz)
        copy = pltpu.make_async_remote_copy(
            src_ref=src, dst_ref=dst, send_sem=side_send.at[i], recv_sem=side_recv.at[i],
            device_id=peer(at(jnp.clip(zi + delta, 0, nz - 1), x)),
            device_id_type=pl.DeviceIdType.MESH)
        pl.when(can_send & soon if split else can_send)(copy.start)
        if split:
            deferred.append(lambda: pl.when(can_send & jnp.logical_not(soon))(copy.start))
        pending.append(lambda: pl.when(can_send)(copy.wait_send))
        return lambda: pl.when(can_recv)(copy.wait_recv)

    def trade(field, low, high, i):
        down = push(field.at[low], field.at[high + 1], -1, i)
        up = push(field.at[high], field.at[low - 1], 1, i + 1)

        def arrived():
            down()
            up()

        return arrived

    lax.fori_loop(0, n, send_density, 0)
    reg_edge = spread(regions, reg, core, 2, 3, 0)
    v0_edge = spread(previous, v0, core, 1, 3, 1)
    reg_in = spread(regions, reg, 1 - core, 3, 1, 3)
    v0_in = spread(previous, v0, 1 - core, 2, 1, 4)

    def dielectric(r):
        return jnp.where(r == 0, INSIDE, SOLVENT).astype(F32)

    right0 = pool_right(nxy, half, nxy)
    right1 = pool_right(half, LANES, half)
    dst1, src1 = iota((quarter // 2, window1), 0), iota((quarter // 2, window1), 1)
    left1 = jnp.where((src1 - (HALO // 2) * x) // 2 == dst1, 1.0, 0.0).astype(F32)

    turn = [0]

    def strips(v):
        return [v[:, i:i + LANES] for i in range(0, v.shape[1], LANES)]

    def scratch():
        turn[0] = (turn[0] + 1) % 8
        return rows_tmp.at[turn[0]]

    def pool_rows(v):
        count = v.shape[0] // 2
        done = []
        for strip in strips(v):
            tmp = scratch()
            tmp[:2 * count] = strip
            done.append(tmp[pl.ds(0, count, stride=2), :] + tmp[pl.ds(1, count, stride=2), :])
        return done[0] if len(done) == 1 else jnp.concatenate(done, axis=1)

    def grow_rows(v):
        count = v.shape[0]
        done = []
        for strip in strips(v):
            tmp = scratch()
            tmp[pl.ds(0, count, stride=2), :] = strip
            tmp[pl.ds(1, count, stride=2), :] = strip
            done.append(tmp[:2 * count])
        return done[0] if len(done) == 1 else jnp.concatenate(done, axis=1)

    def down0(a):
        return 0.125 * times2(pool_rows(a), right0)

    def down1(a):
        return 0.125 * dot2(left1, times2(a, right1))

    reg_edge()
    reg_halo = trade(reg, 2, 5, REG_LO)
    v0_edge()
    v0_halo = trade(v0, 1, 4, V0_LO)
    reg_in()
    far_in = [push(reg.at[3], reg.at[7], -1, FAR_LO), push(reg.at[4], reg.at[0], 1, FAR_HI)]
    e = [dielectric(reg[p]) for p in range(2, 6)]
    k = [jnp.where(reg[p] == 2, SCREEN, 0.0).astype(F32) for p in range(2, 6)]
    for i in range(2):
        e1[3 + i] = down0(e[2 * i] + e[2 * i + 1])
        k1[2 + i] = down0(k[2 * i] + k[2 * i + 1])
    e1_in = [push(e1.at[pl.ds(3, 2)], e1.at[pl.ds(1, 2)], 1, E_P1, True),
             push(e1.at[pl.ds(3, 2)], e1.at[pl.ds(5, 2)], -1, E_M1, True),
             push(e1.at[pl.ds(4, 1)], e1.at[pl.ds(0, 1)], 2, E_P2, True),
             push(e1.at[pl.ds(3, 1)], e1.at[pl.ds(7, 1)], -2, E_M2, True),
             push(k1.at[pl.ds(2, 2)], k1.at[pl.ds(0, 2)], 1, K_P1, True),
             push(k1.at[pl.ds(2, 2)], k1.at[pl.ds(4, 2)], -1, K_M1, True)]
    chip = me // 2
    gk[core, x, z] = down1(e1[3] + e1[4]) + back(down1(k1[2] + k1[3]), 1, LANES // 2)

    def share(ref, i):
        def one(off, carry):
            other = lax.rem(me + 2 * off, n)
            pltpu.make_async_remote_copy(
                src_ref=ref.at[core, chip], dst_ref=ref.at[core, chip], send_sem=many_send.at[i],
                recv_sem=many_recv.at[i], device_id=peer(other),
                device_id_type=pl.DeviceIdType.MESH).start()
            return carry

        lax.fori_loop(1, n // 2, one, 0)

    def relay(ref, i):
        seven = ref.at[0, pl.ds(0, n // 2 - 1)]
        pltpu.make_async_copy(seven, seven, many_recv.at[i]).wait()
        copy = pltpu.make_async_remote_copy(
            src_ref=ref.at[core], dst_ref=ref.at[core], send_sem=many_send.at[i + 2],
            recv_sem=many_recv.at[i + 2], device_id=peer(me + 1 - 2 * core),
            device_id_type=pl.DeviceIdType.MESH)
        copy.start()
        pending.append(pltpu.make_async_copy(seven, seven, many_send.at[i]).wait)
        pending.append(copy.wait_send)
        return copy.wait_recv

    def in_order(ref):
        return [ref[c, 2 * i + j] for i in range(n // 4) for c in range(2) for j in range(2)]

    columns = n // 4

    def along(off, carry):
        other = lax.rem(me + 4 * off, n)
        pltpu.make_async_remote_copy(
            src_ref=gk.at[core, x, z], dst_ref=gk.at[core, x, z], send_sem=many_send.at[0],
            recv_sem=many_recv.at[0], device_id=peer(other),
            device_id_type=pl.DeviceIdType.MESH).start()
        return carry

    lax.fori_loop(1, columns, along, 0)

    def gk_over():
        others = gk.at[0, 0, pl.ds(0, columns - 1)]
        pltpu.make_async_copy(others, others, many_recv.at[0]).wait()
        copy = pltpu.make_async_remote_copy(
            src_ref=gk.at[core, x], dst_ref=gk.at[core, x], send_sem=many_send.at[4],
            recv_sem=many_recv.at[4], device_id=peer(at(zi, 1 - x)),
            device_id_type=pl.DeviceIdType.MESH)
        copy.start()
        pending.append(pltpu.make_async_copy(others, others, many_send.at[0]).wait)
        pending.append(copy.wait_send)
        return copy.wait_recv

    def gk_beside():
        copy = pltpu.make_async_remote_copy(
            src_ref=gk.at[core], dst_ref=gk.at[core], send_sem=many_send.at[2],
            recv_sem=many_recv.at[2], device_id=peer(at(zi + 1 - 2 * core, x)),
            device_id_type=pl.DeviceIdType.MESH)
        copy.start()
        pending.append(copy.wait_send)
        return copy.wait_recv

    totals = []
    for p in range(4):
        fx, fy, total = plane_faces(e[p], 1.0)
        fx0[p] = fx
        fy0[p] = fy
        totals.append(total + k[p])
    for p in range(1, 4):
        fz0[p] = face(e[p - 1], e[p], 1.0)

    def beside0(p, v):
        return (plane_sum(fx0[p], fy0[p], v[p + 1]) + fz0[p] * v[p] + fz0[p + 1] * v[p + 2])

    def sweep0(p, v):
        return (1.0 - DAMPING) * v[p + 1] + wt0[p] * (b0[p] + beside0(p, v))

    def first_part(p):
        v1[p + 1] = (1.0 - DAMPING) * v0[p + 1] + wt0[p] * beside0(p, v0)

    def weights(p):
        diag = totals[p] + fz0[p] + fz0[p + 1]
        dg0[p] = diag
        wt0[p] = DAMPING / diag

    reg_halo()
    fz0[0] = face(jnp.where(zi > 0, dielectric(reg[1]), e[0]), e[0], 1.0)
    fz0[4] = face(e[3], jnp.where(zi < nz - 1, dielectric(reg[6]), e[3]), 1.0)
    weights(0)
    weights(3)
    v0_in()
    v0_halo()
    first_part(0)
    first_part(3)

    pltpu.make_async_copy(b0, b0, dens_recv.at[0]).wait()
    for p in (0, 3):
        v1[p + 1] = v1[p + 1] + wt0[p] * b0[p]
    v1_halo = trade(v1, 1, 4, V1_LO)
    for start in deferred:
        start()
    for arrived in far_in:
        arrived()
    own_rows = pl.ds(pl.multiple_of(HALO * x, HALO), half)

    def near_rows(j):
        return near.at[pl.ds(4 * core, 2), pl.ds(pl.multiple_of(half * j, half), half), :]

    across = pltpu.make_async_remote_copy(
        src_ref=reg.at[pl.ds(4 + 2 * core - 4 * x, 2), own_rows, :], dst_ref=near_rows(x),
        send_sem=side_send.at[NEAR], recv_sem=side_recv.at[NEAR], device_id=peer(at(zi, 1 - x)),
        device_id_type=pl.DeviceIdType.MESH)
    beside = pltpu.make_async_remote_copy(
        src_ref=regions, dst_ref=near.at[pl.ds(4 * core, 2)], send_sem=side_send.at[NEAR_CORE],
        recv_sem=side_recv.at[NEAR_CORE], device_id=peer(at(zi + 1 - 2 * core, x)),
        device_id_type=pl.DeviceIdType.MESH)
    within = pltpu.make_async_copy(reg.at[pl.ds(2 * core + 4 * x, 2), own_rows, :], near_rows(x),
                                   load_sem.at[2])
    for copy in (across, beside, within):
        copy.start()
    pending.append(across.wait_send)
    pending.append(beside.wait_send)
    gk_across = gk_over()

    for p in (1, 2):
        weights(p)
        first_part(p)
        v1[p + 1] = v1[p + 1] + wt0[p] * b0[p]

    for p in (1, 2):
        v2[p + 1] = sweep0(p, v1)
    v1_halo()
    for p in (0, 3):
        v2[p + 1] = sweep0(p, v1)
    v2_halo = trade(v2, 1, 4, V2_LO)
    pack[0] = down0(fz0[4] * v2[4])
    pack[3] = down0(fz0[0] * v2[1])
    edge_in = [push(pack.at[pl.ds(0, 1)], far_lo, 2, B_P2),
               push(pack.at[pl.ds(3, 1)], far_hi, -2, B_M2)]

    def left_over(p):
        r = b0[p] - dg0[p] * v2[p + 1] + plane_sum(fx0[p], fy0[p], v2[p + 1])
        if p > 0:
            r = r + fz0[p] * v2[p]
        if p < 3:
            r = r + fz0[p + 1] * v2[p + 2]
        return r

    for i in range(2):
        pack[1 + i] = down0(left_over(2 * i) + left_over(2 * i + 1))
    b1_in = [push(pack.at[pl.ds(0, 3)], from_lo, 1, B_P1),
             push(pack.at[pl.ds(1, 3)], from_hi, -1, B_M1)] + edge_in
    for arrived in e1_in:
        arrived()

    @pl.when(zi == 0)
    def _():
        e1[2] = e1[3]
        e1[0] = plane1 + 1.0

    @pl.when(zi == 1)
    def _():
        e1[0] = e1[1]

    @pl.when(zi == nz - 1)
    def _():
        e1[5] = e1[4]
        e1[7] = plane1 + 1.0

    @pl.when(zi == nz - 2)
    def _():
        e1[7] = e1[6]

    s1 = 4.0
    for i in range(7):
        fz1[i] = face(e1[i], e1[i + 1], s1)
    for i in range(6):
        fx, fy, total = plane_faces(e1[i + 1], s1)
        fx1[i] = fx
        fy1[i] = fy
        diag = total + fz1[i] + fz1[i + 1] + k1[i]
        dg1[i] = diag
        weight = DAMPING / diag
        if i < 2:
            weight = jnp.where(zi > 0, weight, 0.0)
        if i > 3:
            weight = jnp.where(zi < nz - 1, weight, 0.0)
        wt1[i] = weight

    v2_halo()
    for p in (0, 3, 1, 2):
        base[p + 1] = sweep0(p, v2)
    base_halo = trade(base, 1, 4, BASE_LO)
    for arrived in b1_in:
        arrived()
    b1[0] = from_lo[1] + far_lo[0]
    b1[1] = from_lo[2] + pack[3]
    b1[2] = pack[1] + from_lo[0]
    b1[3] = pack[2] + from_hi[2]
    b1[4] = from_hi[0] + pack[0]
    b1[5] = from_hi[1] + far_hi[0]

    def beside1(i, mine, below, above):
        return plane_sum(fx1[i], fy1[i], mine) + fz1[i] * below + fz1[i + 1] * above

    def sweep1(i, mine, below, above):
        return (1.0 - DAMPING) * mine + wt1[i] * (b1[i] + beside1(i, mine, below, above))

    for i in range(6):
        a1[i] = wt1[i] * b1[i]
    for i in range(1, 5):
        a2[i] = sweep1(i, a1[i], a1[i - 1], a1[i + 1])
    rest = [b1[i] - dg1[i] * a2[i] + beside1(i, a2[i], a2[i - 1], a2[i + 1]) for i in (2, 3)]
    full = down1(rest[0] + rest[1])
    gb[core, chip] = full[:quarter // 4] + back(full[quarter // 4:], 1, LANES // 2)
    share(gb, 1)
    a2_in = [push(a2.at[2], a2.at[0], 1, A2_HI), push(a2.at[3], a2.at[5], -1, A2_LO)]
    gk_across()
    gk_in = gk_beside()
    gk_in()
    e2 = jnp.concatenate([gk[i, j, m] for m in range(n // 4) for i in range(2) for j in range(2)], axis=0)
    coarse = coarse_cycle(e2, back(e2, 1, LANES // 2), nz, quarter, 16.0, 16.0,
                          dot2, times2, (pool_rows, grow_rows))
    base_halo()

    def deliver(j):
        target = 4 * z + 2 * core + j
        piece = swept.at[pl.ds(2 * j, 2), pl.ds(pl.multiple_of(HALO * x, HALO), half), :]
        place = landed.at[:, pl.ds(pl.multiple_of(half * x, half), half), :]
        remote = pltpu.make_async_remote_copy(
            src_ref=piece, dst_ref=place, send_sem=spread_send.at[2, j],
            recv_sem=spread_recv.at[2, x], device_id=peer(target),
            device_id_type=pl.DeviceIdType.MESH)
        here = pltpu.make_async_copy(piece, place, spread_recv.at[2, x])
        away = target != me
        pl.when(away)(remote.start)
        pl.when(jnp.logical_not(away))(here.start)
        pending.append(lambda: pl.when(away)(remote.wait_send))

    for p in range(4):
        swept[p] = sweep0(p, base)
        if p % 2:
            deliver(p // 2)
    gb_in = relay(gb, 1)
    gb_in()
    packed = jnp.stack(in_order(gb))
    b2 = jnp.concatenate([packed, back(packed.reshape(-1, LANES), 1, LANES // 2).reshape(packed.shape)],
                         axis=1).reshape(nz * quarter, LANES)
    c2 = coarse(b2)
    for i in range(nz):
        c2_planes[i] = c2[i * quarter:(i + 1) * quarter]
    fine, mid = iota((window1, quarter), 0), iota((window1, quarter), 1)
    grow_l = jnp.where((fine + first // 2 * x) // 2 == mid, 1.0, 0.0).astype(F32)
    grow_r = spread_right(LANES, half, half)

    def up1(index):
        return dot2(grow_l, times2(c2_planes[index], grow_r))


    for arrived in a2_in:
        arrived()
    mine = up1(zi)
    lower = jnp.where(zi > 0, up1(jnp.maximum(zi - 1, 0)), 0.0)
    upper = jnp.where(zi < nz - 1, up1(jnp.minimum(zi + 1, nz - 1)), 0.0)
    for i, c in enumerate((lower, lower, mine, mine, upper, upper)):
        a2c[i] = a2[i] + c
    for i in range(1, 5):
        a3[i - 1] = sweep1(i, a2c[i], a2c[i - 1], a2c[i + 1])
    for i in (1, 2):
        a4[i] = sweep1(i + 1, a3[i], a3[i - 1], a3[i + 1])

    def hand(count, low, delta, slot, i):
        target = 2 * zi + delta
        exists = (target >= 0) & (target < n)
        piece = a4.at[pl.ds(low, count), pl.ds(pl.multiple_of(HALO // 2 * x, HALO // 2), quarter), :]
        place = corr.at[pl.ds(slot, count), pl.ds(pl.multiple_of(quarter * x, quarter), quarter), :]
        kind = 2 - count
        remote = pltpu.make_async_remote_copy(
            src_ref=piece, dst_ref=place, send_sem=corr_send.at[i], recv_sem=corr_recv.at[kind, x],
            device_id=peer(jnp.clip(target, 0, n - 1)), device_id_type=pl.DeviceIdType.MESH)
        here = pltpu.make_async_copy(piece, place, corr_recv.at[kind, x])
        away = exists & (target != me)
        pl.when(away)(remote.start)
        pl.when(target == me)(here.start)
        pending.append(lambda: pl.when(away)(remote.wait_send))

    hand(2, 1, 0, 1, 0)
    hand(2, 1, 1, 0, 1)
    hand(1, 1, -1, 2, 2)
    hand(1, 2, 2, 0, 3)
    big_l, big_r = spread_left(nxy, half), spread_right(half, nxy, nxy)

    def up0(c):
        return dot2(big_l, times2(c, big_r))

    load_near.wait()
    within.wait()
    across.wait_recv()
    beside.wait_recv()
    en = [dielectric(near[f]) for f in range(6)]
    fzn[0] = face(en[0], en[1], 1.0)
    fzn[1] = face(jnp.where(me > 0, en[1], en[2]), en[2], 1.0)
    fzn[2] = face(en[2], en[3], 1.0)
    fzn[3] = face(en[3], jnp.where(me < n - 1, en[4], en[3]), 1.0)
    fzn[4] = face(en[4], en[5], 1.0)
    for f in range(4):
        fx, fy, total = plane_faces(en[f + 1], 1.0)
        fxn[f] = fx
        fyn[f] = fy
        kn = jnp.where(near[f + 1] == 2, SCREEN, 0.0).astype(F32)
        wtn[f] = DAMPING / (total + kn + fzn[f] + fzn[f + 1])
    for sent in pending:
        sent()
    lax.fori_loop(0, n, sent_density, 0)
    single = jnp.where(lax.rem(me, 2) == 0, me > 0, me < n - 1)
    for j in range(2):
        both = corr.at[pl.ds(0, 2), pl.ds(quarter * j, quarter), :]
        pltpu.make_async_copy(both, both, corr_recv.at[0, j]).wait()
        one = corr.at[pl.ds(0, 1), pl.ds(quarter * j, quarter), :]
        pl.when(single)(pltpu.make_async_copy(one, one, corr_recv.at[1, j]).wait)
    for j in range(2):
        place = landed.at[:, pl.ds(half * j, half), :]
        pltpu.make_async_copy(place, place, spread_recv.at[2, j]).wait()
    below, here, above = (up0(corr[i]) for i in range(3))
    spans = [(below, below, here), (here, below, here), (here, here, above), (above, here, above)]

    def relax(f, mine, low, high):
        return (1.0 - DAMPING) * mine + wtn[f] * (
            plane_sum(fxn[f], fyn[f], mine) + fzn[f] * low + fzn[f + 1] * high)

    y = [relax(f, *spans[f]) for f in range(4)]
    y[0] = jnp.where(me > 0, y[0], 0.0)
    y[3] = jnp.where(me < n - 1, y[3], 0.0)
    for f in (1, 2):
        out[f - 1] = landed[f - 1] + relax(f, y[f], y[f - 1], y[f + 1])


def box_local(partials, regions, previous):
    n = lax.axis_size("slab")
    nxy = regions.shape[1]
    half, quarter = nxy // 2, nxy // 4
    rows = partials.shape[2]
    window, window1 = half + HALO, (half + HALO) // 2
    vmem = lambda *shape: pltpu.VMEM(shape, F32)
    big = lambda count: vmem(count, window, nxy)
    small = lambda count: vmem(count, window1, half)
    return pl.pallas_call(
        functools.partial(box_kernel, n),
        out_shape=pltpu.VMEM(previous.shape, F32),
        in_specs=[pl.BlockSpec(memory_space=pltpu.HBM)] * 3,
        out_specs=pl.BlockSpec(memory_space=pltpu.VMEM),
        scratch_shapes=[
            pltpu.VMEM(partials.shape, partials.dtype), vmem(n // 2, 4, rows, nxy),
            pltpu.VMEM((8, window, nxy), jnp.int32), big(6), big(4),
            big(4), big(4), big(5), big(4), big(4), big(6), big(6), big(6), big(4),
            pltpu.VMEM((6, nxy, nxy), jnp.int32), vmem(4, nxy, nxy), vmem(4, nxy, nxy),
            vmem(5, nxy, nxy), vmem(4, nxy, nxy), vmem(2, nxy, nxy), vmem(3, half, half),
            small(8), small(6), small(6), small(6), small(7), small(6), small(6),
            small(4), small(3), small(3), small(1), small(1),
            small(6), small(6), small(6), small(6), small(4), small(4),
            vmem(2, 2, n // 4, quarter // 2, LANES), vmem(2, n // 2, quarter // 4, LANES),
            vmem(n // 2, quarter, LANES), vmem(8, 2 * nxy, LANES),
            pltpu.SemaphoreType.DMA((3,)),
            pltpu.SemaphoreType.DMA((5, 2)), pltpu.SemaphoreType.DMA((5, 2)),
            pltpu.SemaphoreType.DMA((4,)), pltpu.SemaphoreType.DMA((2, 2)),
            pltpu.SemaphoreType.DMA((n,)), pltpu.SemaphoreType.DMA((1,)),
            pltpu.SemaphoreType.DMA((MESSAGES,)), pltpu.SemaphoreType.DMA((MESSAGES,)),
            pltpu.SemaphoreType.DMA((5,)), pltpu.SemaphoreType.DMA((5,)),
        ],
        compiler_params=pltpu.CompilerParams(
            collective_id=1, has_side_effects=True, vmem_limit_bytes=60 * 1024 * 1024),
    )(partials, regions, previous)


def local(partials, regions, previous):
    n = lax.axis_size("slab")
    nxy = regions.shape[1]
    half, quarter = nxy // 2, nxy // 4
    rows = partials.shape[2]
    vmem = lambda *shape: pltpu.VMEM(shape, F32)
    spec = pl.BlockSpec(memory_space=pltpu.VMEM)
    return pl.pallas_call(
        functools.partial(kernel, n),
        out_shape=jax.ShapeDtypeStruct(previous.shape, F32),
        in_specs=[spec] * 3,
        out_specs=spec,
        scratch_shapes=[
            vmem(n, 2, rows, nxy), vmem(n, 2, rows, nxy), vmem(2, nxy, nxy),
            vmem(2, nxy, nxy), vmem(2, nxy, nxy), vmem(3, nxy, nxy), vmem(2, nxy, nxy),
            vmem(2, nxy, nxy),
            pltpu.VMEM((2, nxy, nxy), jnp.int32), pltpu.VMEM((2, nxy, nxy), jnp.int32),
            vmem(2, nxy, nxy), vmem(2, nxy, nxy), vmem(2, nxy, nxy), vmem(2, nxy, nxy),
            vmem(4, 2, nxy, nxy),
            vmem(2, nxy, nxy), vmem(2, nxy, nxy), vmem(2, nxy, nxy),
            vmem(6, 2, half, half), vmem(5, half, half), vmem(2, half, half),
            vmem(2, n // 2, quarter // 2, LANES), vmem(2, n // 2, quarter, LANES),
            pltpu.SemaphoreType.DMA((6, 2)), pltpu.SemaphoreType.DMA((6, 2)),
            pltpu.SemaphoreType.DMA((6, 2)), pltpu.SemaphoreType.DMA((6, 2)),
            pltpu.SemaphoreType.DMA((5,)), pltpu.SemaphoreType.DMA((5,)),
            vmem(n // 2, quarter, LANES),
        ],
        compiler_params=pltpu.CompilerParams(
            collective_id=0, has_side_effects=True, vmem_limit_bytes=60 * 1024 * 1024),
    )(partials, regions, previous)


def solution(mesh):
    in_specs = (
        P("job", None, "slab", None),
        P(("job", "slab"), None, None),
        P(("job", "slab"), None, None),
    )
    out_specs = P(("job", "slab"), None, None)
    size = mesh.shape["slab"]

    def fits(partials, regions):
        return (size == 16 and partials.shape[2] == 16 * size and partials.shape[1] == 2 * size
                and regions.shape[1] == 16 * size)

    def program(partials, regions, previous):
        chosen = box_local if fits(partials, regions) else local
        return jax.shard_map(chosen, mesh=mesh, in_specs=in_specs, out_specs=out_specs, check_vma=False)(
            partials, regions, previous)

    return program
```

```python
import functools

import jax
import jax.numpy as jnp
from jax import lax
from jax.experimental import pallas as pl
from jax.experimental.pallas import tpu as pltpu
from jax.sharding import PartitionSpec as P

PRE_SWEEPS = 2
POST_SWEEPS = 2
COARSE_SWEEPS = 4

DAMPING = 0.75
INSIDE = 2.0
SOLVENT = 78.4
SCREEN = 1.4
SOURCE = 16.0 * 3.141592653589793

F32 = jnp.float32
LANES = 128


def iota(shape, dim):
    return lax.broadcasted_iota(jnp.int32, shape, dim)


def face(mine, other, spacing):
    return mine * other / ((mine + other) * (0.5 * spacing))


def back(v, dim, by=1):
    return pltpu.roll(v, by, dim)


def ahead(v, dim, by=1):
    return pltpu.roll(v, v.shape[dim] - by, dim)


def terms(v):
    result = []
    for _ in range(3):
        result.append(v.astype(jnp.bfloat16))
        v = v - result[-1].astype(F32)
    return result


def product(a, b):
    return lax.dot_general(a, b, (((1,), (0,)), ((), ())), preferred_element_type=F32)


def times(v, selector):
    high, middle, low = (product(t, selector.astype(jnp.bfloat16)) for t in terms(v))
    return high + (middle + low)


def dot(selector, v):
    high, middle, low = (product(selector.astype(jnp.bfloat16), t) for t in terms(v))
    return high + (middle + low)


def halves(v):
    high = v.astype(jnp.bfloat16)
    return high, (v - high.astype(F32)).astype(jnp.bfloat16)


def times2(v, selector):
    high, low = (product(t, selector.astype(jnp.bfloat16)) for t in halves(v))
    return high + low


def dot2(selector, v):
    high, low = (product(selector.astype(jnp.bfloat16), t) for t in halves(v))
    return high + low


def pool_right(wide, narrow, valid):
    src, dst = iota((wide, narrow), 0), iota((wide, narrow), 1)
    return jnp.where((src // 2 == dst) & (src < valid), 1.0, 0.0).astype(F32)


def pool_left(narrow, wide):
    dst, src = iota((narrow, wide), 0), iota((narrow, wide), 1)
    return jnp.where(src // 2 == dst, 1.0, 0.0).astype(F32)


def spread_right(narrow, wide, valid):
    src, dst = iota((narrow, wide), 0), iota((narrow, wide), 1)
    return jnp.where((dst // 2 == src) & (dst < valid), 1.0, 0.0).astype(F32)


def spread_left(wide, narrow):
    dst, src = iota((wide, narrow), 0), iota((wide, narrow), 1)
    return jnp.where(dst // 2 == src, 1.0, 0.0).astype(F32)


def plane_faces(e, spacing):
    rows, cols = e.shape
    x, y = iota(e.shape, 0), iota(e.shape, 1)
    fx = jnp.where(x > 0, face(e, back(e, 0), spacing), 0.0)
    fy = jnp.where(y > 0, face(e, back(e, 1), spacing), 0.0)
    edges = (jnp.where((x == 0) | (x == rows - 1), 1.0, 0.0)
             + jnp.where((y == 0) | (y == cols - 1), 1.0, 0.0))
    total = fx + ahead(fx, 0) + fy + ahead(fy, 1) + edges * e * (1.0 / spacing)
    return fx, fy, total


def plane_sum(fx, fy, v):
    return fx * back(v, 0) + ahead(fx * v, 0) + fy * back(v, 1) + ahead(fy * v, 1)


def coarse_cycle(e, k, planes, nx, sz, sx, dot, times, pairs=None):
    rows = e.shape[0]
    row, lane = iota(e.shape, 0), iota(e.shape, 1)
    x, z = row % nx, row // nx
    valid = (row < planes * nx) & (lane < nx)
    e = jnp.where(valid, e, 1.0)
    fx = jnp.where(valid & (x > 0), face(e, back(e, 0), sx), 0.0) if nx > 1 else None
    fy = jnp.where(valid & (lane > 0), face(e, back(e, 1), sx), 0.0) if nx > 1 else None
    wrap = nx % rows
    fz = jnp.where(valid & (z > 0), face(e, back(e, 0, wrap), sz), 0.0) if planes > 1 else None
    diag = k + e * (
        (jnp.where(x == 0, 1.0, 0.0) + jnp.where(x == nx - 1, 1.0, 0.0)
         + jnp.where(lane == 0, 1.0, 0.0) + jnp.where(lane == nx - 1, 1.0, 0.0)) * (1.0 / sx)
        + (jnp.where(z == 0, 1.0, 0.0) + jnp.where(z == planes - 1, 1.0, 0.0)) * (1.0 / sz))
    if nx > 1:
        diag = diag + fx + ahead(fx, 0) + fy + ahead(fy, 1)
    if planes > 1:
        diag = diag + fz + ahead(fz, 0, wrap)
    w = jnp.where(valid, DAMPING / jnp.where(valid, diag, 1.0), 0.0)

    def beside(v):
        total = jnp.zeros_like(v)
        if nx > 1:
            total = plane_sum(fx, fy, v)
        if planes > 1:
            total = total + fz * back(v, 0, wrap) + ahead(fz * v, 0, wrap)
        return total

    def sweep(v, b):
        return (1.0 - DAMPING) * v + w * (b + beside(v))

    def coarsest(b):
        v = w * b
        for _ in range(COARSE_SWEEPS - 1):
            v = sweep(v, b)
        return v

    if planes == 1:
        return coarsest
    halve = nx > 1 and nx % 2 == 0
    nx2 = nx // 2 if halve else nx
    sx2 = sx * 4.0 if halve else sx
    step = planes
    while step * nx > 512 and step % 4 == 0:
        step //= 2
    part = step * nx
    if step == planes:
        part = rows
    real2 = planes // 2 * nx2
    rows2 = max(8, real2)
    part2 = rows2 if step == planes else step // 2 * nx2
    ratio = 2 if halve else 1

    def member(fine, coarse):
        return ((fine < step * nx) & ((fine // nx // 2) * nx2 + fine % nx // ratio == coarse))

    down = jnp.where(member(iota((part2, part), 1), iota((part2, part), 0)), 1.0, 0.0)
    up = jnp.where(member(iota((part, part2), 0), iota((part, part2), 1)), 1.0, 0.0)
    if halve:
        right = pool_right(LANES, LANES, nx)
        left = spread_right(LANES, LANES, nx)
        scale = 0.125
    else:
        scale = 0.5

    def coarsen(f):
        if pairs is not None:
            f = jnp.sum(f.reshape(planes // 2, 2, nx, LANES), axis=1).reshape(planes // 2 * nx, LANES)
            return scale * times(pairs[0](f), right)
        if halve:
            f = times(f, right)
        parts = [dot(down, f[i:i + part]) for i in range(0, rows, part)]
        return scale * (parts[0] if len(parts) == 1 else jnp.concatenate(parts, axis=0))

    def refine(f):
        if pairs is not None:
            f = pairs[1](times(f, left)).reshape(planes // 2, 1, nx, LANES)
            return jnp.broadcast_to(f, (planes // 2, 2, nx, LANES)).reshape(planes * nx, LANES)
        if halve:
            f = times(f, left)
        parts = [dot(up, f[i:i + part2]) for i in range(0, rows2, part2)]
        return parts[0] if len(parts) == 1 else jnp.concatenate(parts, axis=0)

    below = coarse_cycle(coarsen(jnp.where(valid, e, 0.0)), coarsen(k),
                         planes // 2, nx2, sz * 4.0, sx2, dot, times, pairs)

    def run(b):
        v = w * b
        for _ in range(PRE_SWEEPS - 1):
            v = sweep(v, b)
        r = jnp.where(valid, b - diag * v + beside(v), 0.0)
        v = v + refine(below(coarsen(r)))
        for _ in range(POST_SWEEPS):
            v = sweep(v, b)
        return v

    return run


REG, V0, V1, V2, BASE, FAR = range(6)
E1, A1, A2, A3, A4, TERM = range(6)


def kernel(n, partials, regions, previous, out,
           dens, got, b0, fx0, fy0, fz0, dg0, wt0, halo_reg, far_reg, fxh, fyh, fzh, wth, halo0, v1, v2, base,
           halo1, plane1, term1, gb, gk,
           big_send, big_recv, small_send, small_recv, many_send, many_recv, c2_planes):
    me = lax.axis_index("slab")
    job = lax.axis_index("job")
    nxy = regions.shape[1]
    half = nxy // 2
    quarter = nxy // 4
    rows = partials.shape[2]
    has_lo, has_hi = me > 0, me < n - 1

    def peer(index):
        return {"slab": index}

    barrier = pltpu.get_barrier_semaphore()

    def greet(off, carry):
        pl.semaphore_signal(barrier, inc=1, device_id=peer(lax.rem(me + off, n)),
                            device_id_type=pl.DeviceIdType.MESH)
        return carry

    lax.fori_loop(1, n, greet, 0)

    @pl.when(jnp.logical_not(has_lo))
    def _():
        for i in range(4):
            halo0[i, 0] = jnp.zeros((nxy, nxy), F32)
        for i in range(6):
            halo1[i, 0] = jnp.zeros((half, half), F32)
        halo_reg[0] = jnp.zeros((nxy, nxy), jnp.int32)
        far_reg[0] = jnp.zeros((nxy, nxy), jnp.int32)

    @pl.when(jnp.logical_not(has_hi))
    def _():
        for i in range(4):
            halo0[i, 1] = jnp.zeros((nxy, nxy), F32)
        for i in range(6):
            halo1[i, 1] = jnp.zeros((half, half), F32)
        halo_reg[1] = jnp.zeros((nxy, nxy), jnp.int32)
        far_reg[1] = jnp.zeros((nxy, nxy), jnp.int32)

    density = partials[0].astype(F32)
    for g in range(1, partials.shape[0]):
        density = density + partials[g].astype(F32)
    dens[...] = (SOURCE * density).reshape(dens.shape)

    pl.semaphore_wait(barrier, n - 1)

    def copies(first, last, dst, sends, recvs, i):
        to_lo = pltpu.make_async_remote_copy(
            src_ref=first, dst_ref=dst.at[1], send_sem=sends.at[i, 0], recv_sem=recvs.at[i, 1],
            device_id=peer(jnp.maximum(me - 1, 0)), device_id_type=pl.DeviceIdType.MESH)
        to_hi = pltpu.make_async_remote_copy(
            src_ref=last, dst_ref=dst.at[0], send_sem=sends.at[i, 1], recv_sem=recvs.at[i, 0],
            device_id=peer(jnp.minimum(me + 1, n - 1)), device_id_type=pl.DeviceIdType.MESH)

        def start():
            pl.when(has_lo)(to_lo.start)
            pl.when(has_hi)(to_hi.start)

        def recv():
            pl.when(has_lo)(to_hi.wait_recv)
            pl.when(has_hi)(to_lo.wait_recv)

        def sent():
            pl.when(has_lo)(to_lo.wait_send)
            pl.when(has_hi)(to_hi.wait_send)

        return start, recv, sent

    pending = []

    def launch(first, last, dst, sends, recvs, i):
        start, recv, sent = copies(first, last, dst, sends, recvs, i)
        start()
        pending.append(sent)
        return recv

    recv_reg = launch(regions.at[0], regions.at[1], halo_reg, big_send, big_recv, REG)
    recv_v0 = launch(previous.at[0], previous.at[1], halo0.at[0], big_send, big_recv, V0)

    def scatter(step, carry):
        other = lax.rem(me + 1 + lax.rem(step + n // 2 - 1, n - 1), n)
        pltpu.make_async_remote_copy(
            src_ref=dens.at[other], dst_ref=got.at[me], send_sem=many_send.at[0],
            recv_sem=many_recv.at[0], device_id=peer(other),
            device_id_type=pl.DeviceIdType.MESH).start()
        return carry

    lax.fori_loop(0, n - 1, scatter, 0)

    def dielectric(r):
        return jnp.where(r == 0, INSIDE, SOLVENT).astype(F32)

    e = [dielectric(regions[p]) for p in range(2)]
    k = [jnp.where(regions[p] == 2, SCREEN, 0.0).astype(F32) for p in range(2)]
    right0, left0 = pool_right(nxy, half, nxy), pool_left(half, nxy)
    right1, left1 = pool_right(half, LANES, half), pool_left(quarter, half)

    def down0(a, b):
        return 0.125 * dot(left0, times(a + b, right0))

    def down1(a):
        return 0.25 * dot(left1, times(a, right1))

    e1, k1 = down0(e[0], e[1]), down0(k[0], k[1])
    plane1[E1] = e1
    recv_e1 = launch(plane1.at[E1], plane1.at[E1], halo1.at[E1], small_send, small_recv, E1)
    core, chip = lax.rem(me, 2), me // 2
    gk[core, chip] = down1(e1) + back(down1(k1), 1, LANES // 2)

    def share(ref, i):
        def one(off, carry):
            other = lax.rem(me + 2 * off, n)
            pltpu.make_async_remote_copy(
                src_ref=ref.at[core, chip], dst_ref=ref.at[core, chip], send_sem=many_send.at[i],
                recv_sem=many_recv.at[i], device_id=peer(other),
                device_id_type=pl.DeviceIdType.MESH).start()
            return carry

        lax.fori_loop(1, n // 2, one, 0)

    def relay(ref, i):
        window = ref.at[0, pl.ds(0, n // 2 - 1)]
        pltpu.make_async_copy(window, window, many_recv.at[i]).wait()
        copy = pltpu.make_async_remote_copy(
            src_ref=ref.at[core], dst_ref=ref.at[core], send_sem=many_send.at[i + 2],
            recv_sem=many_recv.at[i + 2], device_id=peer(me + 1 - 2 * core),
            device_id_type=pl.DeviceIdType.MESH)
        copy.start()
        pending.append(pltpu.make_async_copy(window, window, many_send.at[i]).wait)
        pending.append(copy.wait_send)
        return copy.wait_recv

    def all_in(ref, sems, i):
        window = ref.at[pl.ds(0, n - 1)]
        pltpu.make_async_copy(window, window, sems.at[i]).wait()

    share(gk, 1)

    totals = []
    middle = face(e[0], e[1], 1.0)
    fz0[1] = middle
    part = []
    for p in range(2):
        fx, fy, total = plane_faces(e[p], 1.0)
        fx0[p] = fx
        fy0[p] = fy
        totals.append(total + middle + k[p])
        part.append(plane_sum(fx, fy, previous[p]) + middle * previous[1 - p])
    recv_reg()
    e_side = [jnp.where(has_lo, dielectric(halo_reg[0]), e[0]),
              jnp.where(has_hi, dielectric(halo_reg[1]), e[1])]
    for p in range(2):
        outer = face(e_side[p], e[p], 1.0)
        fz0[2 * p] = outer
        total = totals[p] + outer
        dg0[p] = total
        wt0[p] = DAMPING / total

    def beside0(p, mine, below, above):
        return plane_sum(fx0[p], fy0[p], mine) + fz0[p] * below + fz0[p + 1] * above

    def sweep0(p, mine, below, above):
        return (1.0 - DAMPING) * mine + wt0[p] * (b0[p] + beside0(p, mine, below, above))

    recv_v0()
    for p in range(2):
        v1[p] = (1.0 - DAMPING) * previous[p] + wt0[p] * (part[p] + fz0[2 * p] * halo0[0, p])

    got[me] = dens[me]
    all_in(got, many_recv, 0)
    for p in range(2):
        if rows % 8 == 0:
            b0[p] = got[:, p].reshape(nxy, nxy)
        else:
            for s in range(n):
                b0[p, s * rows:(s + 1) * rows, :] = got[s, p]
    for p in range(2):
        v1[p] = v1[p] + wt0[p] * b0[p]
    recv = launch(v1.at[0], v1.at[1], halo0.at[1], big_send, big_recv, V1)
    recv_gk = relay(gk, 1)
    recv_e1()
    sz1 = sx1 = 4.0
    fx1, fy1, total1 = plane_faces(e1, sx1)
    fz1lo = face(jnp.where(has_lo, halo1[E1, 0], e1), e1, sz1)
    fz1hi = face(jnp.where(has_hi, halo1[E1, 1], e1), e1, sz1)
    dg1 = total1 + fz1lo + fz1hi + k1
    wt1 = DAMPING / dg1

    recv()
    v2[0] = sweep0(0, v1[0], halo0[1, 0], v1[1])
    v2[1] = sweep0(1, v1[1], v1[0], halo0[1, 1])
    term1[0] = 0.125 * dot(left0, times(fz0[0] * v2[0], right0))
    term1[1] = 0.125 * dot(left0, times(fz0[2] * v2[1], right0))
    recv_term = launch(term1.at[0], term1.at[1], halo1.at[TERM], small_send, small_recv, TERM)
    recv_v2 = launch(v2.at[0], v2.at[1], halo0.at[2], big_send, big_recv, V2)
    r0 = b0[0] - dg0[0] * v2[0] + plane_sum(fx0[0], fy0[0], v2[0]) + fz0[1] * v2[1]
    r1 = b0[1] - dg0[1] * v2[1] + plane_sum(fx0[1], fy0[1], v2[1]) + fz0[1] * v2[0]
    b1 = down0(r0, r1)
    recv_far = launch(regions.at[1], regions.at[0], far_reg, big_send, big_recv, FAR)
    recv_gk()
    e2 = 0.5 * (gk[0] + gk[1]).reshape(n // 2 * quarter, LANES)
    k2 = back(e2, 1, LANES // 2)
    coarse = coarse_cycle(e2, k2, n // 2, quarter, 16.0, 16.0, dot, times)
    recv_term()
    b1 = b1 + halo1[TERM, 0] + halo1[TERM, 1]

    def beside1(mine, i):
        return plane_sum(fx1, fy1, mine) + fz1lo * halo1[i, 0] + fz1hi * halo1[i, 1]

    def trade1(value, i):
        plane1[i] = value
        launch(plane1.at[i], plane1.at[i], halo1.at[i], small_send, small_recv, i)()

    a = wt1 * b1
    trade1(a, A1)
    a = (1.0 - DAMPING) * a + wt1 * (b1 + beside1(a, A1))
    trade1(a, A2)
    full = down1(b1 - dg1 * a + beside1(a, A2))
    gb[core, chip] = full[:quarter // 2] + back(full[quarter // 2:], 1, LANES // 2)
    share(gb, 2)
    recv_v2()
    base[0] = sweep0(0, v2[0], halo0[2, 0], v2[1])
    base[1] = sweep0(1, v2[1], v2[0], halo0[2, 1])
    recv_base = launch(base.at[0], base.at[1], halo0.at[3], big_send, big_recv, BASE)
    relay_gb = relay(gb, 2)
    recv_far()
    for p in range(2):
        region = halo_reg[p]
        beyond = face(e_side[p], dielectric(far_reg[p]), 1.0)
        fx, fy, total = plane_faces(e_side[p], 1.0)
        fxh[p] = fx
        fyh[p] = fy
        fzh[p] = beyond
        wth[p] = DAMPING / (total + beyond + fz0[2 * p] + jnp.where(region == 2, SCREEN, 0.0))
    relay_gb()
    packed = 0.5 * (gb[0] + gb[1]).reshape(n // 2 * quarter // 2, LANES)
    split = (n // 2, quarter // 2, LANES)
    b2 = jnp.concatenate(
        [packed.reshape(split), back(packed, 1, LANES // 2).reshape(split)], axis=1
    ).reshape(n // 2 * quarter, LANES)
    c2 = coarse(b2)

    for i in range(n // 2):
        c2_planes[i] = c2[i * quarter:(i + 1) * quarter]
    grow_l, grow_r = spread_left(half, quarter), spread_right(LANES, half, half)

    def up1(index):
        return dot(grow_l, times(c2_planes[index // 2], grow_r))

    halo1[A2, 0] = halo1[A2, 0] + jnp.where(has_lo, up1(jnp.maximum(me - 1, 0)), 0.0)
    halo1[A2, 1] = halo1[A2, 1] + jnp.where(has_hi, up1(jnp.minimum(me + 1, n - 1)), 0.0)
    a = a + up1(me)
    a = (1.0 - DAMPING) * a + wt1 * (b1 + beside1(a, A2))
    trade1(a, A3)
    a = (1.0 - DAMPING) * a + wt1 * (b1 + beside1(a, A3))
    trade1(a, A4)

    big_l, big_r = spread_left(nxy, half), spread_right(half, nxy, nxy)

    def up0(c):
        return dot(big_l, times(c, big_r))

    mine = up0(a)
    recv_base()
    v3, side = [], []
    present = [has_lo, has_hi]
    for p in range(2):
        c = up0(halo1[A4, p])
        own = plane_sum(fx0[p], fy0[p], mine) + fz0[1] * mine + fz0[2 * p] * c
        v3.append(base[p] + (1.0 - DAMPING) * mine + wt0[p] * own)
        other = plane_sum(fxh[p], fyh[p], c) + fzh[p] * c + fz0[2 * p] * mine
        swept = halo0[3, p] + (1.0 - DAMPING) * c + wth[p] * other
        side.append(jnp.where(present[p], swept, 0.0))
    out[0] = sweep0(0, v3[0], side[0], v3[1])
    out[1] = sweep0(1, v3[1], v3[0], side[1])

    for sent in pending:
        sent()
    all_in(got, many_send, 0)


HALO = 16
REG_LO, REG_HI, V0_LO, V0_HI, V1_LO, V1_HI, V2_LO, V2_HI, BASE_LO, BASE_HI = range(10)
E_M1, E_P1, E_M2, E_P2, K_M1, K_P1, B_M1, B_P1, B_M2, B_P2, A2_LO, A2_HI, NEAR, NEAR_CORE, FAR_LO, FAR_HI = range(10, 26)
MESSAGES = 26


def box_kernel(n, partials, regions, previous, out,
               parts, dens, reg, v0, b0, fx0, fy0, fz0, dg0, wt0, v1, v2, base, swept,
               near, fxn, fyn, fzn, wtn, landed, corr,
               e1, k1, fx1, fy1, fz1, dg1, wt1, pack, from_lo, from_hi, far_lo, far_hi,
               b1, a1, a2, a2c, a3, a4, gk, gb, c2_planes, rows_tmp,
               load_sem, spread_send, spread_recv, corr_send, corr_recv, dens_send, dens_recv,
               side_send, side_recv, many_send, many_recv):
    me = lax.axis_index("slab")
    nz = n // 2
    z, x, core = me // 4, lax.rem(me // 2, 2), lax.rem(me, 2)
    zi = 2 * z + core
    nxy = regions.shape[1]
    half, quarter = nxy // 2, nxy // 4
    rows = partials.shape[2]
    window = half + HALO
    window1 = window // 2
    blocks = window // rows
    first = half - HALO

    def peer(index):
        return {"slab": index}

    def at(i, j):
        return (i // 2) * 4 + j * 2 + lax.rem(i, 2)

    load = pltpu.make_async_copy(partials, parts, load_sem.at[0])
    load.start()
    load_near = pltpu.make_async_copy(regions, near.at[pl.ds(2, 2)], load_sem.at[1])
    load_near.start()
    barrier = pltpu.get_barrier_semaphore()

    def greet(off, carry):
        pl.semaphore_signal(barrier, inc=1, device_id=peer(lax.rem(me + off, n)),
                            device_id_type=pl.DeviceIdType.MESH)
        return carry

    lax.fori_loop(1, n, greet, 0)

    plane0 = jnp.zeros((window, nxy), F32)
    plane1 = jnp.zeros((window1, half), F32)

    @pl.when(zi == 0)
    def _():
        for i in range(2):
            reg[i] = jnp.zeros((window, nxy), jnp.int32)
        for v in (v0, v1, v2, base):
            v[0] = plane0
        for i in range(3):
            from_lo[i] = plane1
        for i in range(2):
            e1[i] = plane1 + 1.0
            k1[i] = plane1
        a2[0] = plane1

    @pl.when(zi == nz - 1)
    def _():
        for i in range(2):
            reg[6 + i] = jnp.zeros((window, nxy), jnp.int32)
        for v in (v0, v1, v2, base):
            v[5] = plane0
        for i in range(3):
            from_hi[i] = plane1
        for i in range(2):
            e1[6 + i] = plane1 + 1.0
            k1[4 + i] = plane1
        a2[5] = plane1

    @pl.when(zi < 2)
    def _():
        far_lo[0] = plane1

    @pl.when(zi >= nz - 2)
    def _():
        far_hi[0] = plane1

    @pl.when(me == 0)
    def _():
        corr[0] = jnp.zeros((half, half), F32)

    @pl.when(me == n - 1)
    def _():
        corr[2] = jnp.zeros((half, half), F32)

    load.wait()
    density = parts[0].astype(F32)
    for g in range(1, partials.shape[0]):
        density = density + parts[g].astype(F32)
    dens[...] = (SOURCE * density).reshape(dens.shape)

    pl.semaphore_wait(barrier, n - 1)
    pending = []

    def spread(src, dst, mine, first_slot, step, i):
        for j in range(2):
            target = at(2 * z + x, j)
            piece = src.at[pl.ds(mine, 1), pl.ds(first * j, window), :]
            place = dst.at[pl.ds(first_slot + step * core, 1)]
            remote = pltpu.make_async_remote_copy(
                src_ref=piece, dst_ref=place, send_sem=spread_send.at[i, j],
                recv_sem=spread_recv.at[i, core], device_id=peer(target),
                device_id_type=pl.DeviceIdType.MESH)
            here = pltpu.make_async_copy(piece, place, spread_recv.at[i, core])
            away = target != me
            pl.when(away)(remote.start)
            pl.when(jnp.logical_not(away))(here.start)
            pending.append(lambda remote=remote, away=away: pl.when(away)(remote.wait_send))

        def arrived():
            for j in range(2):
                place = dst.at[pl.ds(first_slot + step * j, 1)]
                pltpu.make_async_copy(place, place, spread_recv.at[i, j]).wait()

        return arrived

    def send_density(step, carry):
        other = lax.rem(me + 1 + lax.rem(step + n // 2 - 1, n), n)
        oz, ox = 2 * (other // 4) + lax.rem(other, 2), lax.rem(other // 2, 2)
        block = me - (first // rows) * ox
        inside = (block >= 0) & (block < blocks)
        block = jnp.clip(block, 0, blocks - 1)
        place = b0.at[:, pl.ds(pl.multiple_of(block * rows, rows), rows), :]

        @pl.when(inside & (other != me))
        def _():
            pltpu.make_async_remote_copy(
                src_ref=dens.at[oz], dst_ref=place, send_sem=dens_send.at[other],
                recv_sem=dens_recv.at[0], device_id=peer(other),
                device_id_type=pl.DeviceIdType.MESH).start()

        @pl.when(inside & (other == me))
        def _():
            pltpu.make_async_copy(dens.at[oz], place, dens_recv.at[0]).start()

        return carry

    def sent_density(other, carry):
        ox = lax.rem(other // 2, 2)
        block = me - (first // rows) * ox

        @pl.when((block >= 0) & (block < blocks) & (other != me))
        def _():
            pltpu.make_async_copy(dens.at[0], dens.at[0], dens_send.at[other]).wait()

        return carry

    def push(src, dst, delta, i):
        can_send = (zi + delta >= 0) & (zi + delta < nz)
        can_recv = (zi - delta >= 0) & (zi - delta < nz)
        copy = pltpu.make_async_remote_copy(
            src_ref=src, dst_ref=dst, send_sem=side_send.at[i], recv_sem=side_recv.at[i],
            device_id=peer(at(jnp.clip(zi + delta, 0, nz - 1), x)),
            device_id_type=pl.DeviceIdType.MESH)
        pl.when(can_send)(copy.start)
        pending.append(lambda: pl.when(can_send)(copy.wait_send))
        return lambda: pl.when(can_recv)(copy.wait_recv)

    def trade(field, low, high, i):
        down = push(field.at[low], field.at[high + 1], -1, i)
        up = push(field.at[high], field.at[low - 1], 1, i + 1)

        def arrived():
            down()
            up()

        return arrived

    lax.fori_loop(0, n, send_density, 0)
    reg_edge = spread(regions, reg, core, 2, 3, 0)
    v0_edge = spread(previous, v0, core, 1, 3, 1)
    reg_in = spread(regions, reg, 1 - core, 3, 1, 3)
    v0_in = spread(previous, v0, 1 - core, 2, 1, 4)

    def dielectric(r):
        return jnp.where(r == 0, INSIDE, SOLVENT).astype(F32)

    right0 = pool_right(nxy, half, nxy)
    right1 = pool_right(half, LANES, half)
    dst1, src1 = iota((quarter // 2, window1), 0), iota((quarter // 2, window1), 1)
    left1 = jnp.where((src1 - (HALO // 2) * x) // 2 == dst1, 1.0, 0.0).astype(F32)

    turn = [0]

    def strips(v):
        return [v[:, i:i + LANES] for i in range(0, v.shape[1], LANES)]

    def scratch():
        turn[0] = (turn[0] + 1) % 8
        return rows_tmp.at[turn[0]]

    def pool_rows(v):
        count = v.shape[0] // 2
        done = []
        for strip in strips(v):
            tmp = scratch()
            tmp[:2 * count] = strip
            done.append(tmp[pl.ds(0, count, stride=2), :] + tmp[pl.ds(1, count, stride=2), :])
        return done[0] if len(done) == 1 else jnp.concatenate(done, axis=1)

    def grow_rows(v):
        count = v.shape[0]
        done = []
        for strip in strips(v):
            tmp = scratch()
            tmp[pl.ds(0, count, stride=2), :] = strip
            tmp[pl.ds(1, count, stride=2), :] = strip
            done.append(tmp[:2 * count])
        return done[0] if len(done) == 1 else jnp.concatenate(done, axis=1)

    def down0(a):
        return 0.125 * times2(pool_rows(a), right0)

    def down1(a):
        return 0.125 * dot2(left1, times2(a, right1))

    reg_edge()
    reg_halo = trade(reg, 2, 5, REG_LO)
    v0_edge()
    v0_halo = trade(v0, 1, 4, V0_LO)
    reg_in()
    far_in = [push(reg.at[3], reg.at[7], -1, FAR_LO), push(reg.at[4], reg.at[0], 1, FAR_HI)]
    e = [dielectric(reg[p]) for p in range(2, 6)]
    k = [jnp.where(reg[p] == 2, SCREEN, 0.0).astype(F32) for p in range(2, 6)]
    for i in range(2):
        e1[3 + i] = down0(e[2 * i] + e[2 * i + 1])
        k1[2 + i] = down0(k[2 * i] + k[2 * i + 1])
    e1_in = [push(e1.at[pl.ds(3, 2)], e1.at[pl.ds(1, 2)], 1, E_P1),
             push(e1.at[pl.ds(3, 2)], e1.at[pl.ds(5, 2)], -1, E_M1),
             push(e1.at[pl.ds(4, 1)], e1.at[pl.ds(0, 1)], 2, E_P2),
             push(e1.at[pl.ds(3, 1)], e1.at[pl.ds(7, 1)], -2, E_M2),
             push(k1.at[pl.ds(2, 2)], k1.at[pl.ds(0, 2)], 1, K_P1),
             push(k1.at[pl.ds(2, 2)], k1.at[pl.ds(4, 2)], -1, K_M1)]
    chip = me // 2
    gk[core, x, z] = down1(e1[3] + e1[4]) + back(down1(k1[2] + k1[3]), 1, LANES // 2)

    def share(ref, i):
        def one(off, carry):
            other = lax.rem(me + 2 * off, n)
            pltpu.make_async_remote_copy(
                src_ref=ref.at[core, chip], dst_ref=ref.at[core, chip], send_sem=many_send.at[i],
                recv_sem=many_recv.at[i], device_id=peer(other),
                device_id_type=pl.DeviceIdType.MESH).start()
            return carry

        lax.fori_loop(1, n // 2, one, 0)

    def relay(ref, i):
        seven = ref.at[0, pl.ds(0, n // 2 - 1)]
        pltpu.make_async_copy(seven, seven, many_recv.at[i]).wait()
        copy = pltpu.make_async_remote_copy(
            src_ref=ref.at[core], dst_ref=ref.at[core], send_sem=many_send.at[i + 2],
            recv_sem=many_recv.at[i + 2], device_id=peer(me + 1 - 2 * core),
            device_id_type=pl.DeviceIdType.MESH)
        copy.start()
        pending.append(pltpu.make_async_copy(seven, seven, many_send.at[i]).wait)
        pending.append(copy.wait_send)
        return copy.wait_recv

    def in_order(ref):
        return [ref[c, 2 * i + j] for i in range(n // 4) for c in range(2) for j in range(2)]

    columns = n // 4

    def along(off, carry):
        other = lax.rem(me + 4 * off, n)
        pltpu.make_async_remote_copy(
            src_ref=gk.at[core, x, z], dst_ref=gk.at[core, x, z], send_sem=many_send.at[0],
            recv_sem=many_recv.at[0], device_id=peer(other),
            device_id_type=pl.DeviceIdType.MESH).start()
        return carry

    lax.fori_loop(1, columns, along, 0)

    def gk_over():
        others = gk.at[0, 0, pl.ds(0, columns - 1)]
        pltpu.make_async_copy(others, others, many_recv.at[0]).wait()
        copy = pltpu.make_async_remote_copy(
            src_ref=gk.at[core, x], dst_ref=gk.at[core, x], send_sem=many_send.at[4],
            recv_sem=many_recv.at[4], device_id=peer(at(zi, 1 - x)),
            device_id_type=pl.DeviceIdType.MESH)
        copy.start()
        pending.append(pltpu.make_async_copy(others, others, many_send.at[0]).wait)
        pending.append(copy.wait_send)
        return copy.wait_recv

    def gk_beside():
        copy = pltpu.make_async_remote_copy(
            src_ref=gk.at[core], dst_ref=gk.at[core], send_sem=many_send.at[2],
            recv_sem=many_recv.at[2], device_id=peer(at(zi + 1 - 2 * core, x)),
            device_id_type=pl.DeviceIdType.MESH)
        copy.start()
        pending.append(copy.wait_send)
        return copy.wait_recv

    totals = []
    for p in range(4):
        fx, fy, total = plane_faces(e[p], 1.0)
        fx0[p] = fx
        fy0[p] = fy
        totals.append(total + k[p])
    for p in range(1, 4):
        fz0[p] = face(e[p - 1], e[p], 1.0)
    v0_in()

    def beside0(p, v):
        return (plane_sum(fx0[p], fy0[p], v[p + 1]) + fz0[p] * v[p] + fz0[p + 1] * v[p + 2])

    def sweep0(p, v):
        return (1.0 - DAMPING) * v[p + 1] + wt0[p] * (b0[p] + beside0(p, v))

    def first_part(p):
        v1[p + 1] = (1.0 - DAMPING) * v0[p + 1] + wt0[p] * beside0(p, v0)

    def weights(p):
        diag = totals[p] + fz0[p] + fz0[p + 1]
        dg0[p] = diag
        wt0[p] = DAMPING / diag

    for p in (1, 2):
        weights(p)
        first_part(p)
    reg_halo()
    fz0[0] = face(jnp.where(zi > 0, dielectric(reg[1]), e[0]), e[0], 1.0)
    fz0[4] = face(e[3], jnp.where(zi < nz - 1, dielectric(reg[6]), e[3]), 1.0)
    weights(0)
    weights(3)
    v0_halo()
    first_part(0)
    first_part(3)

    pltpu.make_async_copy(b0, b0, dens_recv.at[0]).wait()
    for p in (0, 3):
        v1[p + 1] = v1[p + 1] + wt0[p] * b0[p]
    v1_halo = trade(v1, 1, 4, V1_LO)
    for arrived in far_in:
        arrived()
    own_rows = pl.ds(pl.multiple_of(HALO * x, HALO), half)

    def near_rows(j):
        return near.at[pl.ds(4 * core, 2), pl.ds(pl.multiple_of(half * j, half), half), :]

    across = pltpu.make_async_remote_copy(
        src_ref=reg.at[pl.ds(4 + 2 * core - 4 * x, 2), own_rows, :], dst_ref=near_rows(x),
        send_sem=side_send.at[NEAR], recv_sem=side_recv.at[NEAR], device_id=peer(at(zi, 1 - x)),
        device_id_type=pl.DeviceIdType.MESH)
    beside = pltpu.make_async_remote_copy(
        src_ref=regions, dst_ref=near.at[pl.ds(4 * core, 2)], send_sem=side_send.at[NEAR_CORE],
        recv_sem=side_recv.at[NEAR_CORE], device_id=peer(at(zi + 1 - 2 * core, x)),
        device_id_type=pl.DeviceIdType.MESH)
    within = pltpu.make_async_copy(reg.at[pl.ds(2 * core + 4 * x, 2), own_rows, :], near_rows(x),
                                   load_sem.at[2])
    for copy in (across, beside, within):
        copy.start()
    pending.append(across.wait_send)
    pending.append(beside.wait_send)
    gk_across = gk_over()

    for p in (1, 2):
        v1[p + 1] = v1[p + 1] + wt0[p] * b0[p]

    for p in (1, 2):
        v2[p + 1] = sweep0(p, v1)
    v1_halo()
    for p in (0, 3):
        v2[p + 1] = sweep0(p, v1)
    v2_halo = trade(v2, 1, 4, V2_LO)
    pack[0] = down0(fz0[4] * v2[4])
    pack[3] = down0(fz0[0] * v2[1])

    def left_over(p):
        r = b0[p] - dg0[p] * v2[p + 1] + plane_sum(fx0[p], fy0[p], v2[p + 1])
        if p > 0:
            r = r + fz0[p] * v2[p]
        if p < 3:
            r = r + fz0[p + 1] * v2[p + 2]
        return r

    for i in range(2):
        pack[1 + i] = down0(left_over(2 * i) + left_over(2 * i + 1))
    b1_in = [push(pack.at[pl.ds(0, 3)], from_lo, 1, B_P1),
             push(pack.at[pl.ds(1, 3)], from_hi, -1, B_M1),
             push(pack.at[pl.ds(0, 1)], far_lo, 2, B_P2),
             push(pack.at[pl.ds(3, 1)], far_hi, -2, B_M2)]
    for arrived in e1_in:
        arrived()

    @pl.when(zi == 0)
    def _():
        e1[2] = e1[3]
        e1[0] = plane1 + 1.0

    @pl.when(zi == 1)
    def _():
        e1[0] = e1[1]

    @pl.when(zi == nz - 1)
    def _():
        e1[5] = e1[4]
        e1[7] = plane1 + 1.0

    @pl.when(zi == nz - 2)
    def _():
        e1[7] = e1[6]

    s1 = 4.0
    for i in range(7):
        fz1[i] = face(e1[i], e1[i + 1], s1)
    for i in range(6):
        fx, fy, total = plane_faces(e1[i + 1], s1)
        fx1[i] = fx
        fy1[i] = fy
        diag = total + fz1[i] + fz1[i + 1] + k1[i]
        dg1[i] = diag
        weight = DAMPING / diag
        if i < 2:
            weight = jnp.where(zi > 0, weight, 0.0)
        if i > 3:
            weight = jnp.where(zi < nz - 1, weight, 0.0)
        wt1[i] = weight

    v2_halo()
    for p in (0, 3, 1, 2):
        base[p + 1] = sweep0(p, v2)
    base_halo = trade(base, 1, 4, BASE_LO)
    for arrived in b1_in:
        arrived()
    b1[0] = from_lo[1] + far_lo[0]
    b1[1] = from_lo[2] + pack[3]
    b1[2] = pack[1] + from_lo[0]
    b1[3] = pack[2] + from_hi[2]
    b1[4] = from_hi[0] + pack[0]
    b1[5] = from_hi[1] + far_hi[0]

    def beside1(i, mine, below, above):
        return plane_sum(fx1[i], fy1[i], mine) + fz1[i] * below + fz1[i + 1] * above

    def sweep1(i, mine, below, above):
        return (1.0 - DAMPING) * mine + wt1[i] * (b1[i] + beside1(i, mine, below, above))

    for i in range(6):
        a1[i] = wt1[i] * b1[i]
    for i in range(1, 5):
        a2[i] = sweep1(i, a1[i], a1[i - 1], a1[i + 1])
    rest = [b1[i] - dg1[i] * a2[i] + beside1(i, a2[i], a2[i - 1], a2[i + 1]) for i in (2, 3)]
    full = down1(rest[0] + rest[1])
    gb[core, chip] = full[:quarter // 4] + back(full[quarter // 4:], 1, LANES // 2)
    share(gb, 1)
    a2_in = [push(a2.at[2], a2.at[0], 1, A2_HI), push(a2.at[3], a2.at[5], -1, A2_LO)]
    gk_across()
    gk_in = gk_beside()
    gk_in()
    e2 = jnp.concatenate([gk[i, j, m] for m in range(n // 4) for i in range(2) for j in range(2)], axis=0)
    coarse = coarse_cycle(e2, back(e2, 1, LANES // 2), nz, quarter, 16.0, 16.0,
                          dot2, times2, (pool_rows, grow_rows))
    base_halo()

    def deliver(j):
        target = 4 * z + 2 * core + j
        piece = swept.at[pl.ds(2 * j, 2), pl.ds(pl.multiple_of(HALO * x, HALO), half), :]
        place = landed.at[:, pl.ds(pl.multiple_of(half * x, half), half), :]
        remote = pltpu.make_async_remote_copy(
            src_ref=piece, dst_ref=place, send_sem=spread_send.at[2, j],
            recv_sem=spread_recv.at[2, x], device_id=peer(target),
            device_id_type=pl.DeviceIdType.MESH)
        here = pltpu.make_async_copy(piece, place, spread_recv.at[2, x])
        away = target != me
        pl.when(away)(remote.start)
        pl.when(jnp.logical_not(away))(here.start)
        pending.append(lambda: pl.when(away)(remote.wait_send))

    for p in range(4):
        swept[p] = sweep0(p, base)
        if p % 2:
            deliver(p // 2)
    gb_in = relay(gb, 1)
    gb_in()
    packed = jnp.stack(in_order(gb))
    b2 = jnp.concatenate([packed, back(packed.reshape(-1, LANES), 1, LANES // 2).reshape(packed.shape)],
                         axis=1).reshape(nz * quarter, LANES)
    c2 = coarse(b2)
    for i in range(nz):
        c2_planes[i] = c2[i * quarter:(i + 1) * quarter]
    grow_r = spread_right(LANES, half, half)

    def up1(index):
        spread_out, tmp = times2(c2_planes[index], grow_r), scratch()
        tmp[pl.ds(0, quarter, stride=2), :] = spread_out
        tmp[pl.ds(1, quarter, stride=2), :] = spread_out
        return tmp[pl.ds(pl.multiple_of(first // 2 * x, 8), window1), :]


    for arrived in a2_in:
        arrived()
    mine = up1(zi)
    lower = jnp.where(zi > 0, up1(jnp.maximum(zi - 1, 0)), 0.0)
    upper = jnp.where(zi < nz - 1, up1(jnp.minimum(zi + 1, nz - 1)), 0.0)
    for i, c in enumerate((lower, lower, mine, mine, upper, upper)):
        a2c[i] = a2[i] + c
    for i in range(1, 5):
        a3[i - 1] = sweep1(i, a2c[i], a2c[i - 1], a2c[i + 1])
    for i in (1, 2):
        a4[i] = sweep1(i + 1, a3[i], a3[i - 1], a3[i + 1])

    def hand(count, low, delta, slot, i):
        target = 2 * zi + delta
        exists = (target >= 0) & (target < n)
        piece = a4.at[pl.ds(low, count), pl.ds(pl.multiple_of(HALO // 2 * x, HALO // 2), quarter), :]
        place = corr.at[pl.ds(slot, count), pl.ds(pl.multiple_of(quarter * x, quarter), quarter), :]
        kind = 2 - count
        remote = pltpu.make_async_remote_copy(
            src_ref=piece, dst_ref=place, send_sem=corr_send.at[i], recv_sem=corr_recv.at[kind, x],
            device_id=peer(jnp.clip(target, 0, n - 1)), device_id_type=pl.DeviceIdType.MESH)
        here = pltpu.make_async_copy(piece, place, corr_recv.at[kind, x])
        away = exists & (target != me)
        pl.when(away)(remote.start)
        pl.when(target == me)(here.start)
        pending.append(lambda: pl.when(away)(remote.wait_send))

    hand(2, 1, 0, 1, 0)
    hand(2, 1, 1, 0, 1)
    hand(1, 1, -1, 2, 2)
    hand(1, 2, 2, 0, 3)
    big_l, big_r = spread_left(nxy, half), spread_right(half, nxy, nxy)

    def up0(c):
        return dot2(big_l, times2(c, big_r))

    load_near.wait()
    within.wait()
    across.wait_recv()
    beside.wait_recv()
    en = [dielectric(near[f]) for f in range(6)]
    fzn[0] = face(en[0], en[1], 1.0)
    fzn[1] = face(jnp.where(me > 0, en[1], en[2]), en[2], 1.0)
    fzn[2] = face(en[2], en[3], 1.0)
    fzn[3] = face(en[3], jnp.where(me < n - 1, en[4], en[3]), 1.0)
    fzn[4] = face(en[4], en[5], 1.0)
    for f in range(4):
        fx, fy, total = plane_faces(en[f + 1], 1.0)
        fxn[f] = fx
        fyn[f] = fy
        kn = jnp.where(near[f + 1] == 2, SCREEN, 0.0).astype(F32)
        wtn[f] = DAMPING / (total + kn + fzn[f] + fzn[f + 1])
    for sent in pending:
        sent()
    lax.fori_loop(0, n, sent_density, 0)
    single = jnp.where(lax.rem(me, 2) == 0, me > 0, me < n - 1)
    for j in range(2):
        both = corr.at[pl.ds(0, 2), pl.ds(quarter * j, quarter), :]
        pltpu.make_async_copy(both, both, corr_recv.at[0, j]).wait()
        one = corr.at[pl.ds(0, 1), pl.ds(quarter * j, quarter), :]
        pl.when(single)(pltpu.make_async_copy(one, one, corr_recv.at[1, j]).wait)
    for j in range(2):
        place = landed.at[:, pl.ds(half * j, half), :]
        pltpu.make_async_copy(place, place, spread_recv.at[2, j]).wait()
    below, here, above = (up0(corr[i]) for i in range(3))
    spans = [(below, below, here), (here, below, here), (here, here, above), (above, here, above)]

    def relax(f, mine, low, high):
        return (1.0 - DAMPING) * mine + wtn[f] * (
            plane_sum(fxn[f], fyn[f], mine) + fzn[f] * low + fzn[f + 1] * high)

    y = [relax(f, *spans[f]) for f in range(4)]
    y[0] = jnp.where(me > 0, y[0], 0.0)
    y[3] = jnp.where(me < n - 1, y[3], 0.0)
    for f in (1, 2):
        out[f - 1] = landed[f - 1] + relax(f, y[f], y[f - 1], y[f + 1])


def box_local(partials, regions, previous):
    n = lax.axis_size("slab")
    nxy = regions.shape[1]
    half, quarter = nxy // 2, nxy // 4
    rows = partials.shape[2]
    window, window1 = half + HALO, (half + HALO) // 2
    vmem = lambda *shape: pltpu.VMEM(shape, F32)
    big = lambda count: vmem(count, window, nxy)
    small = lambda count: vmem(count, window1, half)
    return pl.pallas_call(
        functools.partial(box_kernel, n),
        out_shape=pltpu.VMEM(previous.shape, F32),
        in_specs=[pl.BlockSpec(memory_space=pltpu.HBM)] * 3,
        out_specs=pl.BlockSpec(memory_space=pltpu.VMEM),
        scratch_shapes=[
            pltpu.VMEM(partials.shape, partials.dtype), vmem(n // 2, 4, rows, nxy),
            pltpu.VMEM((8, window, nxy), jnp.int32), big(6), big(4),
            big(4), big(4), big(5), big(4), big(4), big(6), big(6), big(6), big(4),
            pltpu.VMEM((6, nxy, nxy), jnp.int32), vmem(4, nxy, nxy), vmem(4, nxy, nxy),
            vmem(5, nxy, nxy), vmem(4, nxy, nxy), vmem(2, nxy, nxy), vmem(3, half, half),
            small(8), small(6), small(6), small(6), small(7), small(6), small(6),
            small(4), small(3), small(3), small(1), small(1),
            small(6), small(6), small(6), small(6), small(4), small(4),
            vmem(2, 2, n // 4, quarter // 2, LANES), vmem(2, n // 2, quarter // 4, LANES),
            vmem(n // 2, quarter, LANES), vmem(8, 2 * nxy, LANES),
            pltpu.SemaphoreType.DMA((3,)),
            pltpu.SemaphoreType.DMA((5, 2)), pltpu.SemaphoreType.DMA((5, 2)),
            pltpu.SemaphoreType.DMA((4,)), pltpu.SemaphoreType.DMA((2, 2)),
            pltpu.SemaphoreType.DMA((n,)), pltpu.SemaphoreType.DMA((1,)),
            pltpu.SemaphoreType.DMA((MESSAGES,)), pltpu.SemaphoreType.DMA((MESSAGES,)),
            pltpu.SemaphoreType.DMA((5,)), pltpu.SemaphoreType.DMA((5,)),
        ],
        compiler_params=pltpu.CompilerParams(
            collective_id=1, has_side_effects=True, vmem_limit_bytes=60 * 1024 * 1024),
    )(partials, regions, previous)


def local(partials, regions, previous):
    n = lax.axis_size("slab")
    nxy = regions.shape[1]
    half, quarter = nxy // 2, nxy // 4
    rows = partials.shape[2]
    vmem = lambda *shape: pltpu.VMEM(shape, F32)
    spec = pl.BlockSpec(memory_space=pltpu.VMEM)
    return pl.pallas_call(
        functools.partial(kernel, n),
        out_shape=jax.ShapeDtypeStruct(previous.shape, F32),
        in_specs=[spec] * 3,
        out_specs=spec,
        scratch_shapes=[
            vmem(n, 2, rows, nxy), vmem(n, 2, rows, nxy), vmem(2, nxy, nxy),
            vmem(2, nxy, nxy), vmem(2, nxy, nxy), vmem(3, nxy, nxy), vmem(2, nxy, nxy),
            vmem(2, nxy, nxy),
            pltpu.VMEM((2, nxy, nxy), jnp.int32), pltpu.VMEM((2, nxy, nxy), jnp.int32),
            vmem(2, nxy, nxy), vmem(2, nxy, nxy), vmem(2, nxy, nxy), vmem(2, nxy, nxy),
            vmem(4, 2, nxy, nxy),
            vmem(2, nxy, nxy), vmem(2, nxy, nxy), vmem(2, nxy, nxy),
            vmem(6, 2, half, half), vmem(5, half, half), vmem(2, half, half),
            vmem(2, n // 2, quarter // 2, LANES), vmem(2, n // 2, quarter, LANES),
            pltpu.SemaphoreType.DMA((6, 2)), pltpu.SemaphoreType.DMA((6, 2)),
            pltpu.SemaphoreType.DMA((6, 2)), pltpu.SemaphoreType.DMA((6, 2)),
            pltpu.SemaphoreType.DMA((5,)), pltpu.SemaphoreType.DMA((5,)),
            vmem(n // 2, quarter, LANES),
        ],
        compiler_params=pltpu.CompilerParams(
            collective_id=0, has_side_effects=True, vmem_limit_bytes=60 * 1024 * 1024),
    )(partials, regions, previous)


def solution(mesh):
    in_specs = (
        P("job", None, "slab", None),
        P(("job", "slab"), None, None),
        P(("job", "slab"), None, None),
    )
    out_specs = P(("job", "slab"), None, None)
    size = mesh.shape["slab"]

    def fits(partials, regions):
        return (size == 16 and partials.shape[2] == 16 * size and partials.shape[1] == 2 * size
                and regions.shape[1] == 16 * size)

    def program(partials, regions, previous):
        chosen = box_local if fits(partials, regions) else local
        return jax.shard_map(chosen, mesh=mesh, in_specs=in_specs, out_specs=out_specs, check_vma=False)(
            partials, regions, previous)

    return program
```
